32 devices in a mesh: fsdp: 4 (over y, core), ctx: 2 (over x), tp: 4 (over z).
Axes of the slice: x: 2, y: 2, z: 4, core: 2. Of those that a mesh axis runs over, the one named last changes fastest.
Arguments:
- inputs: bfloat16 [2, 8, 512, 1024], P(None, 'fsdp', 'ctx'), may hold values from -6 to 6
- out_grad: bfloat16 [2, 8, 512, 1024], P(None, 'fsdp', 'ctx'), may hold values from -6 to 6
- segment_ids: int32 [2, 8, 512], P(None, 'fsdp'), may hold values from 0 to 7, never falling along the last dimension, each value on 1 to 256 neighbouring positions
- w_qkv: bfloat16 [1024, 3072], P(('fsdp', 'ctx'), 'tp'), may hold values from -0.25 to 0.25
- bias_qv: bfloat16 [2048], P('tp'), may hold values from -3 to 3
- w_out: bfloat16 [1024, 1024], P(('fsdp', 'ctx'), 'tp'), may hold values from -0.25 to 0.25
- w_up: bfloat16 [1024, 4096], P(('fsdp', 'ctx'), 'tp'), may hold values from -0.1875 to 0.1875
- bias_up: bfloat16 [4096], P('tp'), may hold values from -2 to 2
- w_down: bfloat16 [1024, 4096], P(('fsdp', 'ctx'), 'tp'), may hold values from -0.125 to 0.125
- gains: bfloat16 [1024, 2], P(('fsdp', 'ctx')), may hold values from 0.25 to 1.75
- shifts: bfloat16 [1024, 4], P(('fsdp', 'ctx')), may hold values from -2 to 2
Outputs:
- layer_out: bfloat16 [2, 8, 512, 1024], P(None, 'fsdp', ('ctx', 'tp'))
- input_grad: float32 [2, 8, 512, 1024], P(None, 'fsdp', ('ctx', 'tp'))
- grad_w_qkv: float32 [1024, 3072], P(('fsdp', 'ctx'), 'tp')
- grad_bias_qv: float32 [2048], P('tp')
- grad_w_out: float32 [1024, 1024], P(('fsdp', 'ctx'), 'tp')
- grad_w_up: float32 [1024, 4096], P(('fsdp', 'ctx'), 'tp')
- grad_bias_up: float32 [4096], P('tp')
- grad_w_down: float32 [1024, 4096], P(('fsdp', 'ctx'), 'tp')
- grad_gains: float32 [1024, 2], P(('fsdp', 'ctx'))
- grad_shifts: float32 [1024, 4], P(('fsdp', 'ctx'))
The draws below stay inside these ranges and needn't reach their ends.
Inputs may be any that keep to these rules, and one draw needn't show every extreme that they name: `segment_ids`: within a sequence the ids never fall; each of the 8 documents holds 1 to 256 positions, and one holds exactly 256.
All inputs are finite; a program needn't handle non-finite values.
Results may differ from the reference program's by a relative error of at most 0.018.
Values may be sent and summed in bfloat16 or wider, within the bound.
A program may use at most 64 MiB of HBM per device.

```python
import math
import jax
import jax.numpy as jnp
import numpy as np
from jax import lax

D = 1024
FF = 4096
HD = 64
LEN = 512
SEGS = 8
MOST = 256
MB = 2
SEQS = 8


def level_of(stream_key, dims, cuts, low, high):
    gain, own = 1.0, jax.random.fold_in(stream_key, 6)
    for axis_at, shards_of in cuts:
        draws = jnp.exp(jax.random.uniform(jax.random.fold_in(own, axis_at), (shards_of,), jnp.float32, low / len(cuts), high / len(cuts)))
        gain = gain * jnp.repeat(draws, dims[axis_at] // shards_of).reshape([-1 if axis == axis_at else 1 for axis in range(len(dims))])
    return gain


def profile(amount, total, most, skew):
    loads = [(1 << 20) // math.isqrt(rank ** skew) + 1 for rank in range(2, amount + 1)]
    rest, holding = total - most - (amount - 1), [1] * (amount - 1)
    while rest > 0:
        candidates = [i for i in range(amount - 1) if holding[i] < most]
        pool, left = sum([loads[i] for i in candidates]), rest
        for i in candidates:
            extra = min(most - holding[i], max(1, left * loads[i] // pool), rest)
            holding[i] = holding[i] + extra
            rest = rest - extra
    return np.array([most] + holding)


def ragged_sizes(own_key, count, total, most, slope):
    if count == 2:
        one = jax.random.randint(own_key, (), max(1, total - most), min(most, total - 1) + 1)
        return jnp.stack([one, total - one])
    lengths = jnp.asarray(profile(count, total, most, slope), jnp.int32)
    pairs = (count - 1) // 2
    donor, sink = lengths[1:1 + 2 * pairs:2], lengths[2:2 + 2 * pairs:2]
    slack = jnp.minimum(donor - 1, most - sink)
    passed = jax.random.randint(jax.random.fold_in(own_key, 1), (pairs,), 0, 1 << 20) % (slack + 1)
    lengths = lengths.at[1:1 + 2 * pairs:2].set(donor - passed).at[2:2 + 2 * pairs:2].set(sink + passed)
    return lengths[jax.random.permutation(jax.random.fold_in(own_key, 2), count)]


def scatter_about(stream_key, extent, scale, most, cuts=(), held_as=jnp.bfloat16):
    values = jax.random.normal(stream_key, extent, jnp.float32) * scale
    if len(cuts) > 0:
        values = level_of(stream_key, extent, cuts, -0.22, 0.18) * values
    return jnp.clip(values, min=-most, max=most).astype(held_as)


def setup_inputs(seed: int = 0) -> dict:
    seeds = jax.random.split(jax.random.key(seed), 12)
    inputs = scatter_about(seeds[0], (MB, SEQS, LEN, D), 1.0, 6.0, ((1, 4), (2, 2)))
    out_grad = scatter_about(seeds[1], (MB, SEQS, LEN, D), 1.0, 6.0, ((1, 4), (2, 2)))
    segment_ids = jax.vmap(lambda own: jnp.searchsorted(jnp.cumsum(ragged_sizes(own, SEGS, LEN, MOST, 2)), jnp.arange(LEN), side="right"))(jax.random.split(seeds[2], MB * SEQS)).reshape((MB, SEQS, LEN)).astype(jnp.int32)
    w_qkv = scatter_about(seeds[3], (D, 3 * D), (D // 2) ** -0.5, 0.25, ((0, 8), (1, 4)))
    bias_qv = scatter_about(seeds[4], (2 * D,), 0.5, 3.0, ((0, 4),))
    w_out = scatter_about(seeds[5], (D, D), (D // 2) ** -0.5, 0.25, ((0, 8), (1, 4)))
    w_up = scatter_about(seeds[6], (D, FF), D ** -0.5, 0.1875, ((0, 8), (1, 4)))
    bias_up = scatter_about(seeds[7], (FF,), 0.3, 2.0, ((0, 4),))
    w_down = scatter_about(seeds[8], (D, FF), (FF // 2) ** -0.5, 0.125, ((0, 8), (1, 4)))
    gains = jnp.clip(1.0 + 0.15 * jax.random.normal(seeds[9], (D, 2), jnp.float32), 0.25, 1.75).astype(jnp.bfloat16)
    shifts = scatter_about(seeds[10], (D, 4), 0.3, 2.0, ((0, 8),))
    return {"inputs": inputs, "out_grad": out_grad, "segment_ids": segment_ids, "w_qkv": w_qkv, "bias_qv": bias_qv, "w_out": w_out, "w_up": w_up, "bias_up": bias_up, "w_down": w_down, "gains": gains, "shifts": shifts}


@jax.custom_vjp
def low(v):
    return lax.optimization_barrier(v.astype(jnp.bfloat16)).astype(jnp.float32)

@jax.custom_vjp
def low_back(v):
    return v

def low_keep(v):
    return (low(v), None)

def low_pass(kept, grad):
    return (grad,)

def back_keep(v):
    return (v, None)

def back_low(kept, grad):
    return (low(grad),)
low.defvjp(low_keep, low_pass)
low_back.defvjp(back_keep, back_low)
highest_precision = lax.Precision.HIGHEST
norm_epsilon = 1e-12
masked_score = -1e+30

def norm_rows(rows_in, gain_row, offset):
    average = lax.optimization_barrier(jnp.mean(rows_in, axis=-1, keepdims=True))
    centered = rows_in - average
    spread = lax.optimization_barrier(jnp.mean(centered * centered, axis=-1, keepdims=True))
    return centered * lax.rsqrt(spread + norm_epsilon) * gain_row + offset

def exact_gelu(rows_in):
    return jax.nn.gelu(rows_in, approximate=False)

def attend_one(pieces):
    queries, key_rows, value_rows, segment_row = pieces
    same_segment = segment_row[:, None] == segment_row[None, :]
    scores = jnp.einsum('qhe,khe->hqk', queries, key_rows, precision=highest_precision) * HD ** (-0.5)
    scores = low_back(scores)
    scores = jnp.where(same_segment[None], scores, masked_score)
    row_max = lax.optimization_barrier(jnp.max(scores, axis=-1, keepdims=True))
    weights = jnp.exp(scores - row_max)
    probabilities = weights / lax.optimization_barrier(jnp.sum(weights, axis=-1, keepdims=True))
    return jnp.einsum('hqk,khe->qhe', low(probabilities), value_rows, precision=highest_precision)

def layer(block, weight_set, segment_block):
    w_qkv, bias_qv, w_out, w_up, bias_up, w_down, gains, shifts = weight_set
    group_size, length, model_width = block.shape
    head_count = bias_qv.shape[0] // (2 * HD)
    rows_in = block.reshape(group_size * length, model_width)
    projected = low_back(jnp.dot(rows_in, w_qkv, precision=highest_precision))
    projected = projected.reshape(group_size, length, head_count, 3, HD)
    qv_bias = bias_qv.reshape(head_count, 2, HD)
    queries = low(projected[:, :, :, 0] + qv_bias[:, 0])
    key_rows = low(projected[:, :, :, 1])
    value_rows = low(projected[:, :, :, 2] + qv_bias[:, 1])
    attended = lax.map(jax.checkpoint(attend_one), (queries, key_rows, value_rows, segment_block))
    attended = low(low_back(attended.reshape(group_size * length, head_count * HD)))
    first_sum = rows_in + low_back(jnp.dot(attended, w_out.T, precision=highest_precision)) + shifts[:, 0]
    first_norm = norm_rows(first_sum, gains[:, 0], shifts[:, 1])
    before_act = low_back(jnp.dot(low(first_norm), w_up, precision=highest_precision)) + bias_up
    hidden = low(exact_gelu(before_act))
    second_sum = first_norm + low_back(jnp.dot(hidden, w_down.T, precision=highest_precision)) + shifts[:, 2]
    result = norm_rows(second_sum, gains[:, 1], shifts[:, 3])
    return result.reshape(group_size, length, model_width)

def add_pair(running, update):
    return running + update

def reference(inputs, out_grad, segment_ids, w_qkv, bias_qv, w_out, w_up, bias_up, w_down, gains, shifts):
    model_width = inputs.shape[3]
    length = inputs.shape[2]
    sequence_total = inputs.shape[0] * inputs.shape[1]
    group_size = 1
    for candidate in (8, 4, 2):
        if sequence_total % candidate == 0 and group_size == 1:
            group_size = candidate
    group_count = sequence_total // group_size
    block_inputs = inputs.astype(jnp.float32).reshape(group_count, group_size, length, model_width)
    block_grads = out_grad.astype(jnp.float32).reshape(group_count, group_size, length, model_width)
    block_segments = segment_ids.reshape(group_count, group_size, length)
    params = (w_qkv.astype(jnp.float32), bias_qv.astype(jnp.float32), w_out.astype(jnp.float32), w_up.astype(jnp.float32), bias_up.astype(jnp.float32), w_down.astype(jnp.float32), gains.astype(jnp.float32), shifts.astype(jnp.float32))

    def one_group(totals, pieces):
        block, upstream, segment_block = pieces

        def forward(block_in, weight_set):
            return layer(block_in, weight_set, segment_block)
        result, pullback = jax.vjp(forward, block, params)
        block_grad, param_grads = pullback(upstream)
        totals = jax.tree.map(add_pair, totals, param_grads)
        return (totals, (result, block_grad))
    zero_grads = jax.tree.map(jnp.zeros_like, params)
    totals, outputs = lax.scan(one_group, zero_grads, (block_inputs, block_grads, block_segments))
    results, input_grads = outputs
    layer_out = results.reshape(inputs.shape).astype(jnp.bfloat16)
    input_grad = input_grads.reshape(inputs.shape)
    return (layer_out, input_grad, totals[0], totals[1], totals[2], totals[3], totals[4], totals[5], totals[6], totals[7])
```

```python
import jax
import jax.numpy as jnp
from jax import lax
from jax.experimental import pallas as pl
from jax.experimental.pallas import tpu as pltpu
from jax.sharding import PartitionSpec as P

HD = 64


norm_epsilon = 1e-12
masked_score = -1e30


def norm_rows(rows_in, gain_row, offset):
    average = jnp.mean(rows_in, axis=-1, keepdims=True)
    centered = rows_in - average
    spread = jnp.mean(centered * centered, axis=-1, keepdims=True)
    return centered * lax.rsqrt(spread + norm_epsilon) * gain_row + offset


def exact_gelu(rows_in):
    return jax.nn.gelu(rows_in, approximate=False)


def contract_rows(left_rows, right_rows):
    return lax.dot_general(
        left_rows, right_rows, (((0,), (0,)), ((), ())), preferred_element_type=jnp.float32
    )


def times_transposed(left_rows, right_rows):
    return lax.dot_general(
        left_rows, right_rows, (((1,), (1,)), ((), ())), preferred_element_type=jnp.float32
    )


def masked_scores(queries, key_rows, same_segment, score_scale):
    scores = (
        jnp.einsum("sqhe,skhe->shqk", queries, key_rows, preferred_element_type=jnp.float32)
        * score_scale
    )
    return jnp.where(same_segment[:, None], scores, masked_score)


def add_pair(running, update):
    return running + update


def reduce_rows(part):
    return lax.psum(part, "tp")


def local(
    inputs, out_grad, segment_ids, w_qkv, bias_qv, w_out, w_up, bias_up, w_down, gains, shifts
):
    batches, seq_local, rows_local, model_width = inputs.shape
    tokens = seq_local * rows_local
    heads_local = w_out.shape[1] // HD
    score_scale = HD ** (-0.5)
    row_share = rows_local // lax.axis_size("tp")
    row_start = lax.axis_index("tp") * row_share
    query_start = lax.axis_index("ctx") * rows_local
    qv_bias = bias_qv.astype(jnp.float32).reshape(heads_local, 2, HD)
    up_bias = bias_up.astype(jnp.float32)

    def pick_rows(values):
        shaped = values.reshape(seq_local, rows_local, model_width)
        return lax.dynamic_slice_in_dim(shaped, row_start, row_share, 1)

    full_totals = (
        jnp.zeros((model_width, w_qkv.shape[1]), jnp.float32),
        jnp.zeros((model_width, w_out.shape[1]), jnp.float32),
        jnp.zeros((model_width, w_up.shape[1]), jnp.float32),
        jnp.zeros((model_width, w_down.shape[1]), jnp.float32),
        jnp.zeros((model_width, 2), jnp.float32),
        jnp.zeros((model_width, 4), jnp.float32),
    )
    share_totals = (
        jnp.zeros(w_qkv.shape, jnp.float32),
        jnp.zeros(w_out.shape, jnp.float32),
        jnp.zeros(w_up.shape, jnp.float32),
        jnp.zeros(w_down.shape, jnp.float32),
        jnp.zeros(gains.shape, jnp.float32),
        jnp.zeros(shifts.shape, jnp.float32),
    )
    qv_bias_grad = jnp.zeros(bias_qv.shape, jnp.float32)
    up_bias_grad = jnp.zeros(bias_up.shape, jnp.float32)
    layer_rows = []
    input_rows = []
    for batch_index in range(batches):
        gathered = (
            lax.all_gather(w_qkv, ("fsdp", "ctx"), axis=0, tiled=True),
            lax.all_gather(w_out, ("fsdp", "ctx"), axis=0, tiled=True),
            lax.all_gather(w_up, ("fsdp", "ctx"), axis=0, tiled=True),
            lax.all_gather(w_down, ("fsdp", "ctx"), axis=0, tiled=True),
            lax.all_gather(gains, ("fsdp", "ctx"), axis=0, tiled=True),
            lax.all_gather(shifts, ("fsdp", "ctx"), axis=0, tiled=True),
        )
        full_qkv, full_out, full_up, full_down, full_gains, full_shifts = gathered
        gain_rows = full_gains.astype(jnp.float32)
        shift_rows = full_shifts.astype(jnp.float32)
        x_low = inputs[batch_index].reshape(tokens, model_width)
        x_full = x_low.astype(jnp.float32)
        projected = jnp.dot(x_low, full_qkv, preferred_element_type=jnp.float32)
        projected = projected.reshape(seq_local, rows_local, heads_local, 3, HD)
        queries = (projected[:, :, :, 0] + qv_bias[:, 0]).astype(jnp.bfloat16)
        key_local = projected[:, :, :, 1].astype(jnp.bfloat16)
        value_local = (projected[:, :, :, 2] + qv_bias[:, 1]).astype(jnp.bfloat16)
        joined = jnp.concatenate([key_local, value_local], axis=-1)
        joined_all = lax.all_gather(joined, "ctx", axis=1, tiled=True)
        key_rows = joined_all[..., :HD]
        value_rows = joined_all[..., HD:]
        segments = segment_ids[batch_index]
        query_segments = lax.dynamic_slice_in_dim(segments, query_start, rows_local, 1)
        same_segment = query_segments[:, :, None] == segments[:, None, :]
        scores = masked_scores(queries, key_rows, same_segment, score_scale)
        row_max = jnp.max(scores, axis=-1, keepdims=True)
        weights = jnp.exp(scores - row_max)
        row_total = jnp.sum(weights, axis=-1, keepdims=True)
        log_total = row_max + jnp.log(row_total)
        p_low = (weights / row_total).astype(jnp.bfloat16)
        attended = jnp.einsum(
            "shqk,skhe->sqhe", p_low, value_rows, preferred_element_type=jnp.float32
        )
        attended_low = attended.reshape(tokens, heads_local * HD).astype(jnp.bfloat16)
        attention_part = times_transposed(attended_low, full_out)
        upstream_full = out_grad[batch_index].reshape(tokens, model_width).astype(jnp.float32)
        attention_total = reduce_rows(attention_part)
        first_sum = x_full + attention_total + shift_rows[:, 0]
        first_norm, first_back = jax.vjp(norm_rows, first_sum, gain_rows[:, 0], shift_rows[:, 1])
        norm_low = first_norm.astype(jnp.bfloat16)
        before_act = jnp.dot(norm_low, full_up, preferred_element_type=jnp.float32) + up_bias
        activated, gelu_back = jax.vjp(exact_gelu, before_act)
        hidden = activated.astype(jnp.bfloat16)
        down_part = times_transposed(hidden, full_down)
        down_total = reduce_rows(down_part)
        second_sum = first_norm + down_total + shift_rows[:, 2]
        result, second_back = jax.vjp(norm_rows, second_sum, gain_rows[:, 1], shift_rows[:, 3])
        layer_rows.append(pick_rows(result).astype(jnp.bfloat16))
        second_grad, gain_two, shift_three = second_back(upstream_full)
        shift_two = jnp.sum(second_grad, axis=0)
        second_low = second_grad.astype(jnp.bfloat16)
        down_step = contract_rows(second_low, hidden)
        hidden_grad = jnp.dot(second_low, full_down, preferred_element_type=jnp.float32)
        (act_grad,) = gelu_back(hidden_grad)
        up_bias_grad = up_bias_grad + jnp.sum(act_grad, axis=0)
        act_low = act_grad.astype(jnp.bfloat16)
        up_step = contract_rows(norm_low, act_low)
        back_part = times_transposed(act_low, full_up)
        back_total = reduce_rows(back_part)
        norm_grad = second_grad + back_total
        first_grad, gain_one, shift_one = first_back(norm_grad)
        shift_zero = jnp.sum(first_grad, axis=0)
        first_low = first_grad.astype(jnp.bfloat16)
        out_step = contract_rows(first_low, attended_low)
        attended_grad = jnp.dot(first_low, full_out, preferred_element_type=jnp.float32)
        attended_grad = attended_grad.astype(jnp.bfloat16).reshape(
            seq_local, rows_local, heads_local, HD
        )
        scores = masked_scores(queries, key_rows, same_segment, score_scale)
        probabilities = jnp.exp(scores - log_total)
        value_grad = jnp.einsum(
            "shqk,sqhe->skhe",
            probabilities.astype(jnp.bfloat16),
            attended_grad,
            preferred_element_type=jnp.float32,
        )
        prob_grad = jnp.einsum(
            "sqhe,skhe->shqk", attended_grad, value_rows, preferred_element_type=jnp.float32
        )
        row_dot = jnp.sum(prob_grad * probabilities, axis=-1, keepdims=True)
        score_grad = (probabilities * (prob_grad - row_dot)).astype(jnp.bfloat16)
        query_grad = (
            jnp.einsum("shqk,skhe->sqhe", score_grad, key_rows, preferred_element_type=jnp.float32)
            * score_scale
        )
        key_grad = (
            jnp.einsum("shqk,sqhe->skhe", score_grad, queries, preferred_element_type=jnp.float32)
            * score_scale
        )
        kv_grads = lax.psum_scatter(
            jnp.concatenate([key_grad, value_grad], axis=-1).astype(jnp.bfloat16),
            "ctx",
            scatter_dimension=1,
            tiled=True,
        ).astype(jnp.float32)
        key_mine = kv_grads[..., :HD]
        value_mine = kv_grads[..., HD:]
        bias_step = jnp.stack(
            [jnp.sum(query_grad, axis=(0, 1)), jnp.sum(value_mine, axis=(0, 1))], axis=1
        )
        qv_bias_grad = qv_bias_grad + bias_step.reshape(-1)
        mixed_grad = jnp.stack([query_grad, key_mine, value_mine], axis=3)
        mixed_grad = mixed_grad.reshape(tokens, 3 * heads_local * HD).astype(jnp.bfloat16)
        qkv_step = contract_rows(x_low, mixed_grad)
        input_part = times_transposed(mixed_grad, full_qkv).reshape(
            seq_local, rows_local, model_width
        )
        input_mine = lax.psum_scatter(
            input_part.astype(jnp.bfloat16), "tp", scatter_dimension=1, tiled=True
        ).astype(jnp.float32)
        first_part = pick_rows(first_grad)
        input_rows.append(input_mine + first_part)
        gain_step = jnp.stack([gain_one, gain_two], axis=1)
        shift_step = jnp.stack([shift_zero, shift_one, shift_two, shift_three], axis=1)
        full_totals = tuple(
            map(
                add_pair,
                full_totals,
                (qkv_step, out_step, up_step, down_step, gain_step, shift_step),
            )
        )
    share_totals = (
        lax.psum_scatter(
            full_totals[0].astype(jnp.bfloat16), ("fsdp", "ctx"), scatter_dimension=0, tiled=True
        ).astype(jnp.float32),
        lax.psum_scatter(
            full_totals[1].astype(jnp.bfloat16), ("fsdp", "ctx"), scatter_dimension=0, tiled=True
        ).astype(jnp.float32),
        lax.psum_scatter(
            full_totals[2].astype(jnp.bfloat16), ("fsdp", "ctx"), scatter_dimension=0, tiled=True
        ).astype(jnp.float32),
        lax.psum_scatter(
            full_totals[3].astype(jnp.bfloat16), ("fsdp", "ctx"), scatter_dimension=0, tiled=True
        ).astype(jnp.float32),
        lax.psum_scatter(
            full_totals[4].astype(jnp.bfloat16), ("fsdp", "ctx"), scatter_dimension=0, tiled=True
        ).astype(jnp.float32),
        lax.psum_scatter(
            full_totals[5].astype(jnp.bfloat16), ("fsdp", "ctx"), scatter_dimension=0, tiled=True
        ).astype(jnp.float32),
    )
    qv_total, up_total = lax.psum((qv_bias_grad, up_bias_grad), ("fsdp", "ctx"))
    return (
        jnp.stack(layer_rows, axis=0),
        jnp.stack(input_rows, axis=0),
        share_totals[0],
        qv_total,
        share_totals[1],
        share_totals[2],
        up_total,
        share_totals[3],
        share_totals[4],
        share_totals[5],
    )


MESH = pl.DeviceIdType.MESH
ROW_A, ROW_D, ROW_AD, ROW_B = (0, 48), (48, 48), (0, 96), (96, 32)

class Where:
    def __init__(self):
        fsdp = lax.axis_index("fsdp")
        self.y = fsdp // 2
        self.e = fsdp % 2
        self.c = lax.axis_index("ctx")
        self.t = lax.axis_index("tp")
    def at(self, y=None, e=None, c=None, t=None):
        y = self.y if y is None else y
        e = self.e if e is None else e
        c = self.c if c is None else c
        t = self.t if t is None else t
        return (2 * y + e, c, t)

def when(cond, fn):
    if cond is True:
        fn()
    else:
        pl.when(cond)(fn)

class Net:
    def __init__(self, send_sems, recv_sems):
        self.send_sems, self.recv_sems, self.count, self.pending = send_sems, recv_sems, 0, []
    def pair(self):
        self.count += 1
        return self.count - 1
    def send(self, index, cond, src, dst, device):
        def make():
            return pltpu.make_async_remote_copy(
                src_ref=src(), dst_ref=dst(), send_sem=self.send_sems.at[index],
                recv_sem=self.recv_sems.at[index], device_id=device, device_id_type=MESH)
        when(cond, lambda: make().start())
        self.pending.append((cond, make))
    def recv(self, index, cond, here, device):
        def wait():
            pltpu.make_async_remote_copy(
                src_ref=here(), dst_ref=here(), send_sem=self.send_sems.at[index],
                recv_sem=self.recv_sems.at[index], device_id=device, device_id_type=MESH).wait_recv()
        when(cond, wait)
    def drain(self):
        for cond, make in self.pending:
            when(cond, lambda make=make: make().wait_send())

def slots_of(w):
    t = w.t
    return [("own", t, True), ("l1", t - 1, t >= 1), ("r1", t + 1, t <= 2), ("l2", t - 2, t >= 2),
            ("r2", t + 2, t <= 1), ("l3", t - 3, t >= 3), ("r3", t + 3, t <= 0)]

class Gather:
    STAGES = 7
    def __init__(self, net, w, mine, full, c0, cn, local_sem, routes=(ROW_A, ROW_D, ROW_AD, ROW_B)):
        self.net, self.w, self.mine, self.full, self.local_sem = net, w, mine, full, local_sem
        self.cols = pl.ds(c0, cn)
        self.row_a, self.row_d, self.row_ad, self.row_b = [None if r is None else pl.ds(*r) for r in routes]
        self.slots = slots_of(w)
        self.ids = {}
    def id(self, key):
        if key not in self.ids:
            self.ids[key] = self.net.pair()
        return self.ids[key]
    def blk(self, tt, rows, y=None, c=None):
        w = self.w
        y = w.y if y is None else y
        c = w.c if c is None else c
        return lambda: self.full.at[tt, y, :, c, rows, self.cols]
    def row(self, tt, rows, y=None):
        y = self.w.y if y is None else y
        return lambda: self.full.at[tt, y, :, :, rows, self.cols]
    def colm(self, tt, rows, c=None):
        c = self.w.c if c is None else c
        return lambda: self.full.at[tt, :, :, c, rows, self.cols]
    def plane(self, tt, rows):
        return lambda: self.full.at[tt, :, :, :, rows, self.cols]
    def same(self, key, cond, ref, device):
        self.net.send(self.id(key), cond, ref, ref, device)
    def sib(self):
        w = self.w
        dst = lambda: self.full.at[w.t, w.y, w.e, w.c, :, self.cols]
        self.net.send(self.id("sib"), True, lambda: self.mine.at[1 - w.e, :, self.cols], dst, w.at(e=1 - w.e))
        cp = pltpu.make_async_copy(self.mine.at[w.e, :, self.cols], dst(), self.local_sem)
        cp.start()
        self.own_copy = cp
    def zsend(self, tag, slot, ref):
        w = self.w
        k = {"own": 0, "l1": 1, "r1": 1, "l2": 2, "r2": 2}[slot]
        if slot == "own" or slot[0] == "l":
            name, tt, ok = self.slot("own" if k == 0 else f"l{k}")
            self.same((tag, "zr", k), (w.t < 3) if ok is True else jnp.logical_and(ok, w.t < 3), ref(tt), w.at(t=w.t + 1))
        if slot == "own" or slot[0] == "r":
            name, tt, ok = self.slot("own" if k == 0 else f"r{k}")
            self.same((tag, "zl", k), (w.t > 0) if ok is True else jnp.logical_and(ok, w.t > 0), ref(tt), w.at(t=w.t - 1))
    def zrecv(self, tag, slot, ref):
        w = self.w
        k = int(slot[1])
        _, tt, ok = self.slot(slot)
        if slot[0] == "l":
            self.net.recv(self.id((tag, "zr", k - 1)), ok, ref(tt), w.at(t=w.t - 1))
        else:
            self.net.recv(self.id((tag, "zl", k - 1)), ok, ref(tt), w.at(t=w.t + 1))
    def slot(self, name):
        return next(s for s in self.slots if s[0] == name)
    def first_hop(self, name):
        w = self.w
        _, tt, ok = self.slot(name)
        self.same(("ax", name), ok, self.blk(tt, self.row_a), w.at(c=1 - w.c))
        if self.row_d is not None:
            self.same(("dy", name), ok, self.blk(tt, self.row_d), w.at(y=1 - w.y))
    def second_hop(self, name):
        w = self.w
        _, tt, ok = self.slot(name)
        self.net.recv(self.id(("ax", name)), ok, self.blk(tt, self.row_a, c=1 - w.c), w.at(c=1 - w.c))
        self.same(("ay", name), ok, self.row(tt, self.row_a), w.at(y=1 - w.y))
        if self.row_d is not None:
            self.net.recv(self.id(("dy", name)), ok, self.blk(tt, self.row_d, y=1 - w.y), w.at(y=1 - w.y))
            self.same(("dx", name), ok, self.colm(tt, self.row_d), w.at(c=1 - w.c))
    def last(self, name):
        w = self.w
        _, tt, ok = self.slot(name)
        self.net.recv(self.id(("ay", name)), ok, self.row(tt, self.row_a, y=1 - w.y), w.at(y=1 - w.y))
        if self.row_d is not None:
            self.net.recv(self.id(("dx", name)), ok, self.colm(tt, self.row_d, c=1 - w.c), w.at(c=1 - w.c))
    def stage(self, k):
        w = self.w
        ad = lambda tt: self.blk(tt, self.row_ad)
        bz = lambda tt: self.plane(tt, self.row_b)
        b = self.row_b is not None
        if k == 0:
            self.sib()
        elif k == 1:
            self.own_copy.wait()
            self.net.recv(self.id("sib"), True, lambda: self.full.at[w.t, w.y, 1 - w.e, w.c, :, self.cols], w.at(e=1 - w.e))
            self.zsend("ad", "own", ad)
            if b:
                self.same("bx", True, self.blk(w.t, self.row_b), w.at(c=1 - w.c))
            self.first_hop("own")
        elif k == 2:
            if b:
                self.net.recv(self.id("bx"), True, self.blk(w.t, self.row_b, c=1 - w.c), w.at(c=1 - w.c))
                self.same("by", True, self.row(w.t, self.row_b), w.at(y=1 - w.y))
            for s in ("l1", "r1"):
                self.zrecv("ad", s, ad)
                self.zsend("ad", s, ad)
                self.first_hop(s)
            self.second_hop("own")
        elif k == 3:
            if b:
                self.net.recv(self.id("by"), True, self.row(w.t, self.row_b, y=1 - w.y), w.at(y=1 - w.y))
                self.zsend("b", "own", bz)
            for s in ("l2", "r2"):
                self.zrecv("ad", s, ad)
                self.zsend("ad", s, ad)
                self.first_hop(s)
            for s in ("l1", "r1"):
                self.second_hop(s)
        elif k == 4:
            if b:
                for s in ("l1", "r1"):
                    self.zrecv("b", s, bz)
                    self.zsend("b", s, bz)
            for s in ("l3", "r3"):
                self.zrecv("ad", s, ad)
                self.first_hop(s)
            for s in ("l2", "r2"):
                self.second_hop(s)
        elif k == 5:
            if b:
                for s in ("l2", "r2"):
                    self.zrecv("b", s, bz)
                    self.zsend("b", s, bz)
            for s in ("l3", "r3"):
                self.second_hop(s)
        elif k == 6:
            if b:
                for s in ("l3", "r3"):
                    self.zrecv("b", s, bz)
            for name, _, _ in self.slots:
                self.last(name)

def barrier(w, extra=()):
    sem = pltpu.get_barrier_semaphore()
    one = lambda dev: pl.semaphore_signal(sem, inc=1, device_id=dev, device_id_type=MESH)
    one(w.at(e=1 - w.e)); one(w.at(c=1 - w.c)); one(w.at(y=1 - w.y))
    pl.when(w.t > 0)(lambda: one(w.at(t=w.t - 1)))
    pl.when(w.t < 3)(lambda: one(w.at(t=w.t + 1)))
    ends = jnp.where(w.t == 0, 1, 0) + jnp.where(w.t == 3, 1, 0)
    return sem, one, 5 - ends

def gather_kernel(mine, small, x_in, g_in, full, small_full, x_all, g_own, send_sems, recv_sems, local_sems):
    w = Where()
    sem, one, need = barrier(w)
    cross = w.e != w.c
    diag = w.at(e=1 - w.e, c=1 - w.c)
    pl.when(cross)(lambda: one(diag))
    pl.semaphore_wait(sem, need + jnp.where(cross, 1, 0))
    net = Net(send_sems, recv_sems)
    seq = lambda ref: ref.at[w.t // 2, w.t % 2]
    parts = [Gather(net, w, small, small_full, 0, 128, local_sems.at[0], routes=((0, 16), None, (0, 16), None))]
    parts += [Gather(net, w, mine, full, 512 * i, 512, local_sems.at[1 + i]) for i in range(3)]
    xi, gi, xs = net.pair(), net.pair(), net.pair()
    parts[1].stage(0)
    parts[0].stage(0)
    for idx, src, dst in ((xi, x_in, x_all.at[0]), (gi, g_in, g_own)):
        net.send(idx, cross, lambda src=src: seq(src), lambda dst=dst: dst, diag)
    local = [pltpu.make_async_copy(seq(x_in), x_all.at[0], local_sems.at[4]),
             pltpu.make_async_copy(seq(g_in), g_own, local_sems.at[5])]
    for cp in local:
        pl.when(jnp.logical_not(cross))(lambda cp=cp: cp.start())
    parts[2].stage(0)
    parts[3].stage(0)
    parts[1].stage(1)
    parts[0].stage(1)
    pl.when(jnp.logical_not(cross))(lambda: local[0].wait())
    net.recv(xi, cross, lambda: x_all.at[0], diag)
    net.send(xs, True, lambda: x_all.at[0], lambda: x_all.at[1], w.at(e=1 - w.e))
    for s in range(2, 12):
        for i, start in ((1, 0), (0, 0), (2, 2), (3, 4)):
            k = s - start
            if 1 <= k <= 6:
                parts[i].stage(k)
    pl.when(jnp.logical_not(cross))(lambda: local[1].wait())
    net.recv(gi, cross, lambda: g_own, diag)
    net.recv(xs, True, lambda: x_all.at[1], w.at(e=1 - w.e))
    net.drain()

N_GATHER = 153

def run_gather(mine, small, x_in, g_in):
    any_ = pl.BlockSpec(memory_space=pl.ANY)
    vm = pl.BlockSpec(memory_space=pltpu.VMEM)
    rows, width = x_in.shape[2:]
    return pl.pallas_call(
        gather_kernel,
        out_shape=(jax.ShapeDtypeStruct((4, 2, 2, 2) + mine.shape[1:], mine.dtype),
                   jax.ShapeDtypeStruct((4, 2, 2, 2) + small.shape[1:], small.dtype),
                   jax.ShapeDtypeStruct((2, rows, width), x_in.dtype),
                   jax.ShapeDtypeStruct((rows, width), g_in.dtype)),
        in_specs=[vm, vm, vm, vm],
        out_specs=(any_, any_, any_, any_),
        scratch_shapes=[pltpu.SemaphoreType.DMA((N_GATHER,)), pltpu.SemaphoreType.DMA((N_GATHER,)), pltpu.SemaphoreType.DMA((6,))],
        compiler_params=pltpu.CompilerParams(collective_id=0, has_side_effects=True),
        name="gather",
    )(mine, small, x_in, g_in)


ROWS = {"a": pl.ds(0, 48), "d": pl.ds(48, 48), "ad": pl.ds(0, 96), "b": pl.ds(96, 32)}

class Scatter:
    def __init__(self, net, w, g, bufs, c0, cn):
        self.net, self.w, self.g, self.bufs = net, w, g, bufs
        self.cols = pl.ds(c0, cn)
        self.ids = {}
    def id(self, key):
        if key not in self.ids:
            self.ids[key] = self.net.pair()
        return self.ids[key]
    def take(self, key, cond, buf, place, device):
        cols = self.cols
        def body():
            self.net.recv(self.id(key), True, lambda: buf(), device)
            ref = place()
            ref[...] = (ref[...].astype(jnp.float32) + buf()[...].astype(jnp.float32)).astype(ref.dtype)
        when(cond, body)
    def zstep(self, tag, m, place):
        w = self.w
        for way, me, targets in (("r", m, [j for j in (3, 2, 1) if j >= m]), ("l", 3 - m, [j for j in (0, 1, 2) if j <= 3 - m])):
            buf = self.bufs[tag + "z" + way]
            nxt = w.at(t=w.t + 1) if way == "r" else w.at(t=w.t - 1)
            prv = w.at(t=w.t - 1) if way == "r" else w.at(t=w.t + 1)
            here = w.t == me
            for j in targets:
                land = lambda j=j, buf=buf: buf.at[j, ..., self.cols]
                if m > 0:
                    self.take((tag, way, j), here, land, place(j), prv)
                if j != me:
                    self.net.send(self.id((tag, way, j)), here, place(j), land, nxt)
    def stage(self, k):
        w, g, cols, b = self.w, self.g, self.cols, self.bufs
        X, Y = w.at(c=1 - w.c), w.at(y=1 - w.y)
        ad = lambda j: (lambda: g.at[j, w.y, :, w.c, ROWS["ad"], cols])
        bz = lambda j: (lambda: g.at[j, :, :, :, ROWS["b"], cols])
        order = (3, 0, 2, 1)
        if k == 0:
            self.zstep("b", 0, bz)
            for j in order:
                self.net.send(self.id(("ya", j)), True, lambda j=j: g.at[j, 1 - w.y, :, :, ROWS["a"], cols], lambda j=j: b["ya"].at[j, :, :, :, cols], Y)
                self.net.send(self.id(("xd", j)), True, lambda j=j: g.at[j, :, :, 1 - w.c, ROWS["d"], cols], lambda j=j: b["xd"].at[j, :, :, :, cols], X)
        elif k == 1:
            self.zstep("b", 1, bz)
            for j in order:
                self.take(("ya", j), True, lambda j=j: b["ya"].at[j, :, :, :, cols], lambda j=j: g.at[j, w.y, :, :, ROWS["a"], cols], Y)
                self.net.send(self.id(("xa", j)), True, lambda j=j: g.at[j, w.y, :, 1 - w.c, ROWS["a"], cols], lambda j=j: b["xa"].at[j, :, :, cols], X)
                self.take(("xd", j), True, lambda j=j: b["xd"].at[j, :, :, :, cols], lambda j=j: g.at[j, :, :, w.c, ROWS["d"], cols], X)
                self.net.send(self.id(("yd", j)), True, lambda j=j: g.at[j, 1 - w.y, :, w.c, ROWS["d"], cols], lambda j=j: b["yd"].at[j, :, :, cols], Y)
        elif k == 2:
            self.zstep("b", 2, bz)
            for j in order:
                self.take(("xa", j), True, lambda j=j: b["xa"].at[j, :, :, cols], lambda j=j: g.at[j, w.y, :, w.c, ROWS["a"], cols], X)
                self.take(("yd", j), True, lambda j=j: b["yd"].at[j, :, :, cols], lambda j=j: g.at[j, w.y, :, w.c, ROWS["d"], cols], Y)
            self.zstep("ad", 0, ad)
        elif k == 3:
            self.zstep("b", 3, bz)
            self.net.send(self.id("by"), True, lambda: g.at[w.t, 1 - w.y, :, :, ROWS["b"], cols], lambda: b["by"].at[:, :, :, cols], Y)
            self.zstep("ad", 1, ad)
        elif k == 4:
            self.take("by", True, lambda: b["by"].at[:, :, :, cols], lambda: g.at[w.t, w.y, :, :, ROWS["b"], cols], Y)
            self.net.send(self.id("bx"), True, lambda: g.at[w.t, w.y, :, 1 - w.c, ROWS["b"], cols], lambda: b["bx"].at[:, :, cols], X)
            self.zstep("ad", 2, ad)
        elif k == 5:
            self.zstep("ad", 3, ad)
            self.take("bx", True, lambda: b["bx"].at[:, :, cols], lambda: g.at[w.t, w.y, :, w.c, ROWS["b"], cols], X)
            self.net.send(self.id("sib"), True, lambda: g.at[w.t, w.y, 1 - w.e, w.c, :, cols], lambda: b["sib"].at[:, cols], w.at(e=1 - w.e))
        elif k == 6:
            self.net.recv(self.id("sib"), True, lambda: b["sib"].at[:, cols], w.at(e=1 - w.e))

PIECES = ((0, 384), (384, 128), (512, 512), (1024, 512))

def scatter_kernel(g_in, lo, ig, o_qkv, o_out, o_up, o_down, lo_out, ig_out, g, ya, xa, xd, yd, adzr, adzl, bzr, bzl, by, bx, sib, send_sems, recv_sems, local_sems):
    w = Where()
    sem, one, need = barrier(w)
    same = w.e == w.c
    for d in range(4):
        go = (lambda d=d: one(w.at(e=w.c, c=w.e, t=(w.t + d) % 4)))
        when(True if d else jnp.logical_not(same), go)
    pl.semaphore_wait(sem, need + 3 + jnp.where(same, 0, 1))
    net = Net(send_sems, recv_sems)
    bufs = {"ya": ya, "xa": xa, "xd": xd, "yd": yd, "adzr": adzr, "adzl": adzl, "bzr": bzr, "bzl": bzl, "by": by, "bx": bx, "sib": sib}
    ranges = (1024, 512, 0)
    copies = [pltpu.make_async_copy(g_in.at[..., pl.ds(c0, 512)], g.at[..., pl.ds(c0, 512)], local_sems.at[i]) for i, c0 in enumerate(ranges)]
    for cp in copies:
        cp.start()
    parts = [Scatter(net, w, g, bufs, c0, 512) for c0 in ranges]
    ids = [[net.pair(), net.pair()] for _ in range(4)]
    def rows_out(k, src, dst, local):
        for d in range(4):
            t2 = (w.t + d) % 4
            here = lambda t2=t2: src.at[pl.ds(pl.multiple_of(t2 * 64, 64), 64)]
            there = lambda: dst.at[w.t // 2, w.t % 2]
            net.send(ids[d][k], True if d else jnp.logical_not(same), here, there, w.at(e=w.c, c=w.e, t=t2))
        cp = pltpu.make_async_copy(src.at[pl.ds(pl.multiple_of(w.t * 64, 64), 64)], dst.at[w.t // 2, w.t % 2], local)
        pl.when(same)(lambda: cp.start())
        return cp
    def rows_in(k, dst):
        for d in range(4):
            t2 = (w.t + 4 - d) % 4
            net.recv(ids[d][k], True if d else jnp.logical_not(same), lambda t2=t2: dst.at[t2 // 2, t2 % 2], w.at(e=w.c, c=w.e, t=t2))
    own = []
    def finish(p):
        for (c0, cn), ref in zip(PIECES, (o_qkv, o_out, o_up, o_down)):
            if ranges[p] <= c0 < ranges[p] + 512:
                cols = pl.ds(c0, cn)
                ref[:, pl.ds(pl.multiple_of(w.e * cn, 128), cn)] = g[w.t, w.y, w.e, w.c, :, cols].astype(jnp.float32)
                ref[:, pl.ds(pl.multiple_of((1 - w.e) * cn, 128), cn)] = sib[:, cols].astype(jnp.float32)
    for s in range(11):
        for p, start in ((0, 0), (1, 2), (2, 4)):
            k = s - start
            if 0 <= k <= 6:
                if k == 0:
                    copies[p].wait()
                parts[p].stage(k)
                if k == 6:
                    finish(p)
        if s == 0:
            own.append(rows_out(0, lo, lo_out, local_sems.at[3]))
        if s == 2:
            own.append(rows_out(1, ig, ig_out, local_sems.at[4]))
    for cp in own:
        pl.when(same)(lambda cp=cp: cp.wait())
    rows_in(0, lo_out)
    rows_in(1, ig_out)
    net.drain()

N_SCATTER = 101

def run_scatter(g, lo, ig):
    any_ = pl.BlockSpec(memory_space=pl.ANY)
    vm = pl.BlockSpec(memory_space=pltpu.VMEM)
    f32, bf = jnp.float32, jnp.bfloat16
    n = g.shape[-1]
    share = lo.shape[0] // 4
    sd = jax.ShapeDtypeStruct
    return pl.pallas_call(
        scatter_kernel,
        out_shape=(sd((128, 768), f32), sd((128, 256), f32), sd((128, 1024), f32), sd((128, 1024), f32),
                   sd((2, 2, share, lo.shape[1]), lo.dtype), sd((2, 2, share, ig.shape[1]), ig.dtype)),
        in_specs=[any_, vm, vm],
        out_specs=(vm, vm, vm, vm, any_, any_),
        scratch_shapes=[pltpu.VMEM(g.shape, bf),
                        pltpu.VMEM((4, 2, 2, 48, n), bf), pltpu.VMEM((4, 2, 48, n), bf),
                        pltpu.VMEM((4, 2, 2, 48, n), bf), pltpu.VMEM((4, 2, 48, n), bf),
                        pltpu.VMEM((4, 2, 96, n), bf), pltpu.VMEM((4, 2, 96, n), bf),
                        pltpu.VMEM((4, 2, 2, 2, 32, n), bf), pltpu.VMEM((4, 2, 2, 2, 32, n), bf),
                        pltpu.VMEM((2, 2, 32, n), bf), pltpu.VMEM((2, 32, n), bf), pltpu.VMEM((128, n), bf),
                        pltpu.SemaphoreType.DMA((N_SCATTER,)), pltpu.SemaphoreType.DMA((N_SCATTER,)), pltpu.SemaphoreType.DMA((5,))],
        compiler_params=pltpu.CompilerParams(collective_id=1, has_side_effects=True),
        name="scatter",
    )(g, lo, ig)


def swap_cores(value):
    return lax.ppermute(value, "fsdp", [(i, i ^ 1) for i in range(lax.axis_size("fsdp"))])


def own_rows(part):
    half = part.shape[0] // 2
    return part[:half] + swap_cores(part[half:].astype(jnp.bfloat16)).astype(jnp.float32)


def both_rows(rows_mine):
    return jnp.concatenate([rows_mine, swap_cores(rows_mine)], axis=0)


def dot32(spec, left, right):
    return jnp.einsum(spec, left, right, preferred_element_type=jnp.float32)


def fast_local(
    inputs, out_grad, segment_ids, w_qkv, bias_qv, w_out, w_up, bias_up, w_down, gains, shifts
):
    w = Where()
    bf, f32 = jnp.bfloat16, jnp.float32
    rows, model_width = inputs.shape[2:]
    tokens = 2 * rows
    score_scale = HD ** (-0.5)
    halves = [a.reshape(128, 2, -1) for a in (w_qkv, w_out, w_up, w_down)]
    mine = jnp.concatenate(halves, axis=-1).transpose(1, 0, 2)
    norms_in = jnp.concatenate([gains, shifts], axis=1).T
    small = jnp.concatenate(
        [
            jnp.broadcast_to(norms_in, (2, 6, 128)),
            bias_qv.reshape(2, 2, 128),
            bias_up.reshape(2, 4, 128),
            jnp.zeros((2, 4, 128), bf),
        ],
        axis=1,
    )
    ids_other = swap_cores(segment_ids)
    full, small_full, x_all, upstream = run_gather(mine, small, inputs, out_grad)
    full = full.reshape(4, model_width, -1)
    small_full = small_full.reshape(4, 8, 16, 128)
    norm_all = small_full[0, :, :6].transpose(1, 0, 2).reshape(6, model_width).astype(f32)
    gain_rows, shift_rows = norm_all[:2], norm_all[2:]
    qv_bias = small_full[:, 0, 6:8].astype(f32).reshape(4, 1, 2, 2, HD)
    up_bias = small_full[:, 0, 8:12].astype(f32).reshape(4, 1, -1)
    full_qkv, full_out, full_up, full_down = (full[:, :, c0 : c0 + cn] for c0, cn in PIECES)

    ids = jnp.where(w.e == w.c, segment_ids, ids_other).reshape(4, 2, rows)
    ids = lax.dynamic_index_in_dim(ids, w.t, 0, keepdims=False)
    ids = jnp.where(w.e == 0, ids, ids[::-1]).reshape(tokens)
    same_segment = ids[:, None] == ids[None, :]

    x_low = x_all.reshape(tokens, model_width)
    projected = dot32("nk,tkc->tnc", x_low, full_qkv).reshape(4, tokens, 2, 3, HD)
    queries = (projected[:, :, :, 0] + qv_bias[:, :, :, 0]).astype(bf)
    key_rows = projected[:, :, :, 1].astype(bf)
    value_rows = (projected[:, :, :, 2] + qv_bias[:, :, :, 1]).astype(bf)

    def get_scores():
        scores = dot32("tqhe,tkhe->thqk", queries, key_rows) * score_scale
        return jnp.where(same_segment, scores, masked_score)

    scores = get_scores()
    row_max = jnp.max(scores, axis=-1, keepdims=True)
    weights = jnp.exp(scores - row_max)
    row_total = jnp.sum(weights, axis=-1, keepdims=True)
    probabilities = weights / row_total
    p_low = probabilities.astype(bf)
    attended_low = dot32("thqk,tkhe->tqhe", p_low, value_rows).astype(bf).reshape(4, tokens, 128)
    attention_part = dot32("tnc,tkc->nk", attended_low, full_out)
    first_sum = x_all[0].astype(f32) + own_rows(attention_part) + shift_rows[0]
    first_norm, first_back = jax.vjp(norm_rows, first_sum, gain_rows[0], shift_rows[1])
    norm_low = both_rows(first_norm.astype(bf))
    before_act = dot32("nk,tkc->tnc", norm_low, full_up) + up_bias
    activated, gelu_back = jax.vjp(exact_gelu, before_act)
    hidden = activated.astype(bf)
    down_part = dot32("tnc,tkc->nk", hidden, full_down)
    second_sum = first_norm + own_rows(down_part) + shift_rows[2]
    result, second_back = jax.vjp(norm_rows, second_sum, gain_rows[1], shift_rows[3])
    layer_mine = result.astype(bf)
    second_grad, gain_two, shift_three = second_back(upstream.astype(f32))
    shift_two = jnp.sum(second_grad, axis=0)
    second_low = both_rows(second_grad.astype(bf))
    down_step = dot32("nk,tnc->tkc", second_low, hidden)
    hidden_grad = dot32("nk,tkc->tnc", second_low, full_down)
    (act_grad,) = gelu_back(hidden_grad)
    up_bias_grad = jnp.sum(act_grad, axis=1)
    act_low = act_grad.astype(bf)
    up_step = dot32("nk,tnc->tkc", norm_low, act_low)
    back_part = dot32("tnc,tkc->nk", act_low, full_up)
    norm_grad = second_grad + own_rows(back_part)
    first_grad, gain_one, shift_one = first_back(norm_grad)
    shift_zero = jnp.sum(first_grad, axis=0)
    first_low = both_rows(first_grad.astype(bf))
    out_step = dot32("nk,tnc->tkc", first_low, attended_low)
    attended_grad = dot32("nk,tkc->tnc", first_low, full_out).astype(bf).reshape(4, tokens, 2, HD)
    value_grad = dot32("thqk,tqhe->tkhe", p_low, attended_grad)
    prob_grad = dot32("tqhe,tkhe->thqk", attended_grad, value_rows)
    row_dot = jnp.sum(prob_grad * probabilities, axis=-1, keepdims=True)
    score_grad = (probabilities * (prob_grad - row_dot)).astype(bf)
    query_grad = dot32("thqk,tkhe->tqhe", score_grad, key_rows) * score_scale
    key_grad = dot32("thqk,tqhe->tkhe", score_grad, queries) * score_scale
    qv_grad = jnp.stack([jnp.sum(query_grad, axis=1), jnp.sum(value_grad, axis=1)], axis=2)
    mixed_grad = jnp.stack([query_grad, key_grad, value_grad], axis=3).astype(bf)
    mixed_grad = mixed_grad.reshape(4, tokens, 6 * HD)
    qkv_step = dot32("nk,tnc->tkc", x_low, mixed_grad)
    input_part = dot32("tnc,tkc->nk", mixed_grad, full_qkv)
    input_mine = (first_grad + own_rows(input_part)).astype(bf)

    norm_sums = jnp.stack([gain_one, gain_two, shift_zero, shift_one, shift_two, shift_three])
    head_sums = jnp.concatenate([qv_grad.reshape(4, 256), up_bias_grad.reshape(4, 512)], axis=1)
    head_sums = jnp.stack([jnp.where(w.e == i, head_sums, 0.0) for i in range(2)])
    norm_sums, head_sums = lax.psum((norm_sums, head_sums), ("fsdp", "ctx", "tp"))
    head_mine = lax.dynamic_index_in_dim(head_sums, w.t, 1, keepdims=False)
    block = (2 * w.y + w.e) * 2 + w.c
    norm_mine = lax.dynamic_slice_in_dim(norm_sums, block * 128, 128, 1)

    steps = jnp.concatenate(
        [a.astype(bf) for a in (qkv_step, out_step, up_step, down_step)], axis=-1
    )
    g_qkv, g_out, g_up, g_down, layer_out, input_out = run_scatter(
        steps.reshape(4, 2, 2, 2, 128, -1), layer_mine, input_mine
    )
    return (
        layer_out,
        input_out.astype(f32),
        g_qkv,
        head_mine[:, :256].reshape(-1),
        g_out,
        g_up,
        head_mine[:, 256:].reshape(-1),
        g_down,
        norm_mine[:2].T,
        norm_mine[2:].T,
    )


def fits_fast(mesh):
    return dict(mesh.shape) == {"fsdp": 4, "ctx": 2, "tp": 4}


def solution(mesh):
    placed = (
        P(None, "fsdp", "ctx", None),
        P(None, "fsdp", "ctx", None),
        P(None, "fsdp", None),
        P(("fsdp", "ctx"), "tp"),
        P("tp"),
        P(("fsdp", "ctx"), "tp"),
        P(("fsdp", "ctx"), "tp"),
        P("tp"),
        P(("fsdp", "ctx"), "tp"),
        P(("fsdp", "ctx"), None),
        P(("fsdp", "ctx"), None),
    )
    return jax.shard_map(
        fast_local if fits_fast(mesh) else local,
        mesh=mesh,
        in_specs=placed,
        out_specs=(
            P(None, "fsdp", ("ctx", "tp"), None),
            P(None, "fsdp", ("ctx", "tp"), None),
            P(("fsdp", "ctx"), "tp"),
            P("tp"),
            P(("fsdp", "ctx"), "tp"),
            P(("fsdp", "ctx"), "tp"),
            P("tp"),
            P(("fsdp", "ctx"), "tp"),
            P(("fsdp", "ctx"), None),
            P(("fsdp", "ctx"), None),
        ),
        check_vma=False,
    )
```

```python
import jax
import jax.numpy as jnp
from jax import lax
from jax.experimental import pallas as pl
from jax.experimental.pallas import tpu as pltpu
from jax.sharding import PartitionSpec as P

HD = 64


norm_epsilon = 1e-12
masked_score = -1e30


def norm_rows(rows_in, gain_row, offset):
    average = jnp.mean(rows_in, axis=-1, keepdims=True)
    centered = rows_in - average
    spread = jnp.mean(centered * centered, axis=-1, keepdims=True)
    return centered * lax.rsqrt(spread + norm_epsilon) * gain_row + offset


def exact_gelu(rows_in):
    return jax.nn.gelu(rows_in, approximate=False)


def contract_rows(left_rows, right_rows):
    return lax.dot_general(
        left_rows, right_rows, (((0,), (0,)), ((), ())), preferred_element_type=jnp.float32
    )


def times_transposed(left_rows, right_rows):
    return lax.dot_general(
        left_rows, right_rows, (((1,), (1,)), ((), ())), preferred_element_type=jnp.float32
    )


def masked_scores(queries, key_rows, same_segment, score_scale):
    scores = (
        jnp.einsum("sqhe,skhe->shqk", queries, key_rows, preferred_element_type=jnp.float32)
        * score_scale
    )
    return jnp.where(same_segment[:, None], scores, masked_score)


def add_pair(running, update):
    return running + update


def reduce_rows(part):
    return lax.psum(part, "tp")


def local(
    inputs, out_grad, segment_ids, w_qkv, bias_qv, w_out, w_up, bias_up, w_down, gains, shifts
):
    batches, seq_local, rows_local, model_width = inputs.shape
    tokens = seq_local * rows_local
    heads_local = w_out.shape[1] // HD
    score_scale = HD ** (-0.5)
    row_share = rows_local // lax.axis_size("tp")
    row_start = lax.axis_index("tp") * row_share
    query_start = lax.axis_index("ctx") * rows_local
    qv_bias = bias_qv.astype(jnp.float32).reshape(heads_local, 2, HD)
    up_bias = bias_up.astype(jnp.float32)

    def pick_rows(values):
        shaped = values.reshape(seq_local, rows_local, model_width)
        return lax.dynamic_slice_in_dim(shaped, row_start, row_share, 1)

    full_totals = (
        jnp.zeros((model_width, w_qkv.shape[1]), jnp.float32),
        jnp.zeros((model_width, w_out.shape[1]), jnp.float32),
        jnp.zeros((model_width, w_up.shape[1]), jnp.float32),
        jnp.zeros((model_width, w_down.shape[1]), jnp.float32),
        jnp.zeros((model_width, 2), jnp.float32),
        jnp.zeros((model_width, 4), jnp.float32),
    )
    share_totals = (
        jnp.zeros(w_qkv.shape, jnp.float32),
        jnp.zeros(w_out.shape, jnp.float32),
        jnp.zeros(w_up.shape, jnp.float32),
        jnp.zeros(w_down.shape, jnp.float32),
        jnp.zeros(gains.shape, jnp.float32),
        jnp.zeros(shifts.shape, jnp.float32),
    )
    qv_bias_grad = jnp.zeros(bias_qv.shape, jnp.float32)
    up_bias_grad = jnp.zeros(bias_up.shape, jnp.float32)
    layer_rows = []
    input_rows = []
    for batch_index in range(batches):
        gathered = (
            lax.all_gather(w_qkv, ("fsdp", "ctx"), axis=0, tiled=True),
            lax.all_gather(w_out, ("fsdp", "ctx"), axis=0, tiled=True),
            lax.all_gather(w_up, ("fsdp", "ctx"), axis=0, tiled=True),
            lax.all_gather(w_down, ("fsdp", "ctx"), axis=0, tiled=True),
            lax.all_gather(gains, ("fsdp", "ctx"), axis=0, tiled=True),
            lax.all_gather(shifts, ("fsdp", "ctx"), axis=0, tiled=True),
        )
        full_qkv, full_out, full_up, full_down, full_gains, full_shifts = gathered
        gain_rows = full_gains.astype(jnp.float32)
        shift_rows = full_shifts.astype(jnp.float32)
        x_low = inputs[batch_index].reshape(tokens, model_width)
        x_full = x_low.astype(jnp.float32)
        projected = jnp.dot(x_low, full_qkv, preferred_element_type=jnp.float32)
        projected = projected.reshape(seq_local, rows_local, heads_local, 3, HD)
        queries = (projected[:, :, :, 0] + qv_bias[:, 0]).astype(jnp.bfloat16)
        key_local = projected[:, :, :, 1].astype(jnp.bfloat16)
        value_local = (projected[:, :, :, 2] + qv_bias[:, 1]).astype(jnp.bfloat16)
        joined = jnp.concatenate([key_local, value_local], axis=-1)
        joined_all = lax.all_gather(joined, "ctx", axis=1, tiled=True)
        key_rows = joined_all[..., :HD]
        value_rows = joined_all[..., HD:]
        segments = segment_ids[batch_index]
        query_segments = lax.dynamic_slice_in_dim(segments, query_start, rows_local, 1)
        same_segment = query_segments[:, :, None] == segments[:, None, :]
        scores = masked_scores(queries, key_rows, same_segment, score_scale)
        row_max = jnp.max(scores, axis=-1, keepdims=True)
        weights = jnp.exp(scores - row_max)
        row_total = jnp.sum(weights, axis=-1, keepdims=True)
        log_total = row_max + jnp.log(row_total)
        p_low = (weights / row_total).astype(jnp.bfloat16)
        attended = jnp.einsum(
            "shqk,skhe->sqhe", p_low, value_rows, preferred_element_type=jnp.float32
        )
        attended_low = attended.reshape(tokens, heads_local * HD).astype(jnp.bfloat16)
        attention_part = times_transposed(attended_low, full_out)
        upstream_full = out_grad[batch_index].reshape(tokens, model_width).astype(jnp.float32)
        attention_total = reduce_rows(attention_part)
        first_sum = x_full + attention_total + shift_rows[:, 0]
        first_norm, first_back = jax.vjp(norm_rows, first_sum, gain_rows[:, 0], shift_rows[:, 1])
        norm_low = first_norm.astype(jnp.bfloat16)
        before_act = jnp.dot(norm_low, full_up, preferred_element_type=jnp.float32) + up_bias
        activated, gelu_back = jax.vjp(exact_gelu, before_act)
        hidden = activated.astype(jnp.bfloat16)
        down_part = times_transposed(hidden, full_down)
        down_total = reduce_rows(down_part)
        second_sum = first_norm + down_total + shift_rows[:, 2]
        result, second_back = jax.vjp(norm_rows, second_sum, gain_rows[:, 1], shift_rows[:, 3])
        layer_rows.append(pick_rows(result).astype(jnp.bfloat16))
        second_grad, gain_two, shift_three = second_back(upstream_full)
        shift_two = jnp.sum(second_grad, axis=0)
        second_low = second_grad.astype(jnp.bfloat16)
        down_step = contract_rows(second_low, hidden)
        hidden_grad = jnp.dot(second_low, full_down, preferred_element_type=jnp.float32)
        (act_grad,) = gelu_back(hidden_grad)
        up_bias_grad = up_bias_grad + jnp.sum(act_grad, axis=0)
        act_low = act_grad.astype(jnp.bfloat16)
        up_step = contract_rows(norm_low, act_low)
        back_part = times_transposed(act_low, full_up)
        back_total = reduce_rows(back_part)
        norm_grad = second_grad + back_total
        first_grad, gain_one, shift_one = first_back(norm_grad)
        shift_zero = jnp.sum(first_grad, axis=0)
        first_low = first_grad.astype(jnp.bfloat16)
        out_step = contract_rows(first_low, attended_low)
        attended_grad = jnp.dot(first_low, full_out, preferred_element_type=jnp.float32)
        attended_grad = attended_grad.astype(jnp.bfloat16).reshape(
            seq_local, rows_local, heads_local, HD
        )
        scores = masked_scores(queries, key_rows, same_segment, score_scale)
        probabilities = jnp.exp(scores - log_total)
        value_grad = jnp.einsum(
            "shqk,sqhe->skhe",
            probabilities.astype(jnp.bfloat16),
            attended_grad,
            preferred_element_type=jnp.float32,
        )
        prob_grad = jnp.einsum(
            "sqhe,skhe->shqk", attended_grad, value_rows, preferred_element_type=jnp.float32
        )
        row_dot = jnp.sum(prob_grad * probabilities, axis=-1, keepdims=True)
        score_grad = (probabilities * (prob_grad - row_dot)).astype(jnp.bfloat16)
        query_grad = (
            jnp.einsum("shqk,skhe->sqhe", score_grad, key_rows, preferred_element_type=jnp.float32)
            * score_scale
        )
        key_grad = (
            jnp.einsum("shqk,sqhe->skhe", score_grad, queries, preferred_element_type=jnp.float32)
            * score_scale
        )
        kv_grads = lax.psum_scatter(
            jnp.concatenate([key_grad, value_grad], axis=-1).astype(jnp.bfloat16),
            "ctx",
            scatter_dimension=1,
            tiled=True,
        ).astype(jnp.float32)
        key_mine = kv_grads[..., :HD]
        value_mine = kv_grads[..., HD:]
        bias_step = jnp.stack(
            [jnp.sum(query_grad, axis=(0, 1)), jnp.sum(value_mine, axis=(0, 1))], axis=1
        )
        qv_bias_grad = qv_bias_grad + bias_step.reshape(-1)
        mixed_grad = jnp.stack([query_grad, key_mine, value_mine], axis=3)
        mixed_grad = mixed_grad.reshape(tokens, 3 * heads_local * HD).astype(jnp.bfloat16)
        qkv_step = contract_rows(x_low, mixed_grad)
        input_part = times_transposed(mixed_grad, full_qkv).reshape(
            seq_local, rows_local, model_width
        )
        input_mine = lax.psum_scatter(
            input_part.astype(jnp.bfloat16), "tp", scatter_dimension=1, tiled=True
        ).astype(jnp.float32)
        first_part = pick_rows(first_grad)
        input_rows.append(input_mine + first_part)
        gain_step = jnp.stack([gain_one, gain_two], axis=1)
        shift_step = jnp.stack([shift_zero, shift_one, shift_two, shift_three], axis=1)
        full_totals = tuple(
            map(
                add_pair,
                full_totals,
                (qkv_step, out_step, up_step, down_step, gain_step, shift_step),
            )
        )
    share_totals = (
        lax.psum_scatter(
            full_totals[0].astype(jnp.bfloat16), ("fsdp", "ctx"), scatter_dimension=0, tiled=True
        ).astype(jnp.float32),
        lax.psum_scatter(
            full_totals[1].astype(jnp.bfloat16), ("fsdp", "ctx"), scatter_dimension=0, tiled=True
        ).astype(jnp.float32),
        lax.psum_scatter(
            full_totals[2].astype(jnp.bfloat16), ("fsdp", "ctx"), scatter_dimension=0, tiled=True
        ).astype(jnp.float32),
        lax.psum_scatter(
            full_totals[3].astype(jnp.bfloat16), ("fsdp", "ctx"), scatter_dimension=0, tiled=True
        ).astype(jnp.float32),
        lax.psum_scatter(
            full_totals[4].astype(jnp.bfloat16), ("fsdp", "ctx"), scatter_dimension=0, tiled=True
        ).astype(jnp.float32),
        lax.psum_scatter(
            full_totals[5].astype(jnp.bfloat16), ("fsdp", "ctx"), scatter_dimension=0, tiled=True
        ).astype(jnp.float32),
    )
    qv_total, up_total = lax.psum((qv_bias_grad, up_bias_grad), ("fsdp", "ctx"))
    return (
        jnp.stack(layer_rows, axis=0),
        jnp.stack(input_rows, axis=0),
        share_totals[0],
        qv_total,
        share_totals[1],
        share_totals[2],
        up_total,
        share_totals[3],
        share_totals[4],
        share_totals[5],
    )


MESH = pl.DeviceIdType.MESH
ROW_A, ROW_D, ROW_AD, ROW_B = (0, 48), (48, 48), (0, 96), (96, 32)

class Where:
    def __init__(self):
        fsdp = lax.axis_index("fsdp")
        self.y = fsdp // 2
        self.e = fsdp % 2
        self.c = lax.axis_index("ctx")
        self.t = lax.axis_index("tp")
    def at(self, y=None, e=None, c=None, t=None):
        y = self.y if y is None else y
        e = self.e if e is None else e
        c = self.c if c is None else c
        t = self.t if t is None else t
        return (2 * y + e, c, t)

def when(cond, fn):
    if cond is True:
        fn()
    else:
        pl.when(cond)(fn)

class Net:
    def __init__(self, send_sems, recv_sems):
        self.send_sems, self.recv_sems, self.count, self.pending = send_sems, recv_sems, 0, []
    def pair(self):
        self.count += 1
        return self.count - 1
    def send(self, index, cond, src, dst, device):
        def make():
            return pltpu.make_async_remote_copy(
                src_ref=src(), dst_ref=dst(), send_sem=self.send_sems.at[index],
                recv_sem=self.recv_sems.at[index], device_id=device, device_id_type=MESH)
        when(cond, lambda: make().start())
        self.pending.append((cond, make))
    def recv(self, index, cond, here, device):
        def wait():
            pltpu.make_async_remote_copy(
                src_ref=here(), dst_ref=here(), send_sem=self.send_sems.at[index],
                recv_sem=self.recv_sems.at[index], device_id=device, device_id_type=MESH).wait_recv()
        when(cond, wait)
    def drain(self):
        for cond, make in self.pending:
            when(cond, lambda make=make: make().wait_send())

def slots_of(w):
    t = w.t
    return [("own", t, True), ("l1", t - 1, t >= 1), ("r1", t + 1, t <= 2), ("l2", t - 2, t >= 2),
            ("r2", t + 2, t <= 1), ("l3", t - 3, t >= 3), ("r3", t + 3, t <= 0)]

class Gather:
    STAGES = 7
    def __init__(self, net, w, mine, full, c0, cn, local_sem, routes=(ROW_A, ROW_D, ROW_AD, ROW_B)):
        self.net, self.w, self.mine, self.full, self.local_sem = net, w, mine, full, local_sem
        self.cols = pl.ds(c0, cn)
        self.row_a, self.row_d, self.row_ad, self.row_b = [None if r is None else pl.ds(*r) for r in routes]
        self.slots = slots_of(w)
        self.ids = {}
    def id(self, key):
        if key not in self.ids:
            self.ids[key] = self.net.pair()
        return self.ids[key]
    def blk(self, tt, rows, y=None, c=None):
        w = self.w
        y = w.y if y is None else y
        c = w.c if c is None else c
        return lambda: self.full.at[tt, y, :, c, rows, self.cols]
    def row(self, tt, rows, y=None):
        y = self.w.y if y is None else y
        return lambda: self.full.at[tt, y, :, :, rows, self.cols]
    def colm(self, tt, rows, c=None):
        c = self.w.c if c is None else c
        return lambda: self.full.at[tt, :, :, c, rows, self.cols]
    def plane(self, tt, rows):
        return lambda: self.full.at[tt, :, :, :, rows, self.cols]
    def same(self, key, cond, ref, device):
        self.net.send(self.id(key), cond, ref, ref, device)
    def sib(self):
        w = self.w
        dst = lambda: self.full.at[w.t, w.y, w.e, w.c, :, self.cols]
        self.net.send(self.id("sib"), True, lambda: self.mine.at[1 - w.e, :, self.cols], dst, w.at(e=1 - w.e))
        cp = pltpu.make_async_copy(self.mine.at[w.e, :, self.cols], dst(), self.local_sem)
        cp.start()
        self.own_copy = cp
    def zsend(self, tag, slot, ref):
        w = self.w
        k = {"own": 0, "l1": 1, "r1": 1, "l2": 2, "r2": 2}[slot]
        if slot == "own" or slot[0] == "l":
            name, tt, ok = self.slot("own" if k == 0 else f"l{k}")
            self.same((tag, "zr", k), (w.t < 3) if ok is True else jnp.logical_and(ok, w.t < 3), ref(tt), w.at(t=w.t + 1))
        if slot == "own" or slot[0] == "r":
            name, tt, ok = self.slot("own" if k == 0 else f"r{k}")
            self.same((tag, "zl", k), (w.t > 0) if ok is True else jnp.logical_and(ok, w.t > 0), ref(tt), w.at(t=w.t - 1))
    def zrecv(self, tag, slot, ref):
        w = self.w
        k = int(slot[1])
        _, tt, ok = self.slot(slot)
        if slot[0] == "l":
            self.net.recv(self.id((tag, "zr", k - 1)), ok, ref(tt), w.at(t=w.t - 1))
        else:
            self.net.recv(self.id((tag, "zl", k - 1)), ok, ref(tt), w.at(t=w.t + 1))
    def slot(self, name):
        return next(s for s in self.slots if s[0] == name)
    def first_hop(self, name):
        w = self.w
        _, tt, ok = self.slot(name)
        self.same(("ax", name), ok, self.blk(tt, self.row_a), w.at(c=1 - w.c))
        if self.row_d is not None:
            self.same(("dy", name), ok, self.blk(tt, self.row_d), w.at(y=1 - w.y))
    def second_hop(self, name):
        w = self.w
        _, tt, ok = self.slot(name)
        self.net.recv(self.id(("ax", name)), ok, self.blk(tt, self.row_a, c=1 - w.c), w.at(c=1 - w.c))
        self.same(("ay", name), ok, self.row(tt, self.row_a), w.at(y=1 - w.y))
        if self.row_d is not None:
            self.net.recv(self.id(("dy", name)), ok, self.blk(tt, self.row_d, y=1 - w.y), w.at(y=1 - w.y))
            self.same(("dx", name), ok, self.colm(tt, self.row_d), w.at(c=1 - w.c))
    def last(self, name):
        w = self.w
        _, tt, ok = self.slot(name)
        self.net.recv(self.id(("ay", name)), ok, self.row(tt, self.row_a, y=1 - w.y), w.at(y=1 - w.y))
        if self.row_d is not None:
            self.net.recv(self.id(("dx", name)), ok, self.colm(tt, self.row_d, c=1 - w.c), w.at(c=1 - w.c))
    def stage(self, k):
        w = self.w
        ad = lambda tt: self.blk(tt, self.row_ad)
        bz = lambda tt: self.plane(tt, self.row_b)
        b = self.row_b is not None
        if k == 0:
            self.sib()
        elif k == 1:
            self.own_copy.wait()
            self.net.recv(self.id("sib"), True, lambda: self.full.at[w.t, w.y, 1 - w.e, w.c, :, self.cols], w.at(e=1 - w.e))
            self.zsend("ad", "own", ad)
            if b:
                self.same("bx", True, self.blk(w.t, self.row_b), w.at(c=1 - w.c))
            self.first_hop("own")
        elif k == 2:
            if b:
                self.net.recv(self.id("bx"), True, self.blk(w.t, self.row_b, c=1 - w.c), w.at(c=1 - w.c))
                self.same("by", True, self.row(w.t, self.row_b), w.at(y=1 - w.y))
            for s in ("l1", "r1"):
                self.zrecv("ad", s, ad)
                self.zsend("ad", s, ad)
                self.first_hop(s)
            self.second_hop("own")
        elif k == 3:
            if b:
                self.net.recv(self.id("by"), True, self.row(w.t, self.row_b, y=1 - w.y), w.at(y=1 - w.y))
                self.zsend("b", "own", bz)
            for s in ("l2", "r2"):
                self.zrecv("ad", s, ad)
                self.zsend("ad", s, ad)
                self.first_hop(s)
            for s in ("l1", "r1"):
                self.second_hop(s)
        elif k == 4:
            if b:
                for s in ("l1", "r1"):
                    self.zrecv("b", s, bz)
                    self.zsend("b", s, bz)
            for s in ("l3", "r3"):
                self.zrecv("ad", s, ad)
                self.first_hop(s)
            for s in ("l2", "r2"):
                self.second_hop(s)
        elif k == 5:
            if b:
                for s in ("l2", "r2"):
                    self.zrecv("b", s, bz)
                    self.zsend("b", s, bz)
            for s in ("l3", "r3"):
                self.second_hop(s)
        elif k == 6:
            if b:
                for s in ("l3", "r3"):
                    self.zrecv("b", s, bz)
            for name, _, _ in self.slots:
                self.last(name)

def barrier(w, extra=()):
    sem = pltpu.get_barrier_semaphore()
    one = lambda dev: pl.semaphore_signal(sem, inc=1, device_id=dev, device_id_type=MESH)
    one(w.at(e=1 - w.e)); one(w.at(c=1 - w.c)); one(w.at(y=1 - w.y))
    pl.when(w.t > 0)(lambda: one(w.at(t=w.t - 1)))
    pl.when(w.t < 3)(lambda: one(w.at(t=w.t + 1)))
    ends = jnp.where(w.t == 0, 1, 0) + jnp.where(w.t == 3, 1, 0)
    return sem, one, 5 - ends

def gather_kernel(mine, small, x_in, g_in, full, small_full, x_all, g_own, send_sems, recv_sems, local_sems):
    w = Where()
    sem, one, need = barrier(w)
    cross = w.e != w.c
    diag = w.at(e=1 - w.e, c=1 - w.c)
    pl.when(cross)(lambda: one(diag))
    pl.semaphore_wait(sem, need + jnp.where(cross, 1, 0))
    net = Net(send_sems, recv_sems)
    seq = lambda ref: ref.at[w.t // 2, w.t % 2]
    parts = [Gather(net, w, small, small_full, 0, 128, local_sems.at[0], routes=((0, 16), None, (0, 16), None))]
    parts += [Gather(net, w, mine, full, 512 * i, 512, local_sems.at[1 + i]) for i in range(3)]
    xi, gi, xs = net.pair(), net.pair(), net.pair()
    parts[1].stage(0)
    parts[0].stage(0)
    for idx, src, dst in ((xi, x_in, x_all.at[0]), (gi, g_in, g_own)):
        net.send(idx, cross, lambda src=src: seq(src), lambda dst=dst: dst, diag)
    local = [pltpu.make_async_copy(seq(x_in), x_all.at[0], local_sems.at[4]),
             pltpu.make_async_copy(seq(g_in), g_own, local_sems.at[5])]
    for cp in local:
        pl.when(jnp.logical_not(cross))(lambda cp=cp: cp.start())
    parts[2].stage(0)
    parts[3].stage(0)
    parts[1].stage(1)
    parts[0].stage(1)
    pl.when(jnp.logical_not(cross))(lambda: local[0].wait())
    net.recv(xi, cross, lambda: x_all.at[0], diag)
    net.send(xs, True, lambda: x_all.at[0], lambda: x_all.at[1], w.at(e=1 - w.e))
    for s in range(2, 12):
        for i, start in ((1, 0), (0, 0), (2, 2), (3, 4)):
            k = s - start
            if 1 <= k <= 6:
                parts[i].stage(k)
    pl.when(jnp.logical_not(cross))(lambda: local[1].wait())
    net.recv(gi, cross, lambda: g_own, diag)
    net.recv(xs, True, lambda: x_all.at[1], w.at(e=1 - w.e))
    net.drain()

N_GATHER = 153

def run_gather(mine, small, x_in, g_in):
    any_ = pl.BlockSpec(memory_space=pl.ANY)
    vm = pl.BlockSpec(memory_space=pltpu.VMEM)
    rows, width = x_in.shape[2:]
    return pl.pallas_call(
        gather_kernel,
        out_shape=(jax.ShapeDtypeStruct((4, 2, 2, 2) + mine.shape[1:], mine.dtype),
                   jax.ShapeDtypeStruct((4, 2, 2, 2) + small.shape[1:], small.dtype),
                   jax.ShapeDtypeStruct((2, rows, width), x_in.dtype),
                   jax.ShapeDtypeStruct((rows, width), g_in.dtype)),
        in_specs=[vm, vm, vm, vm],
        out_specs=(any_, any_, any_, any_),
        scratch_shapes=[pltpu.SemaphoreType.DMA((N_GATHER,)), pltpu.SemaphoreType.DMA((N_GATHER,)), pltpu.SemaphoreType.DMA((6,))],
        compiler_params=pltpu.CompilerParams(collective_id=0, has_side_effects=True),
        name="gather",
    )(mine, small, x_in, g_in)


ROWS = {"a": pl.ds(0, 48), "d": pl.ds(48, 48), "ad": pl.ds(0, 96), "b": pl.ds(96, 32)}

class Scatter:
    def __init__(self, net, w, g, bufs, c0, cn):
        self.net, self.w, self.g, self.bufs = net, w, g, bufs
        self.cols = pl.ds(c0, cn)
        self.ids = {}
    def id(self, key):
        if key not in self.ids:
            self.ids[key] = self.net.pair()
        return self.ids[key]
    def take(self, key, cond, buf, place, device):
        cols = self.cols
        def body():
            self.net.recv(self.id(key), True, lambda: buf(), device)
            ref = place()
            ref[...] = (ref[...].astype(jnp.float32) + buf()[...].astype(jnp.float32)).astype(ref.dtype)
        when(cond, body)
    def zstep(self, tag, m, place):
        w = self.w
        for way, me, targets in (("r", m, [j for j in (3, 2, 1) if j >= m]), ("l", 3 - m, [j for j in (0, 1, 2) if j <= 3 - m])):
            buf = self.bufs[tag + "z" + way]
            nxt = w.at(t=w.t + 1) if way == "r" else w.at(t=w.t - 1)
            prv = w.at(t=w.t - 1) if way == "r" else w.at(t=w.t + 1)
            here = w.t == me
            for j in targets:
                land = lambda j=j, buf=buf: buf.at[j, ..., self.cols]
                if m > 0:
                    self.take((tag, way, j), here, land, place(j), prv)
                if j != me:
                    self.net.send(self.id((tag, way, j)), here, place(j), land, nxt)
    def stage(self, k):
        w, g, cols, b = self.w, self.g, self.cols, self.bufs
        X, Y = w.at(c=1 - w.c), w.at(y=1 - w.y)
        ad = lambda j: (lambda: g.at[j, w.y, :, w.c, ROWS["ad"], cols])
        bz = lambda j: (lambda: g.at[j, :, :, :, ROWS["b"], cols])
        order = (3, 0, 2, 1)
        if k == 0:
            self.zstep("b", 0, bz)
            for j in order:
                self.net.send(self.id(("ya", j)), True, lambda j=j: g.at[j, 1 - w.y, :, :, ROWS["a"], cols], lambda j=j: b["ya"].at[j, :, :, :, cols], Y)
                self.net.send(self.id(("xd", j)), True, lambda j=j: g.at[j, :, :, 1 - w.c, ROWS["d"], cols], lambda j=j: b["xd"].at[j, :, :, :, cols], X)
        elif k == 1:
            self.zstep("b", 1, bz)
            for j in order:
                self.take(("ya", j), True, lambda j=j: b["ya"].at[j, :, :, :, cols], lambda j=j: g.at[j, w.y, :, :, ROWS["a"], cols], Y)
                self.net.send(self.id(("xa", j)), True, lambda j=j: g.at[j, w.y, :, 1 - w.c, ROWS["a"], cols], lambda j=j: b["xa"].at[j, :, :, cols], X)
                self.take(("xd", j), True, lambda j=j: b["xd"].at[j, :, :, :, cols], lambda j=j: g.at[j, :, :, w.c, ROWS["d"], cols], X)
                self.net.send(self.id(("yd", j)), True, lambda j=j: g.at[j, 1 - w.y, :, w.c, ROWS["d"], cols], lambda j=j: b["yd"].at[j, :, :, cols], Y)
        elif k == 2:
            self.zstep("b", 2, bz)
            for j in order:
                self.take(("xa", j), True, lambda j=j: b["xa"].at[j, :, :, cols], lambda j=j: g.at[j, w.y, :, w.c, ROWS["a"], cols], X)
                self.take(("yd", j), True, lambda j=j: b["yd"].at[j, :, :, cols], lambda j=j: g.at[j, w.y, :, w.c, ROWS["d"], cols], Y)
            self.zstep("ad", 0, ad)
        elif k == 3:
            self.zstep("b", 3, bz)
            self.net.send(self.id("by"), True, lambda: g.at[w.t, 1 - w.y, :, :, ROWS["b"], cols], lambda: b["by"].at[:, :, :, cols], Y)
            self.zstep("ad", 1, ad)
        elif k == 4:
            self.take("by", True, lambda: b["by"].at[:, :, :, cols], lambda: g.at[w.t, w.y, :, :, ROWS["b"], cols], Y)
            self.net.send(self.id("bx"), True, lambda: g.at[w.t, w.y, :, 1 - w.c, ROWS["b"], cols], lambda: b["bx"].at[:, :, cols], X)
            self.zstep("ad", 2, ad)
        elif k == 5:
            self.zstep("ad", 3, ad)
            self.take("bx", True, lambda: b["bx"].at[:, :, cols], lambda: g.at[w.t, w.y, :, w.c, ROWS["b"], cols], X)
            self.net.send(self.id("sib"), True, lambda: g.at[w.t, w.y, 1 - w.e, w.c, :, cols], lambda: b["sib"].at[:, cols], w.at(e=1 - w.e))
        elif k == 6:
            self.net.recv(self.id("sib"), True, lambda: b["sib"].at[:, cols], w.at(e=1 - w.e))

PIECES = ((0, 384), (384, 128), (512, 512), (1024, 512))

def scatter_kernel(g_qkv, g_out, g_up, g_down, lo, ig, sums, o_qkv, o_out, o_up, o_down, lo_out, ig_out, sums_out, g, ya, xa, xd, yd, adzr, adzl, bzr, bzl, by, bx, sib, sums_run, sums_land, send_sems, recv_sems, local_sems):
    w = Where()
    sem, one, need = barrier(w)
    same = w.e == w.c
    for d in range(4):
        go = (lambda d=d: one(w.at(e=w.c, c=w.e, t=(w.t + d) % 4)))
        when(True if d else jnp.logical_not(same), go)
    one(w.at(t=(w.t + 2) % 4))
    pl.semaphore_wait(sem, need + 4 + jnp.where(same, 0, 1))
    net = Net(send_sems, recv_sems)
    bufs = {"ya": ya, "xa": xa, "xd": xd, "yd": yd, "adzr": adzr, "adzl": adzl, "bzr": bzr, "bzl": bzl, "by": by, "bx": bx, "sib": sib}
    ranges = (1024, 512, 0)
    copies = [[pltpu.make_async_copy(src, g.at[..., pl.ds(*PIECES[i])], local_sems.at[5 + i])] for src, i in ((g_down, 3), (g_up, 2), (g_qkv, 0))]
    copies[2].append(pltpu.make_async_copy(g_out, g.at[..., pl.ds(*PIECES[1])], local_sems.at[6]))
    for cp in sum(copies, []):
        cp.start()
    parts = [Scatter(net, w, g, bufs, c0, 512) for c0 in ranges]
    ids = [[net.pair(), net.pair()] for _ in range(4)]
    def rows_out(k, src, dst, local):
        for d in range(4):
            t2 = (w.t + d) % 4
            here = lambda t2=t2: src.at[pl.ds(pl.multiple_of(t2 * 64, 64), 64)]
            there = lambda: dst.at[w.t // 2, w.t % 2]
            net.send(ids[d][k], True if d else jnp.logical_not(same), here, there, w.at(e=w.c, c=w.e, t=t2))
        cp = pltpu.make_async_copy(src.at[pl.ds(pl.multiple_of(w.t * 64, 64), 64)], dst.at[w.t // 2, w.t % 2], local)
        pl.when(same)(lambda: cp.start())
        return cp
    def rows_in(k, dst):
        for d in range(4):
            t2 = (w.t + 4 - d) % 4
            net.recv(ids[d][k], True if d else jnp.logical_not(same), lambda t2=t2: dst.at[t2 // 2, t2 % 2], w.at(e=w.c, c=w.e, t=t2))
    partners = (w.at(e=1 - w.e), w.at(c=1 - w.c), w.at(y=1 - w.y), w.at(t=w.t + 1 - 2 * (w.t % 2)), w.at(t=(w.t + 2) % 4))
    sums_ids = [net.pair() for _ in partners]
    def sums_step(s):
        if s == 0:
            sums_run[0] = sums[...]
        else:
            net.recv(sums_ids[s - 1], True, lambda: sums_land.at[s - 1], partners[s - 1])
            total = sums_run[s - 1] + sums_land[s - 1]
            if s == 5:
                sums_out[...] = total
            else:
                sums_run[s] = total
        if s < 5:
            net.send(sums_ids[s], True, lambda: sums_run.at[s], lambda: sums_land.at[s], partners[s])
    own = []
    def finish(p):
        for (c0, cn), ref in zip(PIECES, (o_qkv, o_out, o_up, o_down)):
            if ranges[p] <= c0 < ranges[p] + 512:
                cols = pl.ds(c0, cn)
                ref[:, pl.ds(pl.multiple_of(w.e * cn, 128), cn)] = g[w.t, w.y, w.e, w.c, :, cols].astype(jnp.float32)
                ref[:, pl.ds(pl.multiple_of((1 - w.e) * cn, 128), cn)] = sib[:, cols].astype(jnp.float32)
    for s in range(11):
        for p, start in ((0, 0), (1, 2), (2, 4)):
            k = s - start
            if 0 <= k <= 6:
                if k == 0:
                    for cp in copies[p]:
                        cp.wait()
                parts[p].stage(k)
                if k == 6:
                    finish(p)
        if s <= 5:
            sums_step(s)
        if s == 0:
            own.append(rows_out(0, lo, lo_out, local_sems.at[3]))
        if s == 2:
            own.append(rows_out(1, ig, ig_out, local_sems.at[4]))
    for cp in own:
        pl.when(same)(lambda cp=cp: cp.wait())
    rows_in(0, lo_out)
    rows_in(1, ig_out)
    net.drain()

N_SCATTER = 106

def run_scatter(grads, lo, ig, sums):
    any_ = pl.BlockSpec(memory_space=pl.ANY)
    vm = pl.BlockSpec(memory_space=pltpu.VMEM)
    f32, bf = jnp.float32, jnp.bfloat16
    grads = [a.reshape(4, 2, 2, 2, 128, -1) for a in grads]
    n = sum(a.shape[-1] for a in grads)
    share = lo.shape[0] // 4
    sd = jax.ShapeDtypeStruct
    return pl.pallas_call(
        scatter_kernel,
        out_shape=(sd((128, 768), f32), sd((128, 256), f32), sd((128, 1024), f32), sd((128, 1024), f32),
                   sd((2, 2, share, lo.shape[1]), lo.dtype), sd((2, 2, share, ig.shape[1]), ig.dtype), sd(sums.shape, f32)),
        in_specs=[any_] * 4 + [vm] * 3,
        out_specs=(vm, vm, vm, vm, any_, any_, vm),
        scratch_shapes=[pltpu.VMEM((4, 2, 2, 2, 128, n), bf),
                        pltpu.VMEM((4, 2, 2, 48, n), bf), pltpu.VMEM((4, 2, 48, n), bf),
                        pltpu.VMEM((4, 2, 2, 48, n), bf), pltpu.VMEM((4, 2, 48, n), bf),
                        pltpu.VMEM((4, 2, 96, n), bf), pltpu.VMEM((4, 2, 96, n), bf),
                        pltpu.VMEM((4, 2, 2, 2, 32, n), bf), pltpu.VMEM((4, 2, 2, 2, 32, n), bf),
                        pltpu.VMEM((2, 2, 32, n), bf), pltpu.VMEM((2, 32, n), bf), pltpu.VMEM((128, n), bf),
                        pltpu.VMEM((5,) + sums.shape, f32), pltpu.VMEM((5,) + sums.shape, f32),
                        pltpu.SemaphoreType.DMA((N_SCATTER,)), pltpu.SemaphoreType.DMA((N_SCATTER,)), pltpu.SemaphoreType.DMA((9,))],
        compiler_params=pltpu.CompilerParams(collective_id=1, has_side_effects=True),
        name="scatter",
    )(*grads, lo, ig, sums)


def swap_cores(value):
    return lax.ppermute(value, "fsdp", [(i, i ^ 1) for i in range(lax.axis_size("fsdp"))])


def own_rows(part):
    half = part.shape[0] // 2
    return part[:half] + swap_cores(part[half:].astype(jnp.bfloat16)).astype(jnp.float32)


def both_rows(rows_mine):
    return jnp.concatenate([rows_mine, swap_cores(rows_mine)], axis=0)


def dot32(spec, left, right):
    return jnp.einsum(spec, left, right, preferred_element_type=jnp.float32)


def fast_local(
    inputs, out_grad, segment_ids, w_qkv, bias_qv, w_out, w_up, bias_up, w_down, gains, shifts
):
    w = Where()
    bf, f32 = jnp.bfloat16, jnp.float32
    rows, model_width = inputs.shape[2:]
    tokens = 2 * rows
    score_scale = HD ** (-0.5)
    halves = [a.reshape(128, 2, -1) for a in (w_qkv, w_out, w_up, w_down)]
    mine = jnp.concatenate(halves, axis=-1).transpose(1, 0, 2)
    norms_in = jnp.concatenate([gains, shifts], axis=1).T
    small = jnp.concatenate(
        [
            jnp.broadcast_to(norms_in, (2, 6, 128)),
            bias_qv.reshape(2, 2, 128),
            bias_up.reshape(2, 4, 128),
            jnp.zeros((2, 4, 128), bf),
        ],
        axis=1,
    )
    ids_other = swap_cores(segment_ids)
    full, small_full, x_all, upstream = run_gather(mine, small, inputs, out_grad)
    full = full.reshape(4, model_width, -1)
    small_full = small_full.reshape(4, 8, 16, 128)
    norm_all = small_full[0, :, :6].transpose(1, 0, 2).reshape(6, model_width).astype(f32)
    gain_rows, shift_rows = norm_all[:2], norm_all[2:]
    qv_bias = small_full[:, 0, 6:8].astype(f32).reshape(4, 1, 2, 2, HD)
    up_bias = small_full[:, 0, 8:12].astype(f32).reshape(4, 1, -1)
    full_qkv, full_out, full_up, full_down = (full[:, :, c0 : c0 + cn] for c0, cn in PIECES)

    ids = jnp.where(w.e == w.c, segment_ids, ids_other).reshape(4, 2, rows)
    ids = lax.dynamic_index_in_dim(ids, w.t, 0, keepdims=False)
    ids = jnp.where(w.e == 0, ids, ids[::-1]).reshape(tokens)
    same_segment = ids[:, None] == ids[None, :]

    x_low = x_all.reshape(tokens, model_width)
    projected = dot32("nk,tkc->tnc", x_low, full_qkv).reshape(4, tokens, 2, 3, HD)
    queries = (projected[:, :, :, 0] + qv_bias[:, :, :, 0]).astype(bf)
    key_rows = projected[:, :, :, 1].astype(bf)
    value_rows = (projected[:, :, :, 2] + qv_bias[:, :, :, 1]).astype(bf)

    def get_scores():
        scores = dot32("tqhe,tkhe->thqk", queries, key_rows) * score_scale
        return jnp.where(same_segment, scores, masked_score)

    scores = get_scores()
    row_max = jnp.max(scores, axis=-1, keepdims=True)
    weights = jnp.exp(scores - row_max)
    row_total = jnp.sum(weights, axis=-1, keepdims=True)
    probabilities = weights / row_total
    p_low = probabilities.astype(bf)
    attended_low = dot32("thqk,tkhe->tqhe", p_low, value_rows).astype(bf).reshape(4, tokens, 128)
    attention_part = dot32("tnc,tkc->nk", attended_low, full_out)
    first_sum = x_all[0].astype(f32) + own_rows(attention_part) + shift_rows[0]
    first_norm, first_back = jax.vjp(norm_rows, first_sum, gain_rows[0], shift_rows[1])
    norm_low = both_rows(first_norm.astype(bf))
    before_act = dot32("nk,tkc->tnc", norm_low, full_up) + up_bias
    activated, gelu_back = jax.vjp(exact_gelu, before_act)
    hidden = activated.astype(bf)
    down_part = dot32("tnc,tkc->nk", hidden, full_down)
    second_sum = first_norm + own_rows(down_part) + shift_rows[2]
    result, second_back = jax.vjp(norm_rows, second_sum, gain_rows[1], shift_rows[3])
    layer_mine = result.astype(bf)
    second_grad, gain_two, shift_three = second_back(upstream.astype(f32))
    shift_two = jnp.sum(second_grad, axis=0)
    second_low = both_rows(second_grad.astype(bf))
    down_step = dot32("nk,tnc->tkc", second_low, hidden)
    hidden_grad = dot32("nk,tkc->tnc", second_low, full_down)
    (act_grad,) = gelu_back(hidden_grad)
    up_bias_grad = jnp.sum(act_grad, axis=1)
    act_low = act_grad.astype(bf)
    up_step = dot32("nk,tnc->tkc", norm_low, act_low)
    back_part = dot32("tnc,tkc->nk", act_low, full_up)
    norm_grad = second_grad + own_rows(back_part)
    first_grad, gain_one, shift_one = first_back(norm_grad)
    shift_zero = jnp.sum(first_grad, axis=0)
    first_low = both_rows(first_grad.astype(bf))
    out_step = dot32("nk,tnc->tkc", first_low, attended_low)
    attended_grad = dot32("nk,tkc->tnc", first_low, full_out).astype(bf).reshape(4, tokens, 2, HD)
    value_grad = dot32("thqk,tqhe->tkhe", p_low, attended_grad)
    prob_grad = dot32("tqhe,tkhe->thqk", attended_grad, value_rows)
    row_dot = jnp.sum(prob_grad * probabilities, axis=-1, keepdims=True)
    score_grad = (probabilities * (prob_grad - row_dot)).astype(bf)
    query_grad = dot32("thqk,tkhe->tqhe", score_grad, key_rows) * score_scale
    key_grad = dot32("thqk,tqhe->tkhe", score_grad, queries) * score_scale
    qv_grad = jnp.stack([jnp.sum(query_grad, axis=1), jnp.sum(value_grad, axis=1)], axis=2)
    mixed_grad = jnp.stack([query_grad, key_grad, value_grad], axis=3).astype(bf)
    mixed_grad = mixed_grad.reshape(4, tokens, 6 * HD)
    qkv_step = dot32("nk,tnc->tkc", x_low, mixed_grad)
    input_part = dot32("tnc,tkc->nk", mixed_grad, full_qkv)
    input_mine = (first_grad + own_rows(input_part)).astype(bf)

    norm_sums = jnp.stack([gain_one, gain_two, shift_zero, shift_one, shift_two, shift_three])
    head_sums = jnp.concatenate([qv_grad.reshape(4, 256), up_bias_grad.reshape(4, 512)], axis=1)
    head_sums = jnp.stack([jnp.where(w.e == i, head_sums, 0.0) for i in range(2)])
    sums = jnp.concatenate([norm_sums.reshape(48, 128), head_sums.reshape(48, 128)])
    steps = [a.astype(bf) for a in (qkv_step, out_step, up_step, down_step)]
    g_qkv, g_out, g_up, g_down, layer_out, input_out, sums = run_scatter(
        steps, layer_mine, input_mine, sums
    )
    head_sums = sums[48:].reshape(2, 4, 768)
    head_mine = lax.dynamic_index_in_dim(head_sums, w.t, 1, keepdims=False)
    block = (2 * w.y + w.e) * 2 + w.c
    norm_mine = lax.dynamic_index_in_dim(sums[:48].reshape(6, 8, 128), block, 1, keepdims=False)
    return (
        layer_out,
        input_out.astype(f32),
        g_qkv,
        head_mine[:, :256].reshape(-1),
        g_out,
        g_up,
        head_mine[:, 256:].reshape(-1),
        g_down,
        norm_mine[:2].T,
        norm_mine[2:].T,
    )


def fits_fast(mesh):
    return dict(mesh.shape) == {"fsdp": 4, "ctx": 2, "tp": 4}


def solution(mesh):
    placed = (
        P(None, "fsdp", "ctx", None),
        P(None, "fsdp", "ctx", None),
        P(None, "fsdp", None),
        P(("fsdp", "ctx"), "tp"),
        P("tp"),
        P(("fsdp", "ctx"), "tp"),
        P(("fsdp", "ctx"), "tp"),
        P("tp"),
        P(("fsdp", "ctx"), "tp"),
        P(("fsdp", "ctx"), None),
        P(("fsdp", "ctx"), None),
    )
    return jax.shard_map(
        fast_local if fits_fast(mesh) else local,
        mesh=mesh,
        in_specs=placed,
        out_specs=(
            P(None, "fsdp", ("ctx", "tp"), None),
            P(None, "fsdp", ("ctx", "tp"), None),
            P(("fsdp", "ctx"), "tp"),
            P("tp"),
            P(("fsdp", "ctx"), "tp"),
            P(("fsdp", "ctx"), "tp"),
            P("tp"),
            P(("fsdp", "ctx"), "tp"),
            P(("fsdp", "ctx"), None),
            P(("fsdp", "ctx"), None),
        ),
        check_vma=False,
    )
```

```python
import jax
import jax.numpy as jnp
from jax import lax
from jax.experimental import pallas as pl
from jax.experimental.pallas import tpu as pltpu
from jax.sharding import PartitionSpec as P

HD = 64


norm_epsilon = 1e-12
masked_score = -1e30


def norm_rows(rows_in, gain_row, offset):
    average = jnp.mean(rows_in, axis=-1, keepdims=True)
    centered = rows_in - average
    spread = jnp.mean(centered * centered, axis=-1, keepdims=True)
    return centered * lax.rsqrt(spread + norm_epsilon) * gain_row + offset


def exact_gelu(rows_in):
    return jax.nn.gelu(rows_in, approximate=False)


def contract_rows(left_rows, right_rows):
    return lax.dot_general(
        left_rows, right_rows, (((0,), (0,)), ((), ())), preferred_element_type=jnp.float32
    )


def times_transposed(left_rows, right_rows):
    return lax.dot_general(
        left_rows, right_rows, (((1,), (1,)), ((), ())), preferred_element_type=jnp.float32
    )


def masked_scores(queries, key_rows, same_segment, score_scale):
    scores = (
        jnp.einsum("sqhe,skhe->shqk", queries, key_rows, preferred_element_type=jnp.float32)
        * score_scale
    )
    return jnp.where(same_segment[:, None], scores, masked_score)


def add_pair(running, update):
    return running + update


def reduce_rows(part):
    return lax.psum(part, "tp")


def local(
    inputs, out_grad, segment_ids, w_qkv, bias_qv, w_out, w_up, bias_up, w_down, gains, shifts
):
    batches, seq_local, rows_local, model_width = inputs.shape
    tokens = seq_local * rows_local
    heads_local = w_out.shape[1] // HD
    score_scale = HD ** (-0.5)
    row_share = rows_local // lax.axis_size("tp")
    row_start = lax.axis_index("tp") * row_share
    query_start = lax.axis_index("ctx") * rows_local
    qv_bias = bias_qv.astype(jnp.float32).reshape(heads_local, 2, HD)
    up_bias = bias_up.astype(jnp.float32)

    def pick_rows(values):
        shaped = values.reshape(seq_local, rows_local, model_width)
        return lax.dynamic_slice_in_dim(shaped, row_start, row_share, 1)

    full_totals = (
        jnp.zeros((model_width, w_qkv.shape[1]), jnp.float32),
        jnp.zeros((model_width, w_out.shape[1]), jnp.float32),
        jnp.zeros((model_width, w_up.shape[1]), jnp.float32),
        jnp.zeros((model_width, w_down.shape[1]), jnp.float32),
        jnp.zeros((model_width, 2), jnp.float32),
        jnp.zeros((model_width, 4), jnp.float32),
    )
    share_totals = (
        jnp.zeros(w_qkv.shape, jnp.float32),
        jnp.zeros(w_out.shape, jnp.float32),
        jnp.zeros(w_up.shape, jnp.float32),
        jnp.zeros(w_down.shape, jnp.float32),
        jnp.zeros(gains.shape, jnp.float32),
        jnp.zeros(shifts.shape, jnp.float32),
    )
    qv_bias_grad = jnp.zeros(bias_qv.shape, jnp.float32)
    up_bias_grad = jnp.zeros(bias_up.shape, jnp.float32)
    layer_rows = []
    input_rows = []
    for batch_index in range(batches):
        gathered = (
            lax.all_gather(w_qkv, ("fsdp", "ctx"), axis=0, tiled=True),
            lax.all_gather(w_out, ("fsdp", "ctx"), axis=0, tiled=True),
            lax.all_gather(w_up, ("fsdp", "ctx"), axis=0, tiled=True),
            lax.all_gather(w_down, ("fsdp", "ctx"), axis=0, tiled=True),
            lax.all_gather(gains, ("fsdp", "ctx"), axis=0, tiled=True),
            lax.all_gather(shifts, ("fsdp", "ctx"), axis=0, tiled=True),
        )
        full_qkv, full_out, full_up, full_down, full_gains, full_shifts = gathered
        gain_rows = full_gains.astype(jnp.float32)
        shift_rows = full_shifts.astype(jnp.float32)
        x_low = inputs[batch_index].reshape(tokens, model_width)
        x_full = x_low.astype(jnp.float32)
        projected = jnp.dot(x_low, full_qkv, preferred_element_type=jnp.float32)
        projected = projected.reshape(seq_local, rows_local, heads_local, 3, HD)
        queries = (projected[:, :, :, 0] + qv_bias[:, 0]).astype(jnp.bfloat16)
        key_local = projected[:, :, :, 1].astype(jnp.bfloat16)
        value_local = (projected[:, :, :, 2] + qv_bias[:, 1]).astype(jnp.bfloat16)
        joined = jnp.concatenate([key_local, value_local], axis=-1)
        joined_all = lax.all_gather(joined, "ctx", axis=1, tiled=True)
        key_rows = joined_all[..., :HD]
        value_rows = joined_all[..., HD:]
        segments = segment_ids[batch_index]
        query_segments = lax.dynamic_slice_in_dim(segments, query_start, rows_local, 1)
        same_segment = query_segments[:, :, None] == segments[:, None, :]
        scores = masked_scores(queries, key_rows, same_segment, score_scale)
        row_max = jnp.max(scores, axis=-1, keepdims=True)
        weights = jnp.exp(scores - row_max)
        row_total = jnp.sum(weights, axis=-1, keepdims=True)
        log_total = row_max + jnp.log(row_total)
        p_low = (weights / row_total).astype(jnp.bfloat16)
        attended = jnp.einsum(
            "shqk,skhe->sqhe", p_low, value_rows, preferred_element_type=jnp.float32
        )
        attended_low = attended.reshape(tokens, heads_local * HD).astype(jnp.bfloat16)
        attention_part = times_transposed(attended_low, full_out)
        upstream_full = out_grad[batch_index].reshape(tokens, model_width).astype(jnp.float32)
        attention_total = reduce_rows(attention_part)
        first_sum = x_full + attention_total + shift_rows[:, 0]
        first_norm, first_back = jax.vjp(norm_rows, first_sum, gain_rows[:, 0], shift_rows[:, 1])
        norm_low = first_norm.astype(jnp.bfloat16)
        before_act = jnp.dot(norm_low, full_up, preferred_element_type=jnp.float32) + up_bias
        activated, gelu_back = jax.vjp(exact_gelu, before_act)
        hidden = activated.astype(jnp.bfloat16)
        down_part = times_transposed(hidden, full_down)
        down_total = reduce_rows(down_part)
        second_sum = first_norm + down_total + shift_rows[:, 2]
        result, second_back = jax.vjp(norm_rows, second_sum, gain_rows[:, 1], shift_rows[:, 3])
        layer_rows.append(pick_rows(result).astype(jnp.bfloat16))
        second_grad, gain_two, shift_three = second_back(upstream_full)
        shift_two = jnp.sum(second_grad, axis=0)
        second_low = second_grad.astype(jnp.bfloat16)
        down_step = contract_rows(second_low, hidden)
        hidden_grad = jnp.dot(second_low, full_down, preferred_element_type=jnp.float32)
        (act_grad,) = gelu_back(hidden_grad)
        up_bias_grad = up_bias_grad + jnp.sum(act_grad, axis=0)
        act_low = act_grad.astype(jnp.bfloat16)
        up_step = contract_rows(norm_low, act_low)
        back_part = times_transposed(act_low, full_up)
        back_total = reduce_rows(back_part)
        norm_grad = second_grad + back_total
        first_grad, gain_one, shift_one = first_back(norm_grad)
        shift_zero = jnp.sum(first_grad, axis=0)
        first_low = first_grad.astype(jnp.bfloat16)
        out_step = contract_rows(first_low, attended_low)
        attended_grad = jnp.dot(first_low, full_out, preferred_element_type=jnp.float32)
        attended_grad = attended_grad.astype(jnp.bfloat16).reshape(
            seq_local, rows_local, heads_local, HD
        )
        scores = masked_scores(queries, key_rows, same_segment, score_scale)
        probabilities = jnp.exp(scores - log_total)
        value_grad = jnp.einsum(
            "shqk,sqhe->skhe",
            probabilities.astype(jnp.bfloat16),
            attended_grad,
            preferred_element_type=jnp.float32,
        )
        prob_grad = jnp.einsum(
            "sqhe,skhe->shqk", attended_grad, value_rows, preferred_element_type=jnp.float32
        )
        row_dot = jnp.sum(prob_grad * probabilities, axis=-1, keepdims=True)
        score_grad = (probabilities * (prob_grad - row_dot)).astype(jnp.bfloat16)
        query_grad = (
            jnp.einsum("shqk,skhe->sqhe", score_grad, key_rows, preferred_element_type=jnp.float32)
            * score_scale
        )
        key_grad = (
            jnp.einsum("shqk,sqhe->skhe", score_grad, queries, preferred_element_type=jnp.float32)
            * score_scale
        )
        kv_grads = lax.psum_scatter(
            jnp.concatenate([key_grad, value_grad], axis=-1).astype(jnp.bfloat16),
            "ctx",
            scatter_dimension=1,
            tiled=True,
        ).astype(jnp.float32)
        key_mine = kv_grads[..., :HD]
        value_mine = kv_grads[..., HD:]
        bias_step = jnp.stack(
            [jnp.sum(query_grad, axis=(0, 1)), jnp.sum(value_mine, axis=(0, 1))], axis=1
        )
        qv_bias_grad = qv_bias_grad + bias_step.reshape(-1)
        mixed_grad = jnp.stack([query_grad, key_mine, value_mine], axis=3)
        mixed_grad = mixed_grad.reshape(tokens, 3 * heads_local * HD).astype(jnp.bfloat16)
        qkv_step = contract_rows(x_low, mixed_grad)
        input_part = times_transposed(mixed_grad, full_qkv).reshape(
            seq_local, rows_local, model_width
        )
        input_mine = lax.psum_scatter(
            input_part.astype(jnp.bfloat16), "tp", scatter_dimension=1, tiled=True
        ).astype(jnp.float32)
        first_part = pick_rows(first_grad)
        input_rows.append(input_mine + first_part)
        gain_step = jnp.stack([gain_one, gain_two], axis=1)
        shift_step = jnp.stack([shift_zero, shift_one, shift_two, shift_three], axis=1)
        full_totals = tuple(
            map(
                add_pair,
                full_totals,
                (qkv_step, out_step, up_step, down_step, gain_step, shift_step),
            )
        )
    share_totals = (
        lax.psum_scatter(
            full_totals[0].astype(jnp.bfloat16), ("fsdp", "ctx"), scatter_dimension=0, tiled=True
        ).astype(jnp.float32),
        lax.psum_scatter(
            full_totals[1].astype(jnp.bfloat16), ("fsdp", "ctx"), scatter_dimension=0, tiled=True
        ).astype(jnp.float32),
        lax.psum_scatter(
            full_totals[2].astype(jnp.bfloat16), ("fsdp", "ctx"), scatter_dimension=0, tiled=True
        ).astype(jnp.float32),
        lax.psum_scatter(
            full_totals[3].astype(jnp.bfloat16), ("fsdp", "ctx"), scatter_dimension=0, tiled=True
        ).astype(jnp.float32),
        lax.psum_scatter(
            full_totals[4].astype(jnp.bfloat16), ("fsdp", "ctx"), scatter_dimension=0, tiled=True
        ).astype(jnp.float32),
        lax.psum_scatter(
            full_totals[5].astype(jnp.bfloat16), ("fsdp", "ctx"), scatter_dimension=0, tiled=True
        ).astype(jnp.float32),
    )
    qv_total, up_total = lax.psum((qv_bias_grad, up_bias_grad), ("fsdp", "ctx"))
    return (
        jnp.stack(layer_rows, axis=0),
        jnp.stack(input_rows, axis=0),
        share_totals[0],
        qv_total,
        share_totals[1],
        share_totals[2],
        up_total,
        share_totals[3],
        share_totals[4],
        share_totals[5],
    )


MESH = pl.DeviceIdType.MESH
ROW_A, ROW_D, ROW_AD, ROW_B = (0, 48), (48, 48), (0, 96), (96, 32)

class Where:
    def __init__(self):
        fsdp = lax.axis_index("fsdp")
        self.y = fsdp // 2
        self.e = fsdp % 2
        self.c = lax.axis_index("ctx")
        self.t = lax.axis_index("tp")
    def at(self, y=None, e=None, c=None, t=None):
        y = self.y if y is None else y
        e = self.e if e is None else e
        c = self.c if c is None else c
        t = self.t if t is None else t
        return (2 * y + e, c, t)

def when(cond, fn):
    if cond is True:
        fn()
    else:
        pl.when(cond)(fn)

class Net:
    def __init__(self, send_sems, recv_sems):
        self.send_sems, self.recv_sems, self.count, self.pending = send_sems, recv_sems, 0, []
    def pair(self):
        self.count += 1
        return self.count - 1
    def send(self, index, cond, src, dst, device):
        def make():
            return pltpu.make_async_remote_copy(
                src_ref=src(), dst_ref=dst(), send_sem=self.send_sems.at[index],
                recv_sem=self.recv_sems.at[index], device_id=device, device_id_type=MESH)
        when(cond, lambda: make().start())
        self.pending.append((cond, make))
    def recv(self, index, cond, here, device):
        def wait():
            pltpu.make_async_remote_copy(
                src_ref=here(), dst_ref=here(), send_sem=self.send_sems.at[index],
                recv_sem=self.recv_sems.at[index], device_id=device, device_id_type=MESH).wait_recv()
        when(cond, wait)
    def drain(self):
        for cond, make in self.pending:
            when(cond, lambda make=make: make().wait_send())

def slots_of(w):
    t = w.t
    return [("own", t, True), ("l1", t - 1, t >= 1), ("r1", t + 1, t <= 2), ("l2", t - 2, t >= 2),
            ("r2", t + 2, t <= 1), ("l3", t - 3, t >= 3), ("r3", t + 3, t <= 0)]

class Gather:
    STAGES = 7
    def __init__(self, net, w, sources, full, c0, cn, local_sems, routes=(ROW_A, ROW_D, ROW_AD, ROW_B)):
        self.net, self.w, self.sources, self.full, self.local_sems = net, w, sources, full, local_sems
        self.cols = pl.ds(c0, cn)
        self.row_a, self.row_d, self.row_ad, self.row_b = [None if r is None else pl.ds(*r) for r in routes]
        self.slots = slots_of(w)
        self.ids = {}
    def id(self, key):
        if key not in self.ids:
            self.ids[key] = self.net.pair()
        return self.ids[key]
    def blk(self, tt, rows, y=None, c=None):
        w = self.w
        y = w.y if y is None else y
        c = w.c if c is None else c
        return lambda: self.full.at[tt, y, :, c, rows, self.cols]
    def row(self, tt, rows, y=None):
        y = self.w.y if y is None else y
        return lambda: self.full.at[tt, y, :, :, rows, self.cols]
    def colm(self, tt, rows, c=None):
        c = self.w.c if c is None else c
        return lambda: self.full.at[tt, :, :, c, rows, self.cols]
    def plane(self, tt, rows):
        return lambda: self.full.at[tt, :, :, :, rows, self.cols]
    def same(self, key, cond, ref, device):
        self.net.send(self.id(key), cond, ref, ref, device)
    def sib(self):
        w = self.w
        self.own_copies = []
        for n, (src, c0, cn) in enumerate(self.sources):
            dst = lambda c0=c0, cn=cn: self.full.at[w.t, w.y, w.e, w.c, :, pl.ds(c0, cn)]
            self.net.send(self.id(("sib", n)), True, lambda src=src: src(1 - w.e), dst, w.at(e=1 - w.e))
            self.own_copies.append(pltpu.make_async_copy(src(w.e), dst(), self.local_sems[n]))
            self.own_copies[-1].start()
    def sib_done(self):
        w = self.w
        for n, (src, c0, cn) in enumerate(self.sources):
            self.own_copies[n].wait()
            self.net.recv(self.id(("sib", n)), True, lambda c0=c0, cn=cn: self.full.at[w.t, w.y, 1 - w.e, w.c, :, pl.ds(c0, cn)], w.at(e=1 - w.e))
    def zsend(self, tag, slot, ref):
        w = self.w
        k = {"own": 0, "l1": 1, "r1": 1, "l2": 2, "r2": 2}[slot]
        if slot == "own" or slot[0] == "l":
            name, tt, ok = self.slot("own" if k == 0 else f"l{k}")
            self.same((tag, "zr", k), (w.t < 3) if ok is True else jnp.logical_and(ok, w.t < 3), ref(tt), w.at(t=w.t + 1))
        if slot == "own" or slot[0] == "r":
            name, tt, ok = self.slot("own" if k == 0 else f"r{k}")
            self.same((tag, "zl", k), (w.t > 0) if ok is True else jnp.logical_and(ok, w.t > 0), ref(tt), w.at(t=w.t - 1))
    def zrecv(self, tag, slot, ref):
        w = self.w
        k = int(slot[1])
        _, tt, ok = self.slot(slot)
        if slot[0] == "l":
            self.net.recv(self.id((tag, "zr", k - 1)), ok, ref(tt), w.at(t=w.t - 1))
        else:
            self.net.recv(self.id((tag, "zl", k - 1)), ok, ref(tt), w.at(t=w.t + 1))
    def slot(self, name):
        return next(s for s in self.slots if s[0] == name)
    def first_hop(self, name):
        w = self.w
        _, tt, ok = self.slot(name)
        self.same(("ax", name), ok, self.blk(tt, self.row_a), w.at(c=1 - w.c))
        if self.row_d is not None:
            self.same(("dy", name), ok, self.blk(tt, self.row_d), w.at(y=1 - w.y))
    def second_hop(self, name):
        w = self.w
        _, tt, ok = self.slot(name)
        self.net.recv(self.id(("ax", name)), ok, self.blk(tt, self.row_a, c=1 - w.c), w.at(c=1 - w.c))
        self.same(("ay", name), ok, self.row(tt, self.row_a), w.at(y=1 - w.y))
        if self.row_d is not None:
            self.net.recv(self.id(("dy", name)), ok, self.blk(tt, self.row_d, y=1 - w.y), w.at(y=1 - w.y))
            self.same(("dx", name), ok, self.colm(tt, self.row_d), w.at(c=1 - w.c))
    def last(self, name):
        w = self.w
        _, tt, ok = self.slot(name)
        self.net.recv(self.id(("ay", name)), ok, self.row(tt, self.row_a, y=1 - w.y), w.at(y=1 - w.y))
        if self.row_d is not None:
            self.net.recv(self.id(("dx", name)), ok, self.colm(tt, self.row_d, c=1 - w.c), w.at(c=1 - w.c))
    def stage(self, k):
        w = self.w
        ad = lambda tt: self.blk(tt, self.row_ad)
        bz = lambda tt: self.plane(tt, self.row_b)
        b = self.row_b is not None
        if k == 0:
            self.sib()
        elif k == 1:
            self.sib_done()
            self.zsend("ad", "own", ad)
            if b:
                self.same("bx", True, self.blk(w.t, self.row_b), w.at(c=1 - w.c))
            self.first_hop("own")
        elif k == 2:
            if b:
                self.net.recv(self.id("bx"), True, self.blk(w.t, self.row_b, c=1 - w.c), w.at(c=1 - w.c))
                self.same("by", True, self.row(w.t, self.row_b), w.at(y=1 - w.y))
            for s in ("l1", "r1"):
                self.zrecv("ad", s, ad)
                self.zsend("ad", s, ad)
                self.first_hop(s)
            self.second_hop("own")
        elif k == 3:
            if b:
                self.net.recv(self.id("by"), True, self.row(w.t, self.row_b, y=1 - w.y), w.at(y=1 - w.y))
                self.zsend("b", "own", bz)
            for s in ("l2", "r2"):
                self.zrecv("ad", s, ad)
                self.zsend("ad", s, ad)
                self.first_hop(s)
            for s in ("l1", "r1"):
                self.second_hop(s)
        elif k == 4:
            if b:
                for s in ("l1", "r1"):
                    self.zrecv("b", s, bz)
                    self.zsend("b", s, bz)
            for s in ("l3", "r3"):
                self.zrecv("ad", s, ad)
                self.first_hop(s)
            for s in ("l2", "r2"):
                self.second_hop(s)
        elif k == 5:
            if b:
                for s in ("l2", "r2"):
                    self.zrecv("b", s, bz)
                    self.zsend("b", s, bz)
            for s in ("l3", "r3"):
                self.second_hop(s)
        elif k == 6:
            if b:
                for s in ("l3", "r3"):
                    self.zrecv("b", s, bz)
            for name, _, _ in self.slots:
                self.last(name)

def barrier(w, extra=()):
    sem = pltpu.get_barrier_semaphore()
    one = lambda dev: pl.semaphore_signal(sem, inc=1, device_id=dev, device_id_type=MESH)
    one(w.at(e=1 - w.e)); one(w.at(c=1 - w.c)); one(w.at(y=1 - w.y))
    pl.when(w.t > 0)(lambda: one(w.at(t=w.t - 1)))
    pl.when(w.t < 3)(lambda: one(w.at(t=w.t + 1)))
    ends = jnp.where(w.t == 0, 1, 0) + jnp.where(w.t == 3, 1, 0)
    return sem, one, 5 - ends

PIECES = ((0, 384), (384, 128), (512, 512), (1024, 512))


def mm(left, right, dims):
    return lax.dot_general(left, right, (dims, ((), ())), preferred_element_type=jnp.float32)


def gather_kernel(
    w_qkv, w_out, w_up, w_down, small, x_in, g_in, ids_col, ids_row,
    full_out, small_out, x_all, g_own, q_out, k_out, v_out, p_out, att_out, sum_out, norm_all, hid_out, dgelu_out,
    full, small_full, att_s, part, land, send_sems, recv_sems, local_sems,
):
    w = Where()
    sem, one, need = barrier(w)
    cross = w.e != w.c
    diag = w.at(e=1 - w.e, c=1 - w.c)
    sibling = w.at(e=1 - w.e)
    pl.when(cross)(lambda: one(diag))
    pl.semaphore_wait(sem, need + jnp.where(cross, 1, 0))
    net = Net(send_sems, recv_sems)
    bf, f32 = jnp.bfloat16, jnp.float32
    seq = lambda ref: ref.at[w.t // 2, w.t % 2]
    def source(ref, i):
        c0, cn = PIECES[i]
        return (lambda e: ref.at[:, pl.ds(pl.multiple_of(e * cn, 128), cn)]), c0, cn
    lo = lambda n: local_sems.at[n]
    tiny = Gather(net, w, [(lambda e: small.at[e], 0, 128)], small_full, 0, 128, [lo(0)], routes=((0, 16), None, (0, 16), None))
    parts = [
        Gather(net, w, [source(w_qkv, 0), source(w_out, 1)], full, 0, 512, [lo(1), lo(2)]),
        Gather(net, w, [source(w_up, 2)], full, 512, 512, [lo(3)]),
        Gather(net, w, [source(w_down, 3)], full, 1024, 512, [lo(4)]),
    ]
    xi, gi, xs, ps, ns = [net.pair() for _ in range(5)]
    parts[0].stage(0)
    tiny.stage(0)
    for idx, src, dst in ((xi, x_in, x_all.at[0]), (gi, g_in, g_own)):
        net.send(idx, cross, lambda src=src: seq(src), lambda dst=dst: dst, diag)
    local = [pltpu.make_async_copy(seq(x_in), x_all.at[0], lo(5)), pltpu.make_async_copy(seq(g_in), g_own, lo(6))]
    for cp in local:
        pl.when(jnp.logical_not(cross))(lambda cp=cp: cp.start())
    parts[1].stage(0)
    parts[2].stage(0)
    parts[0].stage(1)
    tiny.stage(1)
    pl.when(jnp.logical_not(cross))(lambda: local[0].wait())
    net.recv(xi, cross, lambda: x_all.at[0], diag)
    net.send(xs, True, lambda: x_all.at[0], lambda: x_all.at[1], sibling)

    half = x_all.shape[1]
    tokens = 2 * half
    def norm_row(k):
        rows = small_full[0, :, :, :, pl.ds(k, 1), :].astype(f32).reshape(8, 128)
        return jnp.concatenate([rows[i : i + 1] for i in range(8)], axis=1)
    def bias_row(tt, k, n):
        rows = small_full[tt, 0, 0, 0].astype(f32)
        return jnp.concatenate([rows[k + i : k + i + 1] for i in range(n)], axis=1)
    def weight(tt, i):
        return full[tt, :, :, :, :, pl.ds(*PIECES[i])].reshape(1024, PIECES[i][1])
    def qkv(tt):
        x = x_all[...].reshape(tokens, 1024)
        proj = (mm(x, weight(tt, 0), ((1,), (0,))) + bias_row(tt, 6, 3)).astype(bf)
        for h in range(2):
            for n, ref in enumerate((q_out, k_out, v_out)):
                ref[2 * tt + h] = proj[:, (3 * h + n) * HD : (3 * h + n + 1) * HD]
    def attend(tt):
        def body(n, carry):
            h = 2 * tt + n // 2
            rows = pl.ds(pl.multiple_of((n % 2) * half, half), half)
            scores = mm(q_out[h, rows, :], k_out[h], ((1,), (1,))) * (HD ** -0.5)
            scores = jnp.where(ids_col[rows, :] == ids_row[...], scores, masked_score)
            weights = jnp.exp(scores - jnp.max(scores, axis=1, keepdims=True))
            p_low = (weights / jnp.sum(weights, axis=1, keepdims=True)).astype(bf)
            p_out[h, rows, :] = p_low
            att_s[h, rows, :] = mm(p_low, v_out[h], ((1,), (0,))).astype(bf)
            return carry
        lax.fori_loop(0, 4, body, 0)
        att_out[tt] = jnp.concatenate([att_s[2 * tt], att_s[2 * tt + 1]], axis=1)
    def project():
        for n in (1, 0):
            rows = pl.ds(n * half, half)
            total = sum(mm(att_out[tt, rows, :], weight(tt, 1), ((1,), (1,))) for tt in range(4))
            if n == 1:
                part[...] = total.astype(bf)
                net.send(ps, True, lambda: part, lambda: land, sibling)
            else:
                sum_out[...] = total + x_all[0].astype(f32) + norm_row(2)
    def normalize():
        net.recv(ps, True, lambda: land, sibling)
        total = sum_out[...] + land[...].astype(f32)
        sum_out[...] = total
        norm_all[0] = norm_rows(total, norm_row(0), norm_row(3)).astype(bf)
        net.send(ns, True, lambda: norm_all.at[0], lambda: norm_all.at[1], sibling)
    def expand(tt):
        bias = bias_row(tt, 9, 4)
        def body(n, carry):
            before = mm(norm_all[n], weight(tt, 2), ((1,), (0,))) + bias
            rows = pl.ds(pl.multiple_of(n * half, half), half)
            bell = (1.0 + lax.erf(before * (2.0 ** -0.5))) * 0.5
            hid_out[tt, rows, :] = (before * bell).astype(bf)
            slope = bell + before * jnp.exp(before * before * -0.5) * (0.3989422804014327)
            dgelu_out[tt, rows, :] = slope.astype(bf)
            return carry
        lax.fori_loop(0, 2, body, 0)
    def keep(i):
        cols = pl.ds(512 * i, 512)
        cp = pltpu.make_async_copy(full.at[..., cols], full_out.at[..., cols], lo(7 + i))
        cp.start()
        return cp
    kept = []
    for s in range(2, 11):
        if s == 10:
            expand(2)
            expand(3)
        for g, start in ((parts[0], 0), (tiny, 0), (parts[1], 2), (parts[2], 4)):
            if 1 <= s - start <= 6:
                g.stage(s - start)
        if s == 6:
            net.recv(xs, True, lambda: x_all.at[1], sibling)
            for tt in range(4):
                qkv(tt)
            attend(0)
        elif s == 7:
            kept.append(keep(0))
            attend(1)
            attend(2)
        elif s == 8:
            attend(3)
            project()
        elif s == 9:
            kept.append(keep(1))
            normalize()
            net.recv(ns, True, lambda: norm_all.at[1], sibling)
            expand(0)
            expand(1)
    kept.append(keep(2))
    small_out[...] = small_full[...]
    pl.when(jnp.logical_not(cross))(lambda: local[1].wait())
    net.recv(gi, cross, lambda: g_own, diag)
    for cp in kept:
        cp.wait()
    net.drain()

N_GATHER = 156

def run_gather(w_qkv, w_out, w_up, w_down, small, x_in, g_in, ids):
    any_ = pl.BlockSpec(memory_space=pl.ANY)
    vm = pl.BlockSpec(memory_space=pltpu.VMEM)
    rows, width = x_in.shape[2:]
    n = 2 * rows
    bf, f32 = jnp.bfloat16, jnp.float32
    sd = jax.ShapeDtypeStruct
    head = sd((8, n, HD), bf)
    return pl.pallas_call(
        gather_kernel,
        out_shape=(
            sd((4, 2, 2, 2, 128, 1536), bf), sd((4, 2, 2, 2, 16, 128), bf), sd((2, rows, width), bf), sd((rows, width), bf),
            head, head, head, sd((8, n, n), bf), sd((4, n, 128), bf), sd((rows, width), f32), sd((2, rows, width), bf),
            sd((4, n, 512), bf), sd((4, n, 512), bf),
        ),
        in_specs=[any_] * 4 + [vm] + [any_] * 2 + [vm] * 2,
        out_specs=(any_, vm, vm, any_) + (vm,) * 9,
        scratch_shapes=[
            pltpu.VMEM((4, 2, 2, 2, 128, 1536), bf), pltpu.VMEM((4, 2, 2, 2, 16, 128), bf),
            pltpu.VMEM((8, n, HD), bf), pltpu.VMEM((rows, width), bf), pltpu.VMEM((rows, width), bf),
            pltpu.SemaphoreType.DMA((N_GATHER,)), pltpu.SemaphoreType.DMA((N_GATHER,)), pltpu.SemaphoreType.DMA((10,)),
        ],
        compiler_params=pltpu.CompilerParams(collective_id=0, has_side_effects=True),
        name="gather",
    )(w_qkv, w_out, w_up, w_down, small, x_in, g_in, ids[:, None], ids[None, :])


ROWS = {"a": pl.ds(0, 48), "d": pl.ds(48, 48), "ad": pl.ds(0, 96), "b": pl.ds(96, 32)}

class Scatter:
    def __init__(self, net, w, g, bufs, c0, cn):
        self.net, self.w, self.g, self.bufs = net, w, g, bufs
        self.cols = pl.ds(c0, cn)
        self.ids = {}
    def id(self, key):
        if key not in self.ids:
            self.ids[key] = self.net.pair()
        return self.ids[key]
    def take(self, key, cond, buf, place, device):
        cols = self.cols
        def body():
            self.net.recv(self.id(key), True, lambda: buf(), device)
            ref = place()
            ref[...] = (ref[...].astype(jnp.float32) + buf()[...].astype(jnp.float32)).astype(ref.dtype)
        when(cond, body)
    def zstep(self, tag, m, place):
        w = self.w
        for way, me, targets in (("r", m, [j for j in (3, 2, 1) if j >= m]), ("l", 3 - m, [j for j in (0, 1, 2) if j <= 3 - m])):
            buf = self.bufs[tag + "z" + way]
            nxt = w.at(t=w.t + 1) if way == "r" else w.at(t=w.t - 1)
            prv = w.at(t=w.t - 1) if way == "r" else w.at(t=w.t + 1)
            here = w.t == me
            for j in targets:
                land = lambda j=j, buf=buf: buf.at[j, ..., self.cols]
                if m > 0:
                    self.take((tag, way, j), here, land, place(j), prv)
                if j != me:
                    self.net.send(self.id((tag, way, j)), here, place(j), land, nxt)
    def stage(self, k):
        w, g, cols, b = self.w, self.g, self.cols, self.bufs
        X, Y = w.at(c=1 - w.c), w.at(y=1 - w.y)
        ad = lambda j: (lambda: g.at[j, w.y, :, w.c, ROWS["ad"], cols])
        bz = lambda j: (lambda: g.at[j, :, :, :, ROWS["b"], cols])
        order = (3, 0, 2, 1)
        if k == 0:
            self.zstep("b", 0, bz)
            for j in order:
                self.net.send(self.id(("ya", j)), True, lambda j=j: g.at[j, 1 - w.y, :, :, ROWS["a"], cols], lambda j=j: b["ya"].at[j, :, :, :, cols], Y)
                self.net.send(self.id(("xd", j)), True, lambda j=j: g.at[j, :, :, 1 - w.c, ROWS["d"], cols], lambda j=j: b["xd"].at[j, :, :, :, cols], X)
        elif k == 1:
            self.zstep("b", 1, bz)
            for j in order:
                self.take(("ya", j), True, lambda j=j: b["ya"].at[j, :, :, :, cols], lambda j=j: g.at[j, w.y, :, :, ROWS["a"], cols], Y)
                self.net.send(self.id(("xa", j)), True, lambda j=j: g.at[j, w.y, :, 1 - w.c, ROWS["a"], cols], lambda j=j: b["xa"].at[j, :, :, cols], X)
                self.take(("xd", j), True, lambda j=j: b["xd"].at[j, :, :, :, cols], lambda j=j: g.at[j, :, :, w.c, ROWS["d"], cols], X)
                self.net.send(self.id(("yd", j)), True, lambda j=j: g.at[j, 1 - w.y, :, w.c, ROWS["d"], cols], lambda j=j: b["yd"].at[j, :, :, cols], Y)
        elif k == 2:
            self.zstep("b", 2, bz)
            for j in order:
                self.take(("xa", j), True, lambda j=j: b["xa"].at[j, :, :, cols], lambda j=j: g.at[j, w.y, :, w.c, ROWS["a"], cols], X)
                self.take(("yd", j), True, lambda j=j: b["yd"].at[j, :, :, cols], lambda j=j: g.at[j, w.y, :, w.c, ROWS["d"], cols], Y)
            self.zstep("ad", 0, ad)
        elif k == 3:
            self.zstep("b", 3, bz)
            self.net.send(self.id("by"), True, lambda: g.at[w.t, 1 - w.y, :, :, ROWS["b"], cols], lambda: b["by"].at[:, :, :, cols], Y)
            self.zstep("ad", 1, ad)
        elif k == 4:
            self.take("by", True, lambda: b["by"].at[:, :, :, cols], lambda: g.at[w.t, w.y, :, :, ROWS["b"], cols], Y)
            self.net.send(self.id("bx"), True, lambda: g.at[w.t, w.y, :, 1 - w.c, ROWS["b"], cols], lambda: b["bx"].at[:, :, cols], X)
            self.zstep("ad", 2, ad)
        elif k == 5:
            self.zstep("ad", 3, ad)
            self.take("bx", True, lambda: b["bx"].at[:, :, cols], lambda: g.at[w.t, w.y, :, w.c, ROWS["b"], cols], X)
            self.net.send(self.id("sib"), True, lambda: g.at[w.t, w.y, 1 - w.e, w.c, :, cols], lambda: b["sib"].at[:, cols], w.at(e=1 - w.e))
        elif k == 6:
            self.net.recv(self.id("sib"), True, lambda: b["sib"].at[:, cols], w.at(e=1 - w.e))


def scatter_kernel(g_qkv, g_out, g_up, g_down, lo, ig, sums, o_qkv, o_out, o_up, o_down, lo_out, ig_out, sums_out, g, ya, xa, xd, yd, adzr, adzl, bzr, bzl, by, bx, sib, sums_run, sums_land, send_sems, recv_sems, local_sems):
    w = Where()
    sem, one, need = barrier(w)
    same = w.e == w.c
    for d in range(4):
        go = (lambda d=d: one(w.at(e=w.c, c=w.e, t=(w.t + d) % 4)))
        when(True if d else jnp.logical_not(same), go)
    one(w.at(t=(w.t + 2) % 4))
    pl.semaphore_wait(sem, need + 4 + jnp.where(same, 0, 1))
    net = Net(send_sems, recv_sems)
    bufs = {"ya": ya, "xa": xa, "xd": xd, "yd": yd, "adzr": adzr, "adzl": adzl, "bzr": bzr, "bzl": bzl, "by": by, "bx": bx, "sib": sib}
    ranges = (1024, 512, 0)
    copies = [[pltpu.make_async_copy(src, g.at[..., pl.ds(*PIECES[i])], local_sems.at[5 + i])] for src, i in ((g_down, 3), (g_up, 2), (g_qkv, 0))]
    copies[2].append(pltpu.make_async_copy(g_out, g.at[..., pl.ds(*PIECES[1])], local_sems.at[6]))
    for cp in sum(copies, []):
        cp.start()
    parts = [Scatter(net, w, g, bufs, c0, 512) for c0 in ranges]
    ids = [[net.pair(), net.pair()] for _ in range(4)]
    def rows_out(k, src, dst, local):
        for d in range(4):
            t2 = (w.t + d) % 4
            here = lambda t2=t2: src.at[pl.ds(pl.multiple_of(t2 * 64, 64), 64)]
            there = lambda: dst.at[w.t // 2, w.t % 2]
            net.send(ids[d][k], True if d else jnp.logical_not(same), here, there, w.at(e=w.c, c=w.e, t=t2))
        cp = pltpu.make_async_copy(src.at[pl.ds(pl.multiple_of(w.t * 64, 64), 64)], dst.at[w.t // 2, w.t % 2], local)
        pl.when(same)(lambda: cp.start())
        return cp
    def rows_in(k, dst):
        for d in range(4):
            t2 = (w.t + 4 - d) % 4
            net.recv(ids[d][k], True if d else jnp.logical_not(same), lambda t2=t2: dst.at[t2 // 2, t2 % 2], w.at(e=w.c, c=w.e, t=t2))
    partners = (w.at(e=1 - w.e), w.at(c=1 - w.c), w.at(y=1 - w.y), w.at(t=w.t + 1 - 2 * (w.t % 2)), w.at(t=(w.t + 2) % 4))
    sums_ids = [net.pair() for _ in partners]
    def sums_step(s):
        if s == 0:
            sums_run[0] = sums[...]
        else:
            net.recv(sums_ids[s - 1], True, lambda: sums_land.at[s - 1], partners[s - 1])
            total = sums_run[s - 1] + sums_land[s - 1]
            if s == 5:
                sums_out[...] = total
            else:
                sums_run[s] = total
        if s < 5:
            net.send(sums_ids[s], True, lambda: sums_run.at[s], lambda: sums_land.at[s], partners[s])
    own = []
    def finish(p):
        for (c0, cn), ref in zip(PIECES, (o_qkv, o_out, o_up, o_down)):
            if ranges[p] <= c0 < ranges[p] + 512:
                cols = pl.ds(c0, cn)
                ref[:, pl.ds(pl.multiple_of(w.e * cn, 128), cn)] = g[w.t, w.y, w.e, w.c, :, cols].astype(jnp.float32)
                ref[:, pl.ds(pl.multiple_of((1 - w.e) * cn, 128), cn)] = sib[:, cols].astype(jnp.float32)
    for s in range(9):
        for p, start in ((0, 0), (1, 1), (2, 2)):
            k = s - start
            if 0 <= k <= 6:
                if k == 0:
                    for cp in copies[p]:
                        cp.wait()
                parts[p].stage(k)
                if k == 6:
                    finish(p)
        if s <= 5:
            sums_step(s)
        if s == 0:
            own.append(rows_out(0, lo, lo_out, local_sems.at[3]))
        if s == 2:
            own.append(rows_out(1, ig, ig_out, local_sems.at[4]))
    for cp in own:
        pl.when(same)(lambda cp=cp: cp.wait())
    rows_in(0, lo_out)
    rows_in(1, ig_out)
    net.drain()

N_SCATTER = 106

def run_scatter(grads, lo, ig, sums):
    any_ = pl.BlockSpec(memory_space=pl.ANY)
    vm = pl.BlockSpec(memory_space=pltpu.VMEM)
    f32, bf = jnp.float32, jnp.bfloat16
    grads = [a.reshape(4, 2, 2, 2, 128, -1) for a in grads]
    n = sum(a.shape[-1] for a in grads)
    share = lo.shape[0] // 4
    sd = jax.ShapeDtypeStruct
    return pl.pallas_call(
        scatter_kernel,
        out_shape=(sd((128, 768), f32), sd((128, 256), f32), sd((128, 1024), f32), sd((128, 1024), f32),
                   sd((2, 2, share, lo.shape[1]), lo.dtype), sd((2, 2, share, ig.shape[1]), ig.dtype), sd(sums.shape, f32)),
        in_specs=[any_] * 4 + [vm] * 3,
        out_specs=(vm, vm, vm, vm, any_, any_, vm),
        scratch_shapes=[pltpu.VMEM((4, 2, 2, 2, 128, n), bf),
                        pltpu.VMEM((4, 2, 2, 48, n), bf), pltpu.VMEM((4, 2, 48, n), bf),
                        pltpu.VMEM((4, 2, 2, 48, n), bf), pltpu.VMEM((4, 2, 48, n), bf),
                        pltpu.VMEM((4, 2, 96, n), bf), pltpu.VMEM((4, 2, 96, n), bf),
                        pltpu.VMEM((4, 2, 2, 2, 32, n), bf), pltpu.VMEM((4, 2, 2, 2, 32, n), bf),
                        pltpu.VMEM((2, 2, 32, n), bf), pltpu.VMEM((2, 32, n), bf), pltpu.VMEM((128, n), bf),
                        pltpu.VMEM((5,) + sums.shape, f32), pltpu.VMEM((5,) + sums.shape, f32),
                        pltpu.SemaphoreType.DMA((N_SCATTER,)), pltpu.SemaphoreType.DMA((N_SCATTER,)), pltpu.SemaphoreType.DMA((9,))],
        compiler_params=pltpu.CompilerParams(collective_id=1, has_side_effects=True),
        name="scatter",
    )(*grads, lo, ig, sums)


def swap_cores(value):
    return lax.ppermute(value, "fsdp", [(i, i ^ 1) for i in range(lax.axis_size("fsdp"))])


def own_rows(part):
    half = part.shape[0] // 2
    return part[:half] + swap_cores(part[half:].astype(jnp.bfloat16)).astype(jnp.float32)


def both_rows(rows_mine):
    return jnp.concatenate([rows_mine, swap_cores(rows_mine)], axis=0)


def dot32(spec, left, right):
    return jnp.einsum(spec, left, right, preferred_element_type=jnp.float32)


def fast_local(
    inputs, out_grad, segment_ids, w_qkv, bias_qv, w_out, w_up, bias_up, w_down, gains, shifts
):
    w = Where()
    bf, f32 = jnp.bfloat16, jnp.float32
    rows, model_width = inputs.shape[2:]
    tokens = 2 * rows
    score_scale = HD ** (-0.5)
    norms_in = jnp.concatenate([gains, shifts], axis=1).T
    qv = bias_qv.reshape(2, 2, 2, HD)
    qkv_bias = jnp.stack([qv[:, :, 0], jnp.zeros_like(qv[:, :, 0]), qv[:, :, 1]], axis=2)
    small = jnp.concatenate(
        [
            jnp.broadcast_to(norms_in, (2, 6, 128)),
            qkv_bias.reshape(2, 3, 128),
            bias_up.reshape(2, 4, 128),
            jnp.zeros((2, 3, 128), bf),
        ],
        axis=1,
    )
    ids = jnp.where(w.e == w.c, segment_ids, swap_cores(segment_ids)).reshape(4, 2, rows)
    ids = lax.dynamic_index_in_dim(ids, w.t, 0, keepdims=False)
    ids = jnp.where(w.e == 0, ids, ids[::-1]).reshape(tokens)
    (
        full, small_full, x_all, upstream, queries, key_rows, value_rows, p_low, attended_low,
        first_sum, norm_low, hidden, gelu_slope,
    ) = run_gather(w_qkv, w_out, w_up, w_down, small, inputs, out_grad, ids)
    full = full.reshape(4, model_width, -1)
    small_full = small_full.reshape(4, 8, 16, 128)
    norm_all = small_full[0, :, :6].transpose(1, 0, 2).reshape(6, model_width).astype(f32)
    gain_rows, shift_rows = norm_all[:2], norm_all[2:]
    full_qkv, full_out, full_up, full_down = (full[:, :, c0 : c0 + cn] for c0, cn in PIECES)
    x_low = x_all.reshape(tokens, model_width)
    norm_low = norm_low.reshape(tokens, model_width)
    first_norm, first_back = jax.vjp(norm_rows, first_sum, gain_rows[0], shift_rows[1])
    down_part = dot32("tnc,tkc->nk", hidden, full_down)
    second_sum = first_norm + own_rows(down_part) + shift_rows[2]
    result, second_back = jax.vjp(norm_rows, second_sum, gain_rows[1], shift_rows[3])
    layer_mine = result.astype(bf)
    second_grad, gain_two, shift_three = second_back(upstream.astype(f32))
    shift_two = jnp.sum(second_grad, axis=0)
    second_low = both_rows(second_grad.astype(bf))
    down_step = dot32("nk,tnc->tkc", second_low, hidden)
    hidden_grad = dot32("nk,tkc->tnc", second_low, full_down)
    act_grad = hidden_grad * gelu_slope.astype(f32)
    up_bias_grad = jnp.sum(act_grad, axis=1)
    act_low = act_grad.astype(bf)
    up_step = dot32("nk,tnc->tkc", norm_low, act_low)
    back_part = dot32("tnc,tkc->nk", act_low, full_up)
    norm_grad = second_grad + own_rows(back_part)
    first_grad, gain_one, shift_one = first_back(norm_grad)
    shift_zero = jnp.sum(first_grad, axis=0)
    first_low = both_rows(first_grad.astype(bf))
    out_step = dot32("nk,tnc->tkc", first_low, attended_low)
    attended_grad = dot32("nk,tkc->tnc", first_low, full_out).astype(bf).reshape(4, tokens, 2, HD)
    attended_grad = attended_grad.transpose(0, 2, 1, 3).reshape(8, tokens, HD)
    probabilities = p_low.astype(f32)
    value_grad = dot32("hqk,hqe->hke", p_low, attended_grad)
    prob_grad = dot32("hqe,hke->hqk", attended_grad, value_rows)
    row_dot = jnp.sum(prob_grad * probabilities, axis=-1, keepdims=True)
    score_grad = (probabilities * (prob_grad - row_dot)).astype(bf)
    query_grad = dot32("hqk,hke->hqe", score_grad, key_rows) * score_scale
    key_grad = dot32("hqk,hqe->hke", score_grad, queries) * score_scale
    qv_grad = jnp.stack([jnp.sum(query_grad, axis=1), jnp.sum(value_grad, axis=1)], axis=1)
    mixed_grad = jnp.stack([a.astype(bf) for a in (query_grad, key_grad, value_grad)], axis=1)
    mixed_grad = mixed_grad.reshape(4, 6, tokens, HD).transpose(0, 2, 1, 3).reshape(4, tokens, 6 * HD)
    qkv_step = dot32("nk,tnc->tkc", x_low, mixed_grad)
    input_part = dot32("tnc,tkc->nk", mixed_grad, full_qkv)
    input_mine = (first_grad + own_rows(input_part)).astype(bf)

    norm_sums = jnp.stack([gain_one, gain_two, shift_zero, shift_one, shift_two, shift_three])
    head_sums = jnp.concatenate([qv_grad.reshape(4, 256), up_bias_grad.reshape(4, 512)], axis=1)
    head_sums = jnp.stack([jnp.where(w.e == i, head_sums, 0.0) for i in range(2)])
    sums = jnp.concatenate([norm_sums.reshape(48, 128), head_sums.reshape(48, 128)])
    steps = [a.astype(bf) for a in (qkv_step, out_step, up_step, down_step)]
    g_qkv, g_out, g_up, g_down, layer_out, input_out, sums = run_scatter(
        steps, layer_mine, input_mine, sums
    )
    head_sums = sums[48:].reshape(2, 4, 768)
    head_mine = lax.dynamic_index_in_dim(head_sums, w.t, 1, keepdims=False)
    block = (2 * w.y + w.e) * 2 + w.c
    norm_mine = lax.dynamic_index_in_dim(sums[:48].reshape(6, 8, 128), block, 1, keepdims=False)
    return (
        layer_out,
        input_out.astype(f32),
        g_qkv,
        head_mine[:, :256].reshape(-1),
        g_out,
        g_up,
        head_mine[:, 256:].reshape(-1),
        g_down,
        norm_mine[:2].T,
        norm_mine[2:].T,
    )


def fits_fast(mesh):
    return dict(mesh.shape) == {"fsdp": 4, "ctx": 2, "tp": 4}


def solution(mesh):
    placed = (
        P(None, "fsdp", "ctx", None),
        P(None, "fsdp", "ctx", None),
        P(None, "fsdp", None),
        P(("fsdp", "ctx"), "tp"),
        P("tp"),
        P(("fsdp", "ctx"), "tp"),
        P(("fsdp", "ctx"), "tp"),
        P("tp"),
        P(("fsdp", "ctx"), "tp"),
        P(("fsdp", "ctx"), None),
        P(("fsdp", "ctx"), None),
    )
    return jax.shard_map(
        fast_local if fits_fast(mesh) else local,
        mesh=mesh,
        in_specs=placed,
        out_specs=(
            P(None, "fsdp", ("ctx", "tp"), None),
            P(None, "fsdp", ("ctx", "tp"), None),
            P(("fsdp", "ctx"), "tp"),
            P("tp"),
            P(("fsdp", "ctx"), "tp"),
            P(("fsdp", "ctx"), "tp"),
            P("tp"),
            P(("fsdp", "ctx"), "tp"),
            P(("fsdp", "ctx"), None),
            P(("fsdp", "ctx"), None),
        ),
        check_vma=False,
    )
```

```python
import jax
import jax.numpy as jnp
from jax import lax
from jax.experimental import pallas as pl
from jax.experimental.pallas import tpu as pltpu
from jax.sharding import PartitionSpec as P

HD = 64


norm_epsilon = 1e-12
masked_score = -1e30


def norm_rows(rows_in, gain_row, offset):
    average = jnp.mean(rows_in, axis=-1, keepdims=True)
    centered = rows_in - average
    spread = jnp.mean(centered * centered, axis=-1, keepdims=True)
    return centered * lax.rsqrt(spread + norm_epsilon) * gain_row + offset


def exact_gelu(rows_in):
    return jax.nn.gelu(rows_in, approximate=False)


def contract_rows(left_rows, right_rows):
    return lax.dot_general(
        left_rows, right_rows, (((0,), (0,)), ((), ())), preferred_element_type=jnp.float32
    )


def times_transposed(left_rows, right_rows):
    return lax.dot_general(
        left_rows, right_rows, (((1,), (1,)), ((), ())), preferred_element_type=jnp.float32
    )


def masked_scores(queries, key_rows, same_segment, score_scale):
    scores = (
        jnp.einsum("sqhe,skhe->shqk", queries, key_rows, preferred_element_type=jnp.float32)
        * score_scale
    )
    return jnp.where(same_segment[:, None], scores, masked_score)


def add_pair(running, update):
    return running + update


def reduce_rows(part):
    return lax.psum(part, "tp")


def local(
    inputs, out_grad, segment_ids, w_qkv, bias_qv, w_out, w_up, bias_up, w_down, gains, shifts
):
    batches, seq_local, rows_local, model_width = inputs.shape
    tokens = seq_local * rows_local
    heads_local = w_out.shape[1] // HD
    score_scale = HD ** (-0.5)
    row_share = rows_local // lax.axis_size("tp")
    row_start = lax.axis_index("tp") * row_share
    query_start = lax.axis_index("ctx") * rows_local
    qv_bias = bias_qv.astype(jnp.float32).reshape(heads_local, 2, HD)
    up_bias = bias_up.astype(jnp.float32)

    def pick_rows(values):
        shaped = values.reshape(seq_local, rows_local, model_width)
        return lax.dynamic_slice_in_dim(shaped, row_start, row_share, 1)

    full_totals = (
        jnp.zeros((model_width, w_qkv.shape[1]), jnp.float32),
        jnp.zeros((model_width, w_out.shape[1]), jnp.float32),
        jnp.zeros((model_width, w_up.shape[1]), jnp.float32),
        jnp.zeros((model_width, w_down.shape[1]), jnp.float32),
        jnp.zeros((model_width, 2), jnp.float32),
        jnp.zeros((model_width, 4), jnp.float32),
    )
    share_totals = (
        jnp.zeros(w_qkv.shape, jnp.float32),
        jnp.zeros(w_out.shape, jnp.float32),
        jnp.zeros(w_up.shape, jnp.float32),
        jnp.zeros(w_down.shape, jnp.float32),
        jnp.zeros(gains.shape, jnp.float32),
        jnp.zeros(shifts.shape, jnp.float32),
    )
    qv_bias_grad = jnp.zeros(bias_qv.shape, jnp.float32)
    up_bias_grad = jnp.zeros(bias_up.shape, jnp.float32)
    layer_rows = []
    input_rows = []
    for batch_index in range(batches):
        gathered = (
            lax.all_gather(w_qkv, ("fsdp", "ctx"), axis=0, tiled=True),
            lax.all_gather(w_out, ("fsdp", "ctx"), axis=0, tiled=True),
            lax.all_gather(w_up, ("fsdp", "ctx"), axis=0, tiled=True),
            lax.all_gather(w_down, ("fsdp", "ctx"), axis=0, tiled=True),
            lax.all_gather(gains, ("fsdp", "ctx"), axis=0, tiled=True),
            lax.all_gather(shifts, ("fsdp", "ctx"), axis=0, tiled=True),
        )
        full_qkv, full_out, full_up, full_down, full_gains, full_shifts = gathered
        gain_rows = full_gains.astype(jnp.float32)
        shift_rows = full_shifts.astype(jnp.float32)
        x_low = inputs[batch_index].reshape(tokens, model_width)
        x_full = x_low.astype(jnp.float32)
        projected = jnp.dot(x_low, full_qkv, preferred_element_type=jnp.float32)
        projected = projected.reshape(seq_local, rows_local, heads_local, 3, HD)
        queries = (projected[:, :, :, 0] + qv_bias[:, 0]).astype(jnp.bfloat16)
        key_local = projected[:, :, :, 1].astype(jnp.bfloat16)
        value_local = (projected[:, :, :, 2] + qv_bias[:, 1]).astype(jnp.bfloat16)
        joined = jnp.concatenate([key_local, value_local], axis=-1)
        joined_all = lax.all_gather(joined, "ctx", axis=1, tiled=True)
        key_rows = joined_all[..., :HD]
        value_rows = joined_all[..., HD:]
        segments = segment_ids[batch_index]
        query_segments = lax.dynamic_slice_in_dim(segments, query_start, rows_local, 1)
        same_segment = query_segments[:, :, None] == segments[:, None, :]
        scores = masked_scores(queries, key_rows, same_segment, score_scale)
        row_max = jnp.max(scores, axis=-1, keepdims=True)
        weights = jnp.exp(scores - row_max)
        row_total = jnp.sum(weights, axis=-1, keepdims=True)
        log_total = row_max + jnp.log(row_total)
        p_low = (weights / row_total).astype(jnp.bfloat16)
        attended = jnp.einsum(
            "shqk,skhe->sqhe", p_low, value_rows, preferred_element_type=jnp.float32
        )
        attended_low = attended.reshape(tokens, heads_local * HD).astype(jnp.bfloat16)
        attention_part = times_transposed(attended_low, full_out)
        upstream_full = out_grad[batch_index].reshape(tokens, model_width).astype(jnp.float32)
        attention_total = reduce_rows(attention_part)
        first_sum = x_full + attention_total + shift_rows[:, 0]
        first_norm, first_back = jax.vjp(norm_rows, first_sum, gain_rows[:, 0], shift_rows[:, 1])
        norm_low = first_norm.astype(jnp.bfloat16)
        before_act = jnp.dot(norm_low, full_up, preferred_element_type=jnp.float32) + up_bias
        activated, gelu_back = jax.vjp(exact_gelu, before_act)
        hidden = activated.astype(jnp.bfloat16)
        down_part = times_transposed(hidden, full_down)
        down_total = reduce_rows(down_part)
        second_sum = first_norm + down_total + shift_rows[:, 2]
        result, second_back = jax.vjp(norm_rows, second_sum, gain_rows[:, 1], shift_rows[:, 3])
        layer_rows.append(pick_rows(result).astype(jnp.bfloat16))
        second_grad, gain_two, shift_three = second_back(upstream_full)
        shift_two = jnp.sum(second_grad, axis=0)
        second_low = second_grad.astype(jnp.bfloat16)
        down_step = contract_rows(second_low, hidden)
        hidden_grad = jnp.dot(second_low, full_down, preferred_element_type=jnp.float32)
        (act_grad,) = gelu_back(hidden_grad)
        up_bias_grad = up_bias_grad + jnp.sum(act_grad, axis=0)
        act_low = act_grad.astype(jnp.bfloat16)
        up_step = contract_rows(norm_low, act_low)
        back_part = times_transposed(act_low, full_up)
        back_total = reduce_rows(back_part)
        norm_grad = second_grad + back_total
        first_grad, gain_one, shift_one = first_back(norm_grad)
        shift_zero = jnp.sum(first_grad, axis=0)
        first_low = first_grad.astype(jnp.bfloat16)
        out_step = contract_rows(first_low, attended_low)
        attended_grad = jnp.dot(first_low, full_out, preferred_element_type=jnp.float32)
        attended_grad = attended_grad.astype(jnp.bfloat16).reshape(
            seq_local, rows_local, heads_local, HD
        )
        scores = masked_scores(queries, key_rows, same_segment, score_scale)
        probabilities = jnp.exp(scores - log_total)
        value_grad = jnp.einsum(
            "shqk,sqhe->skhe",
            probabilities.astype(jnp.bfloat16),
            attended_grad,
            preferred_element_type=jnp.float32,
        )
        prob_grad = jnp.einsum(
            "sqhe,skhe->shqk", attended_grad, value_rows, preferred_element_type=jnp.float32
        )
        row_dot = jnp.sum(prob_grad * probabilities, axis=-1, keepdims=True)
        score_grad = (probabilities * (prob_grad - row_dot)).astype(jnp.bfloat16)
        query_grad = (
            jnp.einsum("shqk,skhe->sqhe", score_grad, key_rows, preferred_element_type=jnp.float32)
            * score_scale
        )
        key_grad = (
            jnp.einsum("shqk,sqhe->skhe", score_grad, queries, preferred_element_type=jnp.float32)
            * score_scale
        )
        kv_grads = lax.psum_scatter(
            jnp.concatenate([key_grad, value_grad], axis=-1).astype(jnp.bfloat16),
            "ctx",
            scatter_dimension=1,
            tiled=True,
        ).astype(jnp.float32)
        key_mine = kv_grads[..., :HD]
        value_mine = kv_grads[..., HD:]
        bias_step = jnp.stack(
            [jnp.sum(query_grad, axis=(0, 1)), jnp.sum(value_mine, axis=(0, 1))], axis=1
        )
        qv_bias_grad = qv_bias_grad + bias_step.reshape(-1)
        mixed_grad = jnp.stack([query_grad, key_mine, value_mine], axis=3)
        mixed_grad = mixed_grad.reshape(tokens, 3 * heads_local * HD).astype(jnp.bfloat16)
        qkv_step = contract_rows(x_low, mixed_grad)
        input_part = times_transposed(mixed_grad, full_qkv).reshape(
            seq_local, rows_local, model_width
        )
        input_mine = lax.psum_scatter(
            input_part.astype(jnp.bfloat16), "tp", scatter_dimension=1, tiled=True
        ).astype(jnp.float32)
        first_part = pick_rows(first_grad)
        input_rows.append(input_mine + first_part)
        gain_step = jnp.stack([gain_one, gain_two], axis=1)
        shift_step = jnp.stack([shift_zero, shift_one, shift_two, shift_three], axis=1)
        full_totals = tuple(
            map(
                add_pair,
                full_totals,
                (qkv_step, out_step, up_step, down_step, gain_step, shift_step),
            )
        )
    share_totals = (
        lax.psum_scatter(
            full_totals[0].astype(jnp.bfloat16), ("fsdp", "ctx"), scatter_dimension=0, tiled=True
        ).astype(jnp.float32),
        lax.psum_scatter(
            full_totals[1].astype(jnp.bfloat16), ("fsdp", "ctx"), scatter_dimension=0, tiled=True
        ).astype(jnp.float32),
        lax.psum_scatter(
            full_totals[2].astype(jnp.bfloat16), ("fsdp", "ctx"), scatter_dimension=0, tiled=True
        ).astype(jnp.float32),
        lax.psum_scatter(
            full_totals[3].astype(jnp.bfloat16), ("fsdp", "ctx"), scatter_dimension=0, tiled=True
        ).astype(jnp.float32),
        lax.psum_scatter(
            full_totals[4].astype(jnp.bfloat16), ("fsdp", "ctx"), scatter_dimension=0, tiled=True
        ).astype(jnp.float32),
        lax.psum_scatter(
            full_totals[5].astype(jnp.bfloat16), ("fsdp", "ctx"), scatter_dimension=0, tiled=True
        ).astype(jnp.float32),
    )
    qv_total, up_total = lax.psum((qv_bias_grad, up_bias_grad), ("fsdp", "ctx"))
    return (
        jnp.stack(layer_rows, axis=0),
        jnp.stack(input_rows, axis=0),
        share_totals[0],
        qv_total,
        share_totals[1],
        share_totals[2],
        up_total,
        share_totals[3],
        share_totals[4],
        share_totals[5],
    )


MESH = pl.DeviceIdType.MESH
ROW_A, ROW_D, ROW_AD, ROW_B = (0, 48), (48, 48), (0, 96), (96, 32)

class Where:
    def __init__(self):
        fsdp = lax.axis_index("fsdp")
        self.y = fsdp // 2
        self.e = fsdp % 2
        self.c = lax.axis_index("ctx")
        self.t = lax.axis_index("tp")
    def at(self, y=None, e=None, c=None, t=None):
        y = self.y if y is None else y
        e = self.e if e is None else e
        c = self.c if c is None else c
        t = self.t if t is None else t
        return (2 * y + e, c, t)

def when(cond, fn):
    if cond is True:
        fn()
    else:
        pl.when(cond)(fn)

class Net:
    def __init__(self, send_sems, recv_sems):
        self.send_sems, self.recv_sems, self.count, self.pending = send_sems, recv_sems, 0, []
    def pair(self):
        self.count += 1
        return self.count - 1
    def send(self, index, cond, src, dst, device):
        def make():
            return pltpu.make_async_remote_copy(
                src_ref=src(), dst_ref=dst(), send_sem=self.send_sems.at[index],
                recv_sem=self.recv_sems.at[index], device_id=device, device_id_type=MESH)
        when(cond, lambda: make().start())
        self.pending.append((cond, make))
    def recv(self, index, cond, here, device):
        def wait():
            pltpu.make_async_remote_copy(
                src_ref=here(), dst_ref=here(), send_sem=self.send_sems.at[index],
                recv_sem=self.recv_sems.at[index], device_id=device, device_id_type=MESH).wait_recv()
        when(cond, wait)
    def drain(self):
        for cond, make in self.pending:
            when(cond, lambda make=make: make().wait_send())

def slots_of(w):
    t = w.t
    return [("own", t, True), ("l1", t - 1, t >= 1), ("r1", t + 1, t <= 2), ("l2", t - 2, t >= 2),
            ("r2", t + 2, t <= 1), ("l3", t - 3, t >= 3), ("r3", t + 3, t <= 0)]

class Gather:
    STAGES = 7
    def __init__(self, net, w, sources, full, c0, cn, local_sems, routes=(ROW_A, ROW_D, ROW_AD, ROW_B)):
        self.net, self.w, self.sources, self.full, self.local_sems = net, w, sources, full, local_sems
        self.cols = pl.ds(c0, cn)
        self.row_a, self.row_d, self.row_ad, self.row_b = [None if r is None else pl.ds(*r) for r in routes]
        self.slots = slots_of(w)
        self.ids = {}
    def id(self, key):
        if key not in self.ids:
            self.ids[key] = self.net.pair()
        return self.ids[key]
    def blk(self, tt, rows, y=None, c=None):
        w = self.w
        y = w.y if y is None else y
        c = w.c if c is None else c
        return lambda: self.full.at[tt, y, :, c, rows, self.cols]
    def row(self, tt, rows, y=None):
        y = self.w.y if y is None else y
        return lambda: self.full.at[tt, y, :, :, rows, self.cols]
    def colm(self, tt, rows, c=None):
        c = self.w.c if c is None else c
        return lambda: self.full.at[tt, :, :, c, rows, self.cols]
    def plane(self, tt, rows):
        return lambda: self.full.at[tt, :, :, :, rows, self.cols]
    def same(self, key, cond, ref, device):
        self.net.send(self.id(key), cond, ref, ref, device)
    def sib(self):
        w = self.w
        self.own_copies = []
        for n, (src, c0, cn) in enumerate(self.sources):
            dst = lambda c0=c0, cn=cn: self.full.at[w.t, w.y, w.e, w.c, :, pl.ds(c0, cn)]
            self.net.send(self.id(("sib", n)), True, lambda src=src: src(1 - w.e), dst, w.at(e=1 - w.e))
            self.own_copies.append(pltpu.make_async_copy(src(w.e), dst(), self.local_sems[n]))
            self.own_copies[-1].start()
    def sib_done(self):
        w = self.w
        for n, (src, c0, cn) in enumerate(self.sources):
            self.own_copies[n].wait()
            self.net.recv(self.id(("sib", n)), True, lambda c0=c0, cn=cn: self.full.at[w.t, w.y, 1 - w.e, w.c, :, pl.ds(c0, cn)], w.at(e=1 - w.e))
    def zsend(self, tag, slot, ref):
        w = self.w
        k = {"own": 0, "l1": 1, "r1": 1, "l2": 2, "r2": 2}[slot]
        if slot == "own" or slot[0] == "l":
            name, tt, ok = self.slot("own" if k == 0 else f"l{k}")
            self.same((tag, "zr", k), (w.t < 3) if ok is True else jnp.logical_and(ok, w.t < 3), ref(tt), w.at(t=w.t + 1))
        if slot == "own" or slot[0] == "r":
            name, tt, ok = self.slot("own" if k == 0 else f"r{k}")
            self.same((tag, "zl", k), (w.t > 0) if ok is True else jnp.logical_and(ok, w.t > 0), ref(tt), w.at(t=w.t - 1))
    def zrecv(self, tag, slot, ref):
        w = self.w
        k = int(slot[1])
        _, tt, ok = self.slot(slot)
        if slot[0] == "l":
            self.net.recv(self.id((tag, "zr", k - 1)), ok, ref(tt), w.at(t=w.t - 1))
        else:
            self.net.recv(self.id((tag, "zl", k - 1)), ok, ref(tt), w.at(t=w.t + 1))
    def slot(self, name):
        return next(s for s in self.slots if s[0] == name)
    def first_hop(self, name):
        w = self.w
        _, tt, ok = self.slot(name)
        self.same(("ax", name), ok, self.blk(tt, self.row_a), w.at(c=1 - w.c))
        if self.row_d is not None:
            self.same(("dy", name), ok, self.blk(tt, self.row_d), w.at(y=1 - w.y))
    def second_hop(self, name):
        w = self.w
        _, tt, ok = self.slot(name)
        self.net.recv(self.id(("ax", name)), ok, self.blk(tt, self.row_a, c=1 - w.c), w.at(c=1 - w.c))
        self.same(("ay", name), ok, self.row(tt, self.row_a), w.at(y=1 - w.y))
        if self.row_d is not None:
            self.net.recv(self.id(("dy", name)), ok, self.blk(tt, self.row_d, y=1 - w.y), w.at(y=1 - w.y))
            self.same(("dx", name), ok, self.colm(tt, self.row_d), w.at(c=1 - w.c))
    def last(self, name):
        w = self.w
        _, tt, ok = self.slot(name)
        self.net.recv(self.id(("ay", name)), ok, self.row(tt, self.row_a, y=1 - w.y), w.at(y=1 - w.y))
        if self.row_d is not None:
            self.net.recv(self.id(("dx", name)), ok, self.colm(tt, self.row_d, c=1 - w.c), w.at(c=1 - w.c))
    def stage(self, k):
        w = self.w
        ad = lambda tt: self.blk(tt, self.row_ad)
        bz = lambda tt: self.plane(tt, self.row_b)
        b = self.row_b is not None
        if k == 0:
            self.sib()
        elif k == 1:
            self.sib_done()
            self.zsend("ad", "own", ad)
            if b:
                self.same("bx", True, self.blk(w.t, self.row_b), w.at(c=1 - w.c))
            self.first_hop("own")
        elif k == 2:
            if b:
                self.net.recv(self.id("bx"), True, self.blk(w.t, self.row_b, c=1 - w.c), w.at(c=1 - w.c))
                self.same("by", True, self.row(w.t, self.row_b), w.at(y=1 - w.y))
            for s in ("l1", "r1"):
                self.zrecv("ad", s, ad)
                self.zsend("ad", s, ad)
                self.first_hop(s)
            self.second_hop("own")
        elif k == 3:
            if b:
                self.net.recv(self.id("by"), True, self.row(w.t, self.row_b, y=1 - w.y), w.at(y=1 - w.y))
                self.zsend("b", "own", bz)
            for s in ("l2", "r2"):
                self.zrecv("ad", s, ad)
                self.zsend("ad", s, ad)
                self.first_hop(s)
            for s in ("l1", "r1"):
                self.second_hop(s)
        elif k == 4:
            if b:
                for s in ("l1", "r1"):
                    self.zrecv("b", s, bz)
                    self.zsend("b", s, bz)
            for s in ("l3", "r3"):
                self.zrecv("ad", s, ad)
                self.first_hop(s)
            for s in ("l2", "r2"):
                self.second_hop(s)
        elif k == 5:
            if b:
                for s in ("l2", "r2"):
                    self.zrecv("b", s, bz)
                    self.zsend("b", s, bz)
            for s in ("l3", "r3"):
                self.second_hop(s)
        elif k == 6:
            if b:
                for s in ("l3", "r3"):
                    self.zrecv("b", s, bz)
            for name, _, _ in self.slots:
                self.last(name)

def barrier(w, extra=()):
    sem = pltpu.get_barrier_semaphore()
    one = lambda dev: pl.semaphore_signal(sem, inc=1, device_id=dev, device_id_type=MESH)
    one(w.at(e=1 - w.e)); one(w.at(c=1 - w.c)); one(w.at(y=1 - w.y))
    pl.when(w.t > 0)(lambda: one(w.at(t=w.t - 1)))
    pl.when(w.t < 3)(lambda: one(w.at(t=w.t + 1)))
    ends = jnp.where(w.t == 0, 1, 0) + jnp.where(w.t == 3, 1, 0)
    return sem, one, 5 - ends

PIECES = ((0, 384), (384, 128), (512, 512), (1024, 512))


def mm(left, right, dims):
    return lax.dot_general(left, right, (dims, ((), ())), preferred_element_type=jnp.float32)


def gather_kernel(
    w_qkv, w_out, w_up, w_down, small, x_in, g_in, ids_col, ids_row,
    full_out, small_out, x_all, g_own, q_out, k_out, v_out, p_out, att_out, sum_out, norm_all, hid_out, dgelu_out,
    full, small_full, att_s, part, land, send_sems, recv_sems, local_sems,
):
    w = Where()
    sem, one, need = barrier(w)
    cross = w.e != w.c
    diag = w.at(e=1 - w.e, c=1 - w.c)
    sibling = w.at(e=1 - w.e)
    pl.when(cross)(lambda: one(diag))
    pl.semaphore_wait(sem, need + jnp.where(cross, 1, 0))
    net = Net(send_sems, recv_sems)
    bf, f32 = jnp.bfloat16, jnp.float32
    seq = lambda ref: ref.at[w.t // 2, w.t % 2]
    def source(ref, i):
        c0, cn = PIECES[i]
        return (lambda e: ref.at[:, pl.ds(pl.multiple_of(e * cn, 128), cn)]), c0, cn
    lo = lambda n: local_sems.at[n]
    tiny = Gather(net, w, [(lambda e: small.at[e], 0, 128)], small_full, 0, 128, [lo(0)], routes=((0, 16), None, (0, 16), None))
    parts = [
        Gather(net, w, [source(w_qkv, 0), source(w_out, 1)], full, 0, 512, [lo(1), lo(2)]),
        Gather(net, w, [source(w_up, 2)], full, 512, 512, [lo(3)]),
        Gather(net, w, [source(w_down, 3)], full, 1024, 512, [lo(4)]),
    ]
    xi, gi, xs, ps, ns = [net.pair() for _ in range(5)]
    parts[0].stage(0)
    tiny.stage(0)
    for idx, src, dst in ((xi, x_in, x_all.at[0]), (gi, g_in, g_own)):
        net.send(idx, cross, lambda src=src: seq(src), lambda dst=dst: dst, diag)
    local = [pltpu.make_async_copy(seq(x_in), x_all.at[0], lo(5)), pltpu.make_async_copy(seq(g_in), g_own, lo(6))]
    for cp in local:
        pl.when(jnp.logical_not(cross))(lambda cp=cp: cp.start())
    parts[1].stage(0)
    parts[2].stage(0)
    parts[0].stage(1)
    tiny.stage(1)
    pl.when(jnp.logical_not(cross))(lambda: local[0].wait())
    net.recv(xi, cross, lambda: x_all.at[0], diag)
    net.send(xs, True, lambda: x_all.at[0], lambda: x_all.at[1], sibling)

    half = x_all.shape[1]
    tokens = 2 * half
    def norm_row(k):
        rows = small_full[0, :, :, :, pl.ds(k, 1), :].astype(f32).reshape(8, 128)
        return jnp.concatenate([rows[i : i + 1] for i in range(8)], axis=1)
    def bias_row(tt, k, n):
        rows = small_full[tt, 0, 0, 0].astype(f32)
        return jnp.concatenate([rows[k + i : k + i + 1] for i in range(n)], axis=1)
    def weight(tt, i):
        return full[tt, :, :, :, :, pl.ds(*PIECES[i])].reshape(1024, PIECES[i][1])
    def qkv(tt):
        x = x_all[...].reshape(tokens, 1024)
        proj = (mm(x, weight(tt, 0), ((1,), (0,))) + bias_row(tt, 6, 3)).astype(bf)
        for h in range(2):
            for n, ref in enumerate((q_out, k_out, v_out)):
                ref[2 * tt + h] = proj[:, (3 * h + n) * HD : (3 * h + n + 1) * HD]
    def attend(tt):
        def body(n, carry):
            h = 2 * tt + n // 2
            rows = pl.ds(pl.multiple_of((n % 2) * half, half), half)
            scores = mm(q_out[h, rows, :], k_out[h], ((1,), (1,))) * (HD ** -0.5)
            scores = jnp.where(ids_col[rows, :] == ids_row[...], scores, masked_score)
            weights = jnp.exp(scores - jnp.max(scores, axis=1, keepdims=True))
            p_low = (weights / jnp.sum(weights, axis=1, keepdims=True)).astype(bf)
            p_out[h, rows, :] = p_low
            att_s[h, rows, :] = mm(p_low, v_out[h], ((1,), (0,))).astype(bf)
            return carry
        lax.fori_loop(0, 4, body, 0)
        att_out[tt] = jnp.concatenate([att_s[2 * tt], att_s[2 * tt + 1]], axis=1)
    def project():
        for n in (1, 0):
            rows = pl.ds(n * half, half)
            total = sum(mm(att_out[tt, rows, :], weight(tt, 1), ((1,), (1,))) for tt in range(4))
            if n == 1:
                part[...] = total.astype(bf)
                net.send(ps, True, lambda: part, lambda: land, sibling)
            else:
                sum_out[...] = total + x_all[0].astype(f32) + norm_row(2)
    def normalize():
        net.recv(ps, True, lambda: land, sibling)
        total = sum_out[...] + land[...].astype(f32)
        sum_out[...] = total
        norm_all[0] = norm_rows(total, norm_row(0), norm_row(3)).astype(bf)
        net.send(ns, True, lambda: norm_all.at[0], lambda: norm_all.at[1], sibling)
    def expand(tt):
        bias = bias_row(tt, 9, 4)
        def body(n, carry):
            before = mm(norm_all[n], weight(tt, 2), ((1,), (0,))) + bias
            rows = pl.ds(pl.multiple_of(n * half, half), half)
            bell = (1.0 + lax.erf(before * (2.0 ** -0.5))) * 0.5
            hid_out[tt, rows, :] = (before * bell).astype(bf)
            slope = bell + before * jnp.exp(before * before * -0.5) * (0.3989422804014327)
            dgelu_out[tt, rows, :] = slope.astype(bf)
            return carry
        lax.fori_loop(0, 2, body, 0)
    def keep(i):
        cols = pl.ds(512 * i, 512)
        cp = pltpu.make_async_copy(full.at[..., cols], full_out.at[..., cols], lo(7 + i))
        cp.start()
        return cp
    kept = []
    for s in range(2, 11):
        if s == 10:
            expand(2)
            expand(3)
        for g, start in ((parts[0], 0), (tiny, 0), (parts[1], 2), (parts[2], 4)):
            if 1 <= s - start <= 6:
                g.stage(s - start)
        if s == 6:
            net.recv(xs, True, lambda: x_all.at[1], sibling)
            for tt in range(4):
                qkv(tt)
            attend(0)
        elif s == 7:
            kept.append(keep(0))
            attend(1)
            attend(2)
        elif s == 8:
            attend(3)
            project()
        elif s == 9:
            kept.append(keep(1))
            normalize()
            net.recv(ns, True, lambda: norm_all.at[1], sibling)
            expand(0)
            expand(1)
    kept.append(keep(2))
    small_out[...] = small_full[...]
    pl.when(jnp.logical_not(cross))(lambda: local[1].wait())
    net.recv(gi, cross, lambda: g_own, diag)
    for cp in kept:
        cp.wait()
    net.drain()

N_GATHER = 156

def run_gather(w_qkv, w_out, w_up, w_down, small, x_in, g_in, ids):
    any_ = pl.BlockSpec(memory_space=pl.ANY)
    vm = pl.BlockSpec(memory_space=pltpu.VMEM)
    rows, width = x_in.shape[2:]
    n = 2 * rows
    bf, f32 = jnp.bfloat16, jnp.float32
    sd = jax.ShapeDtypeStruct
    head = sd((8, n, HD), bf)
    return pl.pallas_call(
        gather_kernel,
        out_shape=(
            sd((4, 2, 2, 2, 128, 1536), bf), sd((4, 2, 2, 2, 16, 128), bf), sd((2, rows, width), bf), sd((rows, width), bf),
            head, head, head, sd((8, n, n), bf), sd((4, n, 128), bf), sd((rows, width), f32), sd((2, rows, width), bf),
            sd((4, n, 512), bf), sd((4, n, 512), bf),
        ),
        in_specs=[any_] * 4 + [vm] + [any_] * 2 + [vm] * 2,
        out_specs=(any_, vm, vm, any_) + (vm,) * 9,
        scratch_shapes=[
            pltpu.VMEM((4, 2, 2, 2, 128, 1536), bf), pltpu.VMEM((4, 2, 2, 2, 16, 128), bf),
            pltpu.VMEM((8, n, HD), bf), pltpu.VMEM((rows, width), bf), pltpu.VMEM((rows, width), bf),
            pltpu.SemaphoreType.DMA((N_GATHER,)), pltpu.SemaphoreType.DMA((N_GATHER,)), pltpu.SemaphoreType.DMA((10,)),
        ],
        compiler_params=pltpu.CompilerParams(collective_id=0, has_side_effects=True),
        name="gather",
    )(w_qkv, w_out, w_up, w_down, small, x_in, g_in, ids[:, None], ids[None, :])


ROWS = {"a": pl.ds(0, 48), "d": pl.ds(48, 48), "ad": pl.ds(0, 96), "b": pl.ds(96, 32)}

class Scatter:
    def __init__(self, net, w, g, bufs, c0, cn):
        self.net, self.w, self.g, self.bufs = net, w, g, bufs
        self.cols = pl.ds(c0, cn)
        self.ids = {}
    def id(self, key):
        if key not in self.ids:
            self.ids[key] = self.net.pair()
        return self.ids[key]
    def take(self, key, cond, buf, place, device):
        cols = self.cols
        def body():
            self.net.recv(self.id(key), True, lambda: buf(), device)
            ref = place()
            ref[...] = (ref[...].astype(jnp.float32) + buf()[...].astype(jnp.float32)).astype(ref.dtype)
        when(cond, body)
    def zstep(self, tag, m, place):
        w = self.w
        for way, me, targets in (("r", m, [j for j in (3, 2, 1) if j >= m]), ("l", 3 - m, [j for j in (0, 1, 2) if j <= 3 - m])):
            buf, step = self.bufs[tag + "z"], 1 if way == "r" else 0
            nxt = w.at(t=w.t + 1) if way == "r" else w.at(t=w.t - 1)
            prv = w.at(t=w.t - 1) if way == "r" else w.at(t=w.t + 1)
            here = w.t == me
            for j in targets:
                land = lambda j=j, buf=buf, step=step: buf.at[j + step, ..., self.cols]
                if m > 0:
                    self.take((tag, way, j), here, land, place(j), prv)
                if j != me:
                    self.net.send(self.id((tag, way, j)), here, place(j), land, nxt)
    def stage(self, k, fill=None):
        w, g, cols, b = self.w, self.g, self.cols, self.bufs
        X, Y = w.at(c=1 - w.c), w.at(y=1 - w.y)
        ad = lambda j: (lambda: g.at[j, w.y, :, w.c, ROWS["ad"], cols])
        bz = lambda j: (lambda: g.at[j, :, :, :, ROWS["b"], cols])
        order = (3, 0, 2, 1)
        if k == 0:
            for j in order:
                fill(j)
                self.net.send(self.id(("ya", j)), True, lambda j=j: g.at[j, 1 - w.y, :, :, ROWS["a"], cols], lambda j=j: b["ya"].at[j, :, :, :, cols], Y)
                self.net.send(self.id(("xd", j)), True, lambda j=j: g.at[j, :, :, 1 - w.c, ROWS["d"], cols], lambda j=j: b["xd"].at[j, :, :, :, cols], X)
            self.zstep("b", 0, bz)
        elif k == 1:
            self.zstep("b", 1, bz)
            for j in order:
                self.take(("ya", j), True, lambda j=j: b["ya"].at[j, :, :, :, cols], lambda j=j: g.at[j, w.y, :, :, ROWS["a"], cols], Y)
                self.net.send(self.id(("xa", j)), True, lambda j=j: g.at[j, w.y, :, 1 - w.c, ROWS["a"], cols], lambda j=j: b["xa"].at[j, :, :, cols], X)
                self.take(("xd", j), True, lambda j=j: b["xd"].at[j, :, :, :, cols], lambda j=j: g.at[j, :, :, w.c, ROWS["d"], cols], X)
                self.net.send(self.id(("yd", j)), True, lambda j=j: g.at[j, 1 - w.y, :, w.c, ROWS["d"], cols], lambda j=j: b["yd"].at[j, :, :, cols], Y)
        elif k == 2:
            self.zstep("b", 2, bz)
            for j in order:
                self.take(("xa", j), True, lambda j=j: b["xa"].at[j, :, :, cols], lambda j=j: g.at[j, w.y, :, w.c, ROWS["a"], cols], X)
                self.take(("yd", j), True, lambda j=j: b["yd"].at[j, :, :, cols], lambda j=j: g.at[j, w.y, :, w.c, ROWS["d"], cols], Y)
            self.zstep("ad", 0, ad)
        elif k == 3:
            self.zstep("b", 3, bz)
            self.net.send(self.id("by"), True, lambda: g.at[w.t, 1 - w.y, :, :, ROWS["b"], cols], lambda: b["by"].at[:, :, :, cols], Y)
            self.zstep("ad", 1, ad)
        elif k == 4:
            self.take("by", True, lambda: b["by"].at[:, :, :, cols], lambda: g.at[w.t, w.y, :, :, ROWS["b"], cols], Y)
            self.net.send(self.id("bx"), True, lambda: g.at[w.t, w.y, :, 1 - w.c, ROWS["b"], cols], lambda: b["bx"].at[:, :, cols], X)
            self.zstep("ad", 2, ad)
        elif k == 5:
            self.zstep("ad", 3, ad)
            self.take("bx", True, lambda: b["bx"].at[:, :, cols], lambda: g.at[w.t, w.y, :, w.c, ROWS["b"], cols], X)
            self.net.send(self.id("sib"), True, lambda: g.at[w.t, w.y, 1 - w.e, w.c, :, cols], lambda: b["sib"].at[:, cols], w.at(e=1 - w.e))
        elif k == 6:
            self.net.recv(self.id("sib"), True, lambda: b["sib"].at[:, cols], w.at(e=1 - w.e))


def scatter_kernel(
    second_low, hidden, norm_low, act_low, first_low, att, q, k, v, p_all, x, first_grad, full, lo, sums,
    o_qkv, o_out, o_up, o_down, lo_out, ig_out, sums_out,
    g, ya, xa, xd, yd, adz, bz, by, bx, sib, sums_run, sums_land, wide, p, agrad, dq, dk, dv, mixed, part, land, ig,
    send_sems, recv_sems, local_sems,
):
    w = Where()
    sem, one, need = barrier(w)
    same = w.e == w.c
    sibling = w.at(e=1 - w.e)
    bf, f32 = jnp.bfloat16, jnp.float32
    for d in range(4):
        go = (lambda d=d: one(w.at(e=w.c, c=w.e, t=(w.t + d) % 4)))
        when(True if d else jnp.logical_not(same), go)
    one(w.at(t=(w.t + 2) % 4))
    pl.semaphore_wait(sem, need + 4 + jnp.where(same, 0, 1))
    net = Net(send_sems, recv_sems)
    bufs = {"ya": ya, "xa": xa, "xd": xd, "yd": yd, "adz": adz, "bz": bz, "by": by, "bx": bx, "sib": sib}
    wide_copy = pltpu.make_async_copy(full.at[..., pl.ds(0, 512)], wide, local_sems.at[0])
    wide_copy.start()
    p_copies = [pltpu.make_async_copy(p_all.at[pl.ds(2 * tt, 2)], p.at[tt % 2], local_sems.at[1 + tt]) for tt in range(4)]
    p_copies[0].start()
    p_copies[1].start()
    down, up, rest = parts = [Scatter(net, w, g, bufs, c0, 512) for c0 in (1024, 512, 0)]

    half = lo.shape[0]
    tokens = 2 * half
    def grads(left, right, i):
        def fill(tt):
            def body(n, carry):
                rows = left[:, pl.ds(pl.multiple_of(n * 256, 256), 256)]
                block = mm(rows, right[tt], ((0,), (0,))).astype(bf)
                g[tt, n // 2, n % 2, :, :, pl.ds(*PIECES[i])] = block.reshape(2, 128, PIECES[i][1])
                return carry
            lax.fori_loop(0, 4, body, 0)
        return fill
    def weight(tt, i):
        return wide[tt, :, :, :, :, pl.ds(*PIECES[i])].reshape(1024, PIECES[i][1])
    def attend_back(tt):
        p_copies[tt].wait()
        upstream = mm(first_low[...], weight(tt, 1), ((1,), (0,))).astype(bf)
        agrad[0] = upstream[:, :HD]
        agrad[1] = upstream[:, HD:]
        dk[...] = jnp.zeros_like(dk)
        dv[...] = jnp.zeros_like(dv)
        def body(n, carry):
            h = n // 2
            head = 2 * tt + h
            rows = pl.ds(pl.multiple_of((n % 2) * half, half), half)
            p_low, above = p[tt % 2, h, rows, :], agrad[h, rows, :]
            prob = p_low.astype(f32)
            prob_grad = mm(above, v[head], ((1,), (1,)))
            row_dot = jnp.sum(prob_grad * prob, axis=1, keepdims=True)
            score_grad = (prob * (prob_grad - row_dot)).astype(bf)
            dq[h, rows, :] = mm(score_grad, k[head], ((1,), (0,)))
            dk[h] += mm(score_grad, q[head, rows, :], ((0,), (0,)))
            dv[h] += mm(p_low, above, ((0,), (0,)))
            return carry
        lax.fori_loop(0, 4, body, 0)
        pieces = []
        for h in range(2):
            query_grad, value_grad = dq[h] * (HD ** -0.5), dv[h]
            pieces += [query_grad, dk[h] * (HD ** -0.5), value_grad]
            row = jnp.concatenate([jnp.sum(query_grad, axis=0, keepdims=True), jnp.sum(value_grad, axis=0, keepdims=True)], axis=1)
            sums_run[0, pl.ds(48 + 8 * w.e + 2 * tt + h, 1), :] = row
        mixed[tt] = jnp.concatenate([a.astype(bf) for a in pieces], axis=1)
        if tt < 2:
            p_copies[tt + 2].start()
    def input_rows(n):
        rows = pl.ds(n * half, half)
        return sum(mm(mixed[tt, rows, :], weight(tt, 0), ((1,), (1,))) for tt in range(4))

    ids = [[net.pair(), net.pair()] for _ in range(4)]
    pi = net.pair()
    def rows_out(kind, src, dst, local):
        for d in range(4):
            t2 = (w.t + d) % 4
            here = lambda t2=t2: src.at[pl.ds(pl.multiple_of(t2 * 64, 64), 64)]
            there = lambda: dst.at[w.t // 2, w.t % 2]
            net.send(ids[d][kind], True if d else jnp.logical_not(same), here, there, w.at(e=w.c, c=w.e, t=t2))
        cp = pltpu.make_async_copy(src.at[pl.ds(pl.multiple_of(w.t * 64, 64), 64)], dst.at[w.t // 2, w.t % 2], local)
        pl.when(same)(lambda: cp.start())
        return cp
    def rows_in(kind, dst):
        for d in range(4):
            t2 = (w.t + 4 - d) % 4
            net.recv(ids[d][kind], True if d else jnp.logical_not(same), lambda t2=t2: dst.at[t2 // 2, t2 % 2], w.at(e=w.c, c=w.e, t=t2))
    partners = (sibling, w.at(c=1 - w.c), w.at(y=1 - w.y), w.at(t=w.t + 1 - 2 * (w.t % 2)), w.at(t=(w.t + 2) % 4))
    sums_ids = [net.pair() for _ in partners]
    def sums_step(s):
        if s > 0:
            net.recv(sums_ids[s - 1], True, lambda: sums_land.at[s - 1], partners[s - 1])
            total = sums_run[s - 1] + sums_land[s - 1]
            if s == 5:
                sums_out[...] = total
            else:
                sums_run[s] = total
        if s < 5:
            net.send(sums_ids[s], True, lambda: sums_run.at[s], lambda: sums_land.at[s], partners[s])
    def finish(*pieces):
        for i in pieces:
            c0, cn = PIECES[i]
            ref = (o_qkv, o_out, o_up, o_down)[i]
            cols = pl.ds(c0, cn)
            ref[:, pl.ds(pl.multiple_of(w.e * cn, 128), cn)] = g[w.t, w.y, w.e, w.c, :, cols].astype(f32)
            ref[:, pl.ds(pl.multiple_of((1 - w.e) * cn, 128), cn)] = sib[:, cols].astype(f32)

    sums_run[0] = sums[...]
    down.stage(0, grads(second_low, hidden, 3))
    up.stage(0, grads(norm_low, act_low, 2))
    own = [rows_out(0, lo, lo_out, local_sems.at[5])]
    wide_copy.wait()
    attend_back(0)
    down.stage(1)
    attend_back(1)
    attend_back(2)
    down.stage(2)
    up.stage(1)
    attend_back(3)
    sums_step(0)
    fill_qkv, fill_out = grads(x, mixed, 0), grads(first_low, att, 1)
    def fill_rest(tt):
        fill_qkv(tt)
        fill_out(tt)
    rest.stage(0, fill_rest)
    sums_step(1)
    down.stage(3)
    up.stage(2)
    part[...] = input_rows(1).astype(bf)
    net.send(pi, True, lambda: part, lambda: land, sibling)
    sums_step(2)
    down.stage(4)
    up.stage(3)
    ig_mine = first_grad[...] + input_rows(0)
    net.recv(pi, True, lambda: land, sibling)
    ig[...] = (ig_mine + land[...].astype(f32)).astype(bf)
    own.append(rows_out(1, ig, ig_out, local_sems.at[6]))
    rest.stage(1)
    sums_step(3)
    down.stage(5)
    up.stage(4)
    rest.stage(2)
    sums_step(4)
    down.stage(6)
    finish(3)
    up.stage(5)
    rest.stage(3)
    up.stage(6)
    finish(2)
    sums_step(5)
    rest.stage(4)
    rest.stage(5)
    rest.stage(6)
    finish(0, 1)
    for cp in own:
        pl.when(same)(lambda cp=cp: cp.wait())
    rows_in(0, lo_out)
    rows_in(1, ig_out)
    net.drain()

N_SCATTER = 107

def run_scatter(second_low, hidden, norm_low, act_low, first_low, att, q, k, v, p_low, x, first_grad, full, lo, sums):
    any_ = pl.BlockSpec(memory_space=pl.ANY)
    vm = pl.BlockSpec(memory_space=pltpu.VMEM)
    f32, bf = jnp.float32, jnp.bfloat16
    n = full.shape[-1]
    rows, width = lo.shape
    tokens = 2 * rows
    share = rows // 4
    sd = jax.ShapeDtypeStruct
    return pl.pallas_call(
        scatter_kernel,
        out_shape=(sd((128, 768), f32), sd((128, 256), f32), sd((128, 1024), f32), sd((128, 1024), f32),
                   sd((2, 2, share, width), bf), sd((2, 2, share, width), bf), sd(sums.shape, f32)),
        in_specs=[vm] * 9 + [any_] + [vm] * 2 + [any_] + [vm] * 2,
        out_specs=(vm, vm, vm, vm, any_, any_, vm),
        scratch_shapes=[pltpu.VMEM((4, 2, 2, 2, 128, n), bf),
                        pltpu.VMEM((4, 2, 2, 48, n), bf), pltpu.VMEM((4, 2, 48, n), bf),
                        pltpu.VMEM((4, 2, 2, 48, n), bf), pltpu.VMEM((4, 2, 48, n), bf),
                        pltpu.VMEM((5, 2, 96, n), bf), pltpu.VMEM((5, 2, 2, 2, 32, n), bf),
                        pltpu.VMEM((2, 2, 32, n), bf), pltpu.VMEM((2, 32, n), bf), pltpu.VMEM((128, n), bf),
                        pltpu.VMEM((5,) + sums.shape, f32), pltpu.VMEM((5,) + sums.shape, f32),
                        pltpu.VMEM((4, 2, 2, 2, 128, 512), bf), pltpu.VMEM((2, 2, tokens, tokens), bf),
                        pltpu.VMEM((2, tokens, HD), bf), pltpu.VMEM((2, tokens, HD), f32), pltpu.VMEM((2, tokens, HD), f32),
                        pltpu.VMEM((2, tokens, HD), f32), pltpu.VMEM((4, tokens, 6 * HD), bf),
                        pltpu.VMEM((rows, width), bf), pltpu.VMEM((rows, width), bf), pltpu.VMEM((rows, width), bf),
                        pltpu.SemaphoreType.DMA((N_SCATTER,)), pltpu.SemaphoreType.DMA((N_SCATTER,)), pltpu.SemaphoreType.DMA((7,))],
        compiler_params=pltpu.CompilerParams(collective_id=1, has_side_effects=True, vmem_limit_bytes=67043328),
        name="scatter",
    )(second_low, hidden, norm_low, act_low, first_low, att, q, k, v, p_low, x, first_grad, full, lo, sums)


def swap_cores(value):
    return lax.ppermute(value, "fsdp", [(i, i ^ 1) for i in range(lax.axis_size("fsdp"))])


def own_rows(part):
    half = part.shape[0] // 2
    return part[:half] + swap_cores(part[half:].astype(jnp.bfloat16)).astype(jnp.float32)


def both_rows(rows_mine):
    return jnp.concatenate([rows_mine, swap_cores(rows_mine)], axis=0)


def dot32(spec, left, right):
    return jnp.einsum(spec, left, right, preferred_element_type=jnp.float32)


def fast_local(
    inputs, out_grad, segment_ids, w_qkv, bias_qv, w_out, w_up, bias_up, w_down, gains, shifts
):
    w = Where()
    bf, f32 = jnp.bfloat16, jnp.float32
    rows, model_width = inputs.shape[2:]
    tokens = 2 * rows
    score_scale = HD ** (-0.5)
    norms_in = jnp.concatenate([gains, shifts], axis=1).T
    qv = bias_qv.reshape(2, 2, 2, HD)
    qkv_bias = jnp.stack([qv[:, :, 0], jnp.zeros_like(qv[:, :, 0]), qv[:, :, 1]], axis=2)
    small = jnp.concatenate(
        [
            jnp.broadcast_to(norms_in, (2, 6, 128)),
            qkv_bias.reshape(2, 3, 128),
            bias_up.reshape(2, 4, 128),
            jnp.zeros((2, 3, 128), bf),
        ],
        axis=1,
    )
    ids = jnp.where(w.e == w.c, segment_ids, swap_cores(segment_ids)).reshape(4, 2, rows)
    ids = lax.dynamic_index_in_dim(ids, w.t, 0, keepdims=False)
    ids = jnp.where(w.e == 0, ids, ids[::-1]).reshape(tokens)
    (
        full_all, small_full, x_all, upstream, queries, key_rows, value_rows, p_low, attended_low,
        first_sum, norm_low, hidden, gelu_slope,
    ) = run_gather(w_qkv, w_out, w_up, w_down, small, inputs, out_grad, ids)
    full = full_all.reshape(4, model_width, -1)
    small_full = small_full.reshape(4, 8, 16, 128)
    norm_all = small_full[0, :, :6].transpose(1, 0, 2).reshape(6, model_width).astype(f32)
    gain_rows, shift_rows = norm_all[:2], norm_all[2:]
    full_up, full_down = (full[:, :, c0 : c0 + cn] for c0, cn in PIECES[2:])
    x_low = x_all.reshape(tokens, model_width)
    norm_low = norm_low.reshape(tokens, model_width)
    first_norm, first_back = jax.vjp(norm_rows, first_sum, gain_rows[0], shift_rows[1])
    down_part = dot32("tnc,tkc->nk", hidden, full_down)
    second_sum = first_norm + own_rows(down_part) + shift_rows[2]
    result, second_back = jax.vjp(norm_rows, second_sum, gain_rows[1], shift_rows[3])
    layer_mine = result.astype(bf)
    second_grad, gain_two, shift_three = second_back(upstream.astype(f32))
    shift_two = jnp.sum(second_grad, axis=0)
    second_low = both_rows(second_grad.astype(bf))
    hidden_grad = dot32("nk,tkc->tnc", second_low, full_down)
    act_grad = hidden_grad * gelu_slope.astype(f32)
    up_bias_grad = jnp.sum(act_grad, axis=1)
    act_low = act_grad.astype(bf)
    back_part = dot32("tnc,tkc->nk", act_low, full_up)
    norm_grad = second_grad + own_rows(back_part)
    first_grad, gain_one, shift_one = first_back(norm_grad)
    shift_zero = jnp.sum(first_grad, axis=0)
    first_low = both_rows(first_grad.astype(bf))
    norm_sums = jnp.stack([gain_one, gain_two, shift_zero, shift_one, shift_two, shift_three])
    up_sums = jnp.stack([jnp.where(w.e == i, up_bias_grad, 0.0) for i in range(2)])
    sums = jnp.concatenate(
        [norm_sums.reshape(48, 128), jnp.zeros((16, 128), f32), up_sums.reshape(32, 128)]
    )
    g_qkv, g_out, g_up, g_down, layer_out, input_out, sums = run_scatter(
        second_low, hidden, norm_low, act_low, first_low, attended_low, queries, key_rows,
        value_rows, p_low, x_low, first_grad, full_all, layer_mine, sums,
    )
    qv_mine = lax.dynamic_index_in_dim(sums[48:64].reshape(2, 4, 256), w.t, 1, keepdims=False)
    up_mine = lax.dynamic_index_in_dim(sums[64:].reshape(2, 4, 512), w.t, 1, keepdims=False)
    block = (2 * w.y + w.e) * 2 + w.c
    norm_mine = lax.dynamic_index_in_dim(sums[:48].reshape(6, 8, 128), block, 1, keepdims=False)
    return (
        layer_out,
        input_out.astype(f32),
        g_qkv,
        qv_mine.reshape(-1),
        g_out,
        g_up,
        up_mine.reshape(-1),
        g_down,
        norm_mine[:2].T,
        norm_mine[2:].T,
    )


def fits_fast(mesh):
    return dict(mesh.shape) == {"fsdp": 4, "ctx": 2, "tp": 4}


def solution(mesh):
    placed = (
        P(None, "fsdp", "ctx", None),
        P(None, "fsdp", "ctx", None),
        P(None, "fsdp", None),
        P(("fsdp", "ctx"), "tp"),
        P("tp"),
        P(("fsdp", "ctx"), "tp"),
        P(("fsdp", "ctx"), "tp"),
        P("tp"),
        P(("fsdp", "ctx"), "tp"),
        P(("fsdp", "ctx"), None),
        P(("fsdp", "ctx"), None),
    )
    return jax.shard_map(
        fast_local if fits_fast(mesh) else local,
        mesh=mesh,
        in_specs=placed,
        out_specs=(
            P(None, "fsdp", ("ctx", "tp"), None),
            P(None, "fsdp", ("ctx", "tp"), None),
            P(("fsdp", "ctx"), "tp"),
            P("tp"),
            P(("fsdp", "ctx"), "tp"),
            P(("fsdp", "ctx"), "tp"),
            P("tp"),
            P(("fsdp", "ctx"), "tp"),
            P(("fsdp", "ctx"), None),
            P(("fsdp", "ctx"), None),
        ),
        check_vma=False,
    )
```

```python
import jax
import jax.numpy as jnp
from jax import lax
from jax.experimental import pallas as pl
from jax.experimental.pallas import tpu as pltpu
from jax.sharding import PartitionSpec as P

HD = 64


norm_epsilon = 1e-12
masked_score = -1e30


def norm_rows(rows_in, gain_row, offset):
    average = jnp.mean(rows_in, axis=-1, keepdims=True)
    centered = rows_in - average
    spread = jnp.mean(centered * centered, axis=-1, keepdims=True)
    return centered * lax.rsqrt(spread + norm_epsilon) * gain_row + offset


def exact_gelu(rows_in):
    return jax.nn.gelu(rows_in, approximate=False)


def contract_rows(left_rows, right_rows):
    return lax.dot_general(
        left_rows, right_rows, (((0,), (0,)), ((), ())), preferred_element_type=jnp.float32
    )


def times_transposed(left_rows, right_rows):
    return lax.dot_general(
        left_rows, right_rows, (((1,), (1,)), ((), ())), preferred_element_type=jnp.float32
    )


def masked_scores(queries, key_rows, same_segment, score_scale):
    scores = (
        jnp.einsum("sqhe,skhe->shqk", queries, key_rows, preferred_element_type=jnp.float32)
        * score_scale
    )
    return jnp.where(same_segment[:, None], scores, masked_score)


def add_pair(running, update):
    return running + update


def reduce_rows(part):
    return lax.psum(part, "tp")


def local(
    inputs, out_grad, segment_ids, w_qkv, bias_qv, w_out, w_up, bias_up, w_down, gains, shifts
):
    batches, seq_local, rows_local, model_width = inputs.shape
    tokens = seq_local * rows_local
    heads_local = w_out.shape[1] // HD
    score_scale = HD ** (-0.5)
    row_share = rows_local // lax.axis_size("tp")
    row_start = lax.axis_index("tp") * row_share
    query_start = lax.axis_index("ctx") * rows_local
    qv_bias = bias_qv.astype(jnp.float32).reshape(heads_local, 2, HD)
    up_bias = bias_up.astype(jnp.float32)

    def pick_rows(values):
        shaped = values.reshape(seq_local, rows_local, model_width)
        return lax.dynamic_slice_in_dim(shaped, row_start, row_share, 1)

    full_totals = (
        jnp.zeros((model_width, w_qkv.shape[1]), jnp.float32),
        jnp.zeros((model_width, w_out.shape[1]), jnp.float32),
        jnp.zeros((model_width, w_up.shape[1]), jnp.float32),
        jnp.zeros((model_width, w_down.shape[1]), jnp.float32),
        jnp.zeros((model_width, 2), jnp.float32),
        jnp.zeros((model_width, 4), jnp.float32),
    )
    share_totals = (
        jnp.zeros(w_qkv.shape, jnp.float32),
        jnp.zeros(w_out.shape, jnp.float32),
        jnp.zeros(w_up.shape, jnp.float32),
        jnp.zeros(w_down.shape, jnp.float32),
        jnp.zeros(gains.shape, jnp.float32),
        jnp.zeros(shifts.shape, jnp.float32),
    )
    qv_bias_grad = jnp.zeros(bias_qv.shape, jnp.float32)
    up_bias_grad = jnp.zeros(bias_up.shape, jnp.float32)
    layer_rows = []
    input_rows = []
    for batch_index in range(batches):
        gathered = (
            lax.all_gather(w_qkv, ("fsdp", "ctx"), axis=0, tiled=True),
            lax.all_gather(w_out, ("fsdp", "ctx"), axis=0, tiled=True),
            lax.all_gather(w_up, ("fsdp", "ctx"), axis=0, tiled=True),
            lax.all_gather(w_down, ("fsdp", "ctx"), axis=0, tiled=True),
            lax.all_gather(gains, ("fsdp", "ctx"), axis=0, tiled=True),
            lax.all_gather(shifts, ("fsdp", "ctx"), axis=0, tiled=True),
        )
        full_qkv, full_out, full_up, full_down, full_gains, full_shifts = gathered
        gain_rows = full_gains.astype(jnp.float32)
        shift_rows = full_shifts.astype(jnp.float32)
        x_low = inputs[batch_index].reshape(tokens, model_width)
        x_full = x_low.astype(jnp.float32)
        projected = jnp.dot(x_low, full_qkv, preferred_element_type=jnp.float32)
        projected = projected.reshape(seq_local, rows_local, heads_local, 3, HD)
        queries = (projected[:, :, :, 0] + qv_bias[:, 0]).astype(jnp.bfloat16)
        key_local = projected[:, :, :, 1].astype(jnp.bfloat16)
        value_local = (projected[:, :, :, 2] + qv_bias[:, 1]).astype(jnp.bfloat16)
        joined = jnp.concatenate([key_local, value_local], axis=-1)
        joined_all = lax.all_gather(joined, "ctx", axis=1, tiled=True)
        key_rows = joined_all[..., :HD]
        value_rows = joined_all[..., HD:]
        segments = segment_ids[batch_index]
        query_segments = lax.dynamic_slice_in_dim(segments, query_start, rows_local, 1)
        same_segment = query_segments[:, :, None] == segments[:, None, :]
        scores = masked_scores(queries, key_rows, same_segment, score_scale)
        row_max = jnp.max(scores, axis=-1, keepdims=True)
        weights = jnp.exp(scores - row_max)
        row_total = jnp.sum(weights, axis=-1, keepdims=True)
        log_total = row_max + jnp.log(row_total)
        p_low = (weights / row_total).astype(jnp.bfloat16)
        attended = jnp.einsum(
            "shqk,skhe->sqhe", p_low, value_rows, preferred_element_type=jnp.float32
        )
        attended_low = attended.reshape(tokens, heads_local * HD).astype(jnp.bfloat16)
        attention_part = times_transposed(attended_low, full_out)
        upstream_full = out_grad[batch_index].reshape(tokens, model_width).astype(jnp.float32)
        attention_total = reduce_rows(attention_part)
        first_sum = x_full + attention_total + shift_rows[:, 0]
        first_norm, first_back = jax.vjp(norm_rows, first_sum, gain_rows[:, 0], shift_rows[:, 1])
        norm_low = first_norm.astype(jnp.bfloat16)
        before_act = jnp.dot(norm_low, full_up, preferred_element_type=jnp.float32) + up_bias
        activated, gelu_back = jax.vjp(exact_gelu, before_act)
        hidden = activated.astype(jnp.bfloat16)
        down_part = times_transposed(hidden, full_down)
        down_total = reduce_rows(down_part)
        second_sum = first_norm + down_total + shift_rows[:, 2]
        result, second_back = jax.vjp(norm_rows, second_sum, gain_rows[:, 1], shift_rows[:, 3])
        layer_rows.append(pick_rows(result).astype(jnp.bfloat16))
        second_grad, gain_two, shift_three = second_back(upstream_full)
        shift_two = jnp.sum(second_grad, axis=0)
        second_low = second_grad.astype(jnp.bfloat16)
        down_step = contract_rows(second_low, hidden)
        hidden_grad = jnp.dot(second_low, full_down, preferred_element_type=jnp.float32)
        (act_grad,) = gelu_back(hidden_grad)
        up_bias_grad = up_bias_grad + jnp.sum(act_grad, axis=0)
        act_low = act_grad.astype(jnp.bfloat16)
        up_step = contract_rows(norm_low, act_low)
        back_part = times_transposed(act_low, full_up)
        back_total = reduce_rows(back_part)
        norm_grad = second_grad + back_total
        first_grad, gain_one, shift_one = first_back(norm_grad)
        shift_zero = jnp.sum(first_grad, axis=0)
        first_low = first_grad.astype(jnp.bfloat16)
        out_step = contract_rows(first_low, attended_low)
        attended_grad = jnp.dot(first_low, full_out, preferred_element_type=jnp.float32)
        attended_grad = attended_grad.astype(jnp.bfloat16).reshape(
            seq_local, rows_local, heads_local, HD
        )
        scores = masked_scores(queries, key_rows, same_segment, score_scale)
        probabilities = jnp.exp(scores - log_total)
        value_grad = jnp.einsum(
            "shqk,sqhe->skhe",
            probabilities.astype(jnp.bfloat16),
            attended_grad,
            preferred_element_type=jnp.float32,
        )
        prob_grad = jnp.einsum(
            "sqhe,skhe->shqk", attended_grad, value_rows, preferred_element_type=jnp.float32
        )
        row_dot = jnp.sum(prob_grad * probabilities, axis=-1, keepdims=True)
        score_grad = (probabilities * (prob_grad - row_dot)).astype(jnp.bfloat16)
        query_grad = (
            jnp.einsum("shqk,skhe->sqhe", score_grad, key_rows, preferred_element_type=jnp.float32)
            * score_scale
        )
        key_grad = (
            jnp.einsum("shqk,sqhe->skhe", score_grad, queries, preferred_element_type=jnp.float32)
            * score_scale
        )
        kv_grads = lax.psum_scatter(
            jnp.concatenate([key_grad, value_grad], axis=-1).astype(jnp.bfloat16),
            "ctx",
            scatter_dimension=1,
            tiled=True,
        ).astype(jnp.float32)
        key_mine = kv_grads[..., :HD]
        value_mine = kv_grads[..., HD:]
        bias_step = jnp.stack(
            [jnp.sum(query_grad, axis=(0, 1)), jnp.sum(value_mine, axis=(0, 1))], axis=1
        )
        qv_bias_grad = qv_bias_grad + bias_step.reshape(-1)
        mixed_grad = jnp.stack([query_grad, key_mine, value_mine], axis=3)
        mixed_grad = mixed_grad.reshape(tokens, 3 * heads_local * HD).astype(jnp.bfloat16)
        qkv_step = contract_rows(x_low, mixed_grad)
        input_part = times_transposed(mixed_grad, full_qkv).reshape(
            seq_local, rows_local, model_width
        )
        input_mine = lax.psum_scatter(
            input_part.astype(jnp.bfloat16), "tp", scatter_dimension=1, tiled=True
        ).astype(jnp.float32)
        first_part = pick_rows(first_grad)
        input_rows.append(input_mine + first_part)
        gain_step = jnp.stack([gain_one, gain_two], axis=1)
        shift_step = jnp.stack([shift_zero, shift_one, shift_two, shift_three], axis=1)
        full_totals = tuple(
            map(
                add_pair,
                full_totals,
                (qkv_step, out_step, up_step, down_step, gain_step, shift_step),
            )
        )
    share_totals = (
        lax.psum_scatter(
            full_totals[0].astype(jnp.bfloat16), ("fsdp", "ctx"), scatter_dimension=0, tiled=True
        ).astype(jnp.float32),
        lax.psum_scatter(
            full_totals[1].astype(jnp.bfloat16), ("fsdp", "ctx"), scatter_dimension=0, tiled=True
        ).astype(jnp.float32),
        lax.psum_scatter(
            full_totals[2].astype(jnp.bfloat16), ("fsdp", "ctx"), scatter_dimension=0, tiled=True
        ).astype(jnp.float32),
        lax.psum_scatter(
            full_totals[3].astype(jnp.bfloat16), ("fsdp", "ctx"), scatter_dimension=0, tiled=True
        ).astype(jnp.float32),
        lax.psum_scatter(
            full_totals[4].astype(jnp.bfloat16), ("fsdp", "ctx"), scatter_dimension=0, tiled=True
        ).astype(jnp.float32),
        lax.psum_scatter(
            full_totals[5].astype(jnp.bfloat16), ("fsdp", "ctx"), scatter_dimension=0, tiled=True
        ).astype(jnp.float32),
    )
    qv_total, up_total = lax.psum((qv_bias_grad, up_bias_grad), ("fsdp", "ctx"))
    return (
        jnp.stack(layer_rows, axis=0),
        jnp.stack(input_rows, axis=0),
        share_totals[0],
        qv_total,
        share_totals[1],
        share_totals[2],
        up_total,
        share_totals[3],
        share_totals[4],
        share_totals[5],
    )


MESH = pl.DeviceIdType.MESH
ROW_A, ROW_D, ROW_AD, ROW_B = (0, 48), (48, 48), (0, 96), (96, 32)

class Where:
    def __init__(self):
        fsdp = lax.axis_index("fsdp")
        self.y = fsdp // 2
        self.e = fsdp % 2
        self.c = lax.axis_index("ctx")
        self.t = lax.axis_index("tp")
    def at(self, y=None, e=None, c=None, t=None):
        y = self.y if y is None else y
        e = self.e if e is None else e
        c = self.c if c is None else c
        t = self.t if t is None else t
        return (2 * y + e, c, t)

def when(cond, fn):
    if cond is True:
        fn()
    else:
        pl.when(cond)(fn)

class Net:
    def __init__(self, send_sems, recv_sems):
        self.send_sems, self.recv_sems, self.count, self.pending = send_sems, recv_sems, 0, []
    def pair(self):
        self.count += 1
        return self.count - 1
    def send(self, index, cond, src, dst, device):
        def make():
            return pltpu.make_async_remote_copy(
                src_ref=src(), dst_ref=dst(), send_sem=self.send_sems.at[index],
                recv_sem=self.recv_sems.at[index], device_id=device, device_id_type=MESH)
        when(cond, lambda: make().start())
        self.pending.append((cond, make))
    def recv(self, index, cond, here, device):
        def wait():
            pltpu.make_async_remote_copy(
                src_ref=here(), dst_ref=here(), send_sem=self.send_sems.at[index],
                recv_sem=self.recv_sems.at[index], device_id=device, device_id_type=MESH).wait_recv()
        when(cond, wait)
    def drain(self):
        for cond, make in self.pending:
            when(cond, lambda make=make: make().wait_send())

def slots_of(w):
    t = w.t
    return [("own", t, True), ("l1", t - 1, t >= 1), ("r1", t + 1, t <= 2), ("l2", t - 2, t >= 2),
            ("r2", t + 2, t <= 1), ("l3", t - 3, t >= 3), ("r3", t + 3, t <= 0)]

class Gather:
    STAGES = 7
    def __init__(self, net, w, sources, full, c0, cn, local_sems, routes=(ROW_A, ROW_D, ROW_AD, ROW_B)):
        self.net, self.w, self.sources, self.full, self.local_sems = net, w, sources, full, local_sems
        self.cols = pl.ds(c0, cn)
        self.row_a, self.row_d, self.row_ad, self.row_b = [None if r is None else pl.ds(*r) for r in routes]
        self.slots = slots_of(w)
        self.ids = {}
    def id(self, key):
        if key not in self.ids:
            self.ids[key] = self.net.pair()
        return self.ids[key]
    def blk(self, tt, rows, y=None, c=None):
        w = self.w
        y = w.y if y is None else y
        c = w.c if c is None else c
        return lambda: self.full.at[tt, y, :, c, rows, self.cols]
    def row(self, tt, rows, y=None):
        y = self.w.y if y is None else y
        return lambda: self.full.at[tt, y, :, :, rows, self.cols]
    def colm(self, tt, rows, c=None):
        c = self.w.c if c is None else c
        return lambda: self.full.at[tt, :, :, c, rows, self.cols]
    def plane(self, tt, rows):
        return lambda: self.full.at[tt, :, :, :, rows, self.cols]
    def same(self, key, cond, ref, device):
        self.net.send(self.id(key), cond, ref, ref, device)
    def sib(self):
        w = self.w
        self.own_copies = []
        for n, (src, c0, cn) in enumerate(self.sources):
            dst = lambda c0=c0, cn=cn: self.full.at[w.t, w.y, w.e, w.c, :, pl.ds(c0, cn)]
            self.net.send(self.id(("sib", n)), True, lambda src=src: src(1 - w.e), dst, w.at(e=1 - w.e))
            self.own_copies.append(pltpu.make_async_copy(src(w.e), dst(), self.local_sems[n]))
            self.own_copies[-1].start()
    def sib_done(self):
        w = self.w
        for n, (src, c0, cn) in enumerate(self.sources):
            self.own_copies[n].wait()
            self.net.recv(self.id(("sib", n)), True, lambda c0=c0, cn=cn: self.full.at[w.t, w.y, 1 - w.e, w.c, :, pl.ds(c0, cn)], w.at(e=1 - w.e))
    def zsend(self, tag, slot, ref):
        w = self.w
        k = {"own": 0, "l1": 1, "r1": 1, "l2": 2, "r2": 2}[slot]
        if slot == "own" or slot[0] == "l":
            name, tt, ok = self.slot("own" if k == 0 else f"l{k}")
            self.same((tag, "zr", k), (w.t < 3) if ok is True else jnp.logical_and(ok, w.t < 3), ref(tt), w.at(t=w.t + 1))
        if slot == "own" or slot[0] == "r":
            name, tt, ok = self.slot("own" if k == 0 else f"r{k}")
            self.same((tag, "zl", k), (w.t > 0) if ok is True else jnp.logical_and(ok, w.t > 0), ref(tt), w.at(t=w.t - 1))
    def zrecv(self, tag, slot, ref):
        w = self.w
        k = int(slot[1])
        _, tt, ok = self.slot(slot)
        if slot[0] == "l":
            self.net.recv(self.id((tag, "zr", k - 1)), ok, ref(tt), w.at(t=w.t - 1))
        else:
            self.net.recv(self.id((tag, "zl", k - 1)), ok, ref(tt), w.at(t=w.t + 1))
    def slot(self, name):
        return next(s for s in self.slots if s[0] == name)
    def first_hop(self, name):
        w = self.w
        _, tt, ok = self.slot(name)
        self.same(("ax", name), ok, self.blk(tt, self.row_a), w.at(c=1 - w.c))
        if self.row_d is not None:
            self.same(("dy", name), ok, self.blk(tt, self.row_d), w.at(y=1 - w.y))
    def second_hop(self, name):
        w = self.w
        _, tt, ok = self.slot(name)
        self.net.recv(self.id(("ax", name)), ok, self.blk(tt, self.row_a, c=1 - w.c), w.at(c=1 - w.c))
        self.same(("ay", name), ok, self.row(tt, self.row_a), w.at(y=1 - w.y))
        if self.row_d is not None:
            self.net.recv(self.id(("dy", name)), ok, self.blk(tt, self.row_d, y=1 - w.y), w.at(y=1 - w.y))
            self.same(("dx", name), ok, self.colm(tt, self.row_d), w.at(c=1 - w.c))
    def last(self, name):
        w = self.w
        _, tt, ok = self.slot(name)
        self.net.recv(self.id(("ay", name)), ok, self.row(tt, self.row_a, y=1 - w.y), w.at(y=1 - w.y))
        if self.row_d is not None:
            self.net.recv(self.id(("dx", name)), ok, self.colm(tt, self.row_d, c=1 - w.c), w.at(c=1 - w.c))
    def stage(self, k):
        w = self.w
        ad = lambda tt: self.blk(tt, self.row_ad)
        bz = lambda tt: self.plane(tt, self.row_b)
        b = self.row_b is not None
        if k == 0:
            self.sib()
        elif k == 1:
            self.sib_done()
            self.zsend("ad", "own", ad)
            if b:
                self.same("bx", True, self.blk(w.t, self.row_b), w.at(c=1 - w.c))
            self.first_hop("own")
        elif k == 2:
            if b:
                self.net.recv(self.id("bx"), True, self.blk(w.t, self.row_b, c=1 - w.c), w.at(c=1 - w.c))
                self.same("by", True, self.row(w.t, self.row_b), w.at(y=1 - w.y))
            for s in ("l1", "r1"):
                self.zrecv("ad", s, ad)
                self.zsend("ad", s, ad)
                self.first_hop(s)
            self.second_hop("own")
        elif k == 3:
            if b:
                self.net.recv(self.id("by"), True, self.row(w.t, self.row_b, y=1 - w.y), w.at(y=1 - w.y))
                self.zsend("b", "own", bz)
            for s in ("l2", "r2"):
                self.zrecv("ad", s, ad)
                self.zsend("ad", s, ad)
                self.first_hop(s)
            for s in ("l1", "r1"):
                self.second_hop(s)
        elif k == 4:
            if b:
                for s in ("l1", "r1"):
                    self.zrecv("b", s, bz)
                    self.zsend("b", s, bz)
            for s in ("l3", "r3"):
                self.zrecv("ad", s, ad)
                self.first_hop(s)
            for s in ("l2", "r2"):
                self.second_hop(s)
        elif k == 5:
            if b:
                for s in ("l2", "r2"):
                    self.zrecv("b", s, bz)
                    self.zsend("b", s, bz)
            for s in ("l3", "r3"):
                self.second_hop(s)
        elif k == 6:
            if b:
                for s in ("l3", "r3"):
                    self.zrecv("b", s, bz)
            for name, _, _ in self.slots:
                self.last(name)

def barrier(w, extra=()):
    sem = pltpu.get_barrier_semaphore()
    one = lambda dev: pl.semaphore_signal(sem, inc=1, device_id=dev, device_id_type=MESH)
    one(w.at(e=1 - w.e)); one(w.at(c=1 - w.c)); one(w.at(y=1 - w.y))
    pl.when(w.t > 0)(lambda: one(w.at(t=w.t - 1)))
    pl.when(w.t < 3)(lambda: one(w.at(t=w.t + 1)))
    ends = jnp.where(w.t == 0, 1, 0) + jnp.where(w.t == 3, 1, 0)
    return sem, one, 5 - ends

PIECES = ((0, 384), (384, 128), (512, 512), (1024, 512))


def mm(left, right, dims):
    return lax.dot_general(left, right, (dims, ((), ())), preferred_element_type=jnp.float32)


def gather_kernel(
    w_qkv, w_out, w_up, w_down, small, x_in, g_in, ids_col, ids_row,
    full_out, small_out, x_all, g_own, q_out, k_out, v_out, p_out, att_out, sum_out, norm_all, hid_out, dgelu_out,
    full, small_full, att_s, part, land, send_sems, recv_sems, local_sems,
):
    w = Where()
    sem, one, need = barrier(w)
    cross = w.e != w.c
    diag = w.at(e=1 - w.e, c=1 - w.c)
    sibling = w.at(e=1 - w.e)
    pl.when(cross)(lambda: one(diag))
    pl.semaphore_wait(sem, need + jnp.where(cross, 1, 0))
    net = Net(send_sems, recv_sems)
    bf, f32 = jnp.bfloat16, jnp.float32
    seq = lambda ref: ref.at[w.t // 2, w.t % 2]
    def source(ref, i):
        c0, cn = PIECES[i]
        return (lambda e: ref.at[:, pl.ds(pl.multiple_of(e * cn, 128), cn)]), c0, cn
    lo = lambda n: local_sems.at[n]
    tiny = Gather(net, w, [(lambda e: small.at[e], 0, 128)], small_full, 0, 128, [lo(0)], routes=((0, 16), None, (0, 16), None))
    parts = [
        Gather(net, w, [source(w_qkv, 0), source(w_out, 1)], full, 0, 512, [lo(1), lo(2)]),
        Gather(net, w, [source(w_up, 2)], full, 512, 512, [lo(3)]),
        Gather(net, w, [source(w_down, 3)], full, 1024, 512, [lo(4)]),
    ]
    xi, gi, xs, ps, ns = [net.pair() for _ in range(5)]
    parts[0].stage(0)
    tiny.stage(0)
    for idx, src, dst in ((xi, x_in, x_all.at[0]), (gi, g_in, g_own)):
        net.send(idx, cross, lambda src=src: seq(src), lambda dst=dst: dst, diag)
    local = [pltpu.make_async_copy(seq(x_in), x_all.at[0], lo(5)), pltpu.make_async_copy(seq(g_in), g_own, lo(6))]
    for cp in local:
        pl.when(jnp.logical_not(cross))(lambda cp=cp: cp.start())
    parts[1].stage(0)
    parts[2].stage(0)
    parts[0].stage(1)
    tiny.stage(1)
    pl.when(jnp.logical_not(cross))(lambda: local[0].wait())
    net.recv(xi, cross, lambda: x_all.at[0], diag)
    net.send(xs, True, lambda: x_all.at[0], lambda: x_all.at[1], sibling)

    half = x_all.shape[1]
    tokens = 2 * half
    def norm_row(k):
        rows = small_full[0, :, :, :, pl.ds(k, 1), :].astype(f32).reshape(8, 128)
        return jnp.concatenate([rows[i : i + 1] for i in range(8)], axis=1)
    def bias_row(tt, k, n):
        rows = small_full[tt, 0, 0, 0].astype(f32)
        return jnp.concatenate([rows[k + i : k + i + 1] for i in range(n)], axis=1)
    def weight(tt, i):
        return full[tt, :, :, :, :, pl.ds(*PIECES[i])].reshape(1024, PIECES[i][1])
    def qkv(tt):
        x = x_all[...].reshape(tokens, 1024)
        proj = (mm(x, weight(tt, 0), ((1,), (0,))) + bias_row(tt, 6, 3)).astype(bf)
        for h in range(2):
            for n, ref in enumerate((q_out, k_out, v_out)):
                ref[2 * tt + h] = proj[:, (3 * h + n) * HD : (3 * h + n + 1) * HD]
    def attend(tt):
        def body(n, carry):
            h = 2 * tt + n // 2
            rows = pl.ds(pl.multiple_of((n % 2) * half, half), half)
            scores = mm(q_out[h, rows, :], k_out[h], ((1,), (1,))) * (HD ** -0.5)
            scores = jnp.where(ids_col[rows, :] == ids_row[...], scores, masked_score)
            weights = jnp.exp(scores - jnp.max(scores, axis=1, keepdims=True))
            p_low = (weights / jnp.sum(weights, axis=1, keepdims=True)).astype(bf)
            p_out[h, rows, :] = p_low
            att_s[h, rows, :] = mm(p_low, v_out[h], ((1,), (0,))).astype(bf)
            return carry
        lax.fori_loop(0, 4, body, 0)
        att_out[tt] = jnp.concatenate([att_s[2 * tt], att_s[2 * tt + 1]], axis=1)
    def project():
        for n in (1, 0):
            rows = pl.ds(n * half, half)
            total = sum(mm(att_out[tt, rows, :], weight(tt, 1), ((1,), (1,))) for tt in range(4))
            if n == 1:
                part[...] = total.astype(bf)
                net.send(ps, True, lambda: part, lambda: land, sibling)
            else:
                sum_out[...] = total + x_all[0].astype(f32) + norm_row(2)
    def normalize():
        net.recv(ps, True, lambda: land, sibling)
        total = sum_out[...] + land[...].astype(f32)
        sum_out[...] = total
        norm_all[0] = norm_rows(total, norm_row(0), norm_row(3)).astype(bf)
        net.send(ns, True, lambda: norm_all.at[0], lambda: norm_all.at[1], sibling)
    def expand(tt):
        bias = bias_row(tt, 9, 4)
        def body(n, carry):
            before = mm(norm_all[n], weight(tt, 2), ((1,), (0,))) + bias
            rows = pl.ds(pl.multiple_of(n * half, half), half)
            bell = (1.0 + lax.erf(before * (2.0 ** -0.5))) * 0.5
            hid_out[tt, rows, :] = (before * bell).astype(bf)
            slope = bell + before * jnp.exp(before * before * -0.5) * (0.3989422804014327)
            dgelu_out[tt, rows, :] = slope.astype(bf)
            return carry
        lax.fori_loop(0, 2, body, 0)
    def keep(i):
        cols = pl.ds(512 * i, 512)
        cp = pltpu.make_async_copy(full.at[..., cols], full_out.at[..., cols], lo(7 + i))
        cp.start()
        return cp
    kept = []
    for s in range(2, 11):
        if s == 10:
            expand(2)
            expand(3)
        for g, start in ((parts[0], 0), (tiny, 0), (parts[1], 2), (parts[2], 4)):
            if 1 <= s - start <= 6:
                g.stage(s - start)
        if s == 6:
            net.recv(xs, True, lambda: x_all.at[1], sibling)
            for tt in range(4):
                qkv(tt)
            attend(0)
        elif s == 7:
            kept.append(keep(0))
            attend(1)
            attend(2)
        elif s == 8:
            attend(3)
            project()
        elif s == 9:
            kept.append(keep(1))
            normalize()
            net.recv(ns, True, lambda: norm_all.at[1], sibling)
            expand(0)
            expand(1)
    kept.append(keep(2))
    small_out[...] = small_full[...]
    pl.when(jnp.logical_not(cross))(lambda: local[1].wait())
    net.recv(gi, cross, lambda: g_own, diag)
    for cp in kept:
        cp.wait()
    net.drain()

N_GATHER = 156

def run_gather(w_qkv, w_out, w_up, w_down, small, x_in, g_in, ids):
    any_ = pl.BlockSpec(memory_space=pl.ANY)
    vm = pl.BlockSpec(memory_space=pltpu.VMEM)
    rows, width = x_in.shape[2:]
    n = 2 * rows
    bf, f32 = jnp.bfloat16, jnp.float32
    sd = jax.ShapeDtypeStruct
    head = sd((8, n, HD), bf)
    return pl.pallas_call(
        gather_kernel,
        out_shape=(
            sd((4, 2, 2, 2, 128, 1536), bf), sd((4, 2, 2, 2, 16, 128), bf), sd((2, rows, width), bf), sd((rows, width), bf),
            head, head, head, sd((8, n, n), bf), sd((4, n, 128), bf), sd((rows, width), f32), sd((2, rows, width), bf),
            sd((4, n, 512), bf), sd((4, n, 512), bf),
        ),
        in_specs=[any_] * 4 + [vm] + [any_] * 2 + [vm] * 2,
        out_specs=(any_, vm, vm, any_) + (vm,) * 9,
        scratch_shapes=[
            pltpu.VMEM((4, 2, 2, 2, 128, 1536), bf), pltpu.VMEM((4, 2, 2, 2, 16, 128), bf),
            pltpu.VMEM((8, n, HD), bf), pltpu.VMEM((rows, width), bf), pltpu.VMEM((rows, width), bf),
            pltpu.SemaphoreType.DMA((N_GATHER,)), pltpu.SemaphoreType.DMA((N_GATHER,)), pltpu.SemaphoreType.DMA((10,)),
        ],
        compiler_params=pltpu.CompilerParams(collective_id=0, has_side_effects=True),
        name="gather",
    )(w_qkv, w_out, w_up, w_down, small, x_in, g_in, ids[:, None], ids[None, :])


ROWS = {"a": pl.ds(0, 48), "d": pl.ds(48, 48), "ad": pl.ds(0, 96), "b": pl.ds(96, 32)}

class Scatter:
    def __init__(self, net, w, g, bufs, c0, cn):
        self.net, self.w, self.g, self.bufs = net, w, g, bufs
        self.cols = pl.ds(c0, cn)
        self.ids = {}
    def id(self, key):
        if key not in self.ids:
            self.ids[key] = self.net.pair()
        return self.ids[key]
    def take(self, key, cond, buf, place, device):
        cols = self.cols
        def body():
            self.net.recv(self.id(key), True, lambda: buf(), device)
            ref = place()
            ref[...] = (ref[...].astype(jnp.float32) + buf()[...].astype(jnp.float32)).astype(ref.dtype)
        when(cond, body)
    def zstep(self, tag, m, place):
        w = self.w
        for way, me, targets in (("r", m, [j for j in (3, 2, 1) if j >= m]), ("l", 3 - m, [j for j in (0, 1, 2) if j <= 3 - m])):
            buf, step = self.bufs[tag + "z"], 1 if way == "r" else 0
            nxt = w.at(t=w.t + 1) if way == "r" else w.at(t=w.t - 1)
            prv = w.at(t=w.t - 1) if way == "r" else w.at(t=w.t + 1)
            here = w.t == me
            for j in targets:
                land = lambda j=j, buf=buf, step=step: buf.at[j + step, ..., self.cols]
                if m > 0:
                    self.take((tag, way, j), here, land, place(j), prv)
                if j != me:
                    self.net.send(self.id((tag, way, j)), here, place(j), land, nxt)
    def stage(self, k, fill=None):
        w, g, cols, b = self.w, self.g, self.cols, self.bufs
        X, Y = w.at(c=1 - w.c), w.at(y=1 - w.y)
        ad = lambda j: (lambda: g.at[j, w.y, :, w.c, ROWS["ad"], cols])
        bz = lambda j: (lambda: g.at[j, :, :, :, ROWS["b"], cols])
        order = (3, 0, 2, 1)
        if k == 0:
            for j in order:
                fill(j)
                self.net.send(self.id(("ya", j)), True, lambda j=j: g.at[j, 1 - w.y, :, :, ROWS["a"], cols], lambda j=j: b["ya"].at[j, :, :, :, cols], Y)
                self.net.send(self.id(("xd", j)), True, lambda j=j: g.at[j, :, :, 1 - w.c, ROWS["d"], cols], lambda j=j: b["xd"].at[j, :, :, :, cols], X)
            self.zstep("b", 0, bz)
        elif k == 1:
            self.zstep("b", 1, bz)
            for j in order:
                self.take(("ya", j), True, lambda j=j: b["ya"].at[j, :, :, :, cols], lambda j=j: g.at[j, w.y, :, :, ROWS["a"], cols], Y)
                self.net.send(self.id(("xa", j)), True, lambda j=j: g.at[j, w.y, :, 1 - w.c, ROWS["a"], cols], lambda j=j: b["xa"].at[j, :, :, cols], X)
                self.take(("xd", j), True, lambda j=j: b["xd"].at[j, :, :, :, cols], lambda j=j: g.at[j, :, :, w.c, ROWS["d"], cols], X)
                self.net.send(self.id(("yd", j)), True, lambda j=j: g.at[j, 1 - w.y, :, w.c, ROWS["d"], cols], lambda j=j: b["yd"].at[j, :, :, cols], Y)
        elif k == 2:
            self.zstep("b", 2, bz)
            for j in order:
                self.take(("xa", j), True, lambda j=j: b["xa"].at[j, :, :, cols], lambda j=j: g.at[j, w.y, :, w.c, ROWS["a"], cols], X)
                self.take(("yd", j), True, lambda j=j: b["yd"].at[j, :, :, cols], lambda j=j: g.at[j, w.y, :, w.c, ROWS["d"], cols], Y)
            self.zstep("ad", 0, ad)
        elif k == 3:
            self.zstep("b", 3, bz)
            self.net.send(self.id("by"), True, lambda: g.at[w.t, 1 - w.y, :, :, ROWS["b"], cols], lambda: b["by"].at[:, :, :, cols], Y)
            self.zstep("ad", 1, ad)
        elif k == 4:
            self.take("by", True, lambda: b["by"].at[:, :, :, cols], lambda: g.at[w.t, w.y, :, :, ROWS["b"], cols], Y)
            self.net.send(self.id("bx"), True, lambda: g.at[w.t, w.y, :, 1 - w.c, ROWS["b"], cols], lambda: b["bx"].at[:, :, cols], X)
            self.zstep("ad", 2, ad)
        elif k == 5:
            self.zstep("ad", 3, ad)
            self.take("bx", True, lambda: b["bx"].at[:, :, cols], lambda: g.at[w.t, w.y, :, w.c, ROWS["b"], cols], X)
            self.net.send(self.id("sib"), True, lambda: g.at[w.t, w.y, 1 - w.e, w.c, :, cols], lambda: b["sib"].at[:, cols], w.at(e=1 - w.e))
        elif k == 6:
            self.net.recv(self.id("sib"), True, lambda: b["sib"].at[:, cols], w.at(e=1 - w.e))


def scatter_kernel(
    second_low, hidden, norm_low, slope_all, att, q, k, v, p_all, x, first_sum, second_grad, gain, full, lo, sums,
    o_qkv, o_out, o_up, o_down, lo_out, ig_out, sums_out,
    g, ya, xa, xd, yd, adz, bz, by, bx, sib, sums_run, sums_land, wide, stream, slope, act_low, first_low, first_grad, back, agrad, dq, dk, dv, mixed, part, land, part_two, land_two, ig,
    send_sems, recv_sems, local_sems,
):
    w = Where()
    sem, one, need = barrier(w)
    same = w.e == w.c
    sibling = w.at(e=1 - w.e)
    bf, f32 = jnp.bfloat16, jnp.float32
    for d in range(4):
        go = (lambda d=d: one(w.at(e=w.c, c=w.e, t=(w.t + d) % 4)))
        when(True if d else jnp.logical_not(same), go)
    one(w.at(t=(w.t + 2) % 4))
    pl.semaphore_wait(sem, need + 4 + jnp.where(same, 0, 1))
    net = Net(send_sems, recv_sems)
    bufs = {"ya": ya, "xa": xa, "xd": xd, "yd": yd, "adz": adz, "bz": bz, "by": by, "bx": bx, "sib": sib}
    wide_copy = pltpu.make_async_copy(full.at[..., pl.ds(0, 512)], wide, local_sems.at[0])
    wide_copy.start()
    order = (3, 0, 2, 1)
    sources = [full.at[tt, :, :, :, :, pl.ds(*PIECES[3])] for tt in order] + [full.at[tt, :, :, :, :, pl.ds(*PIECES[2])] for tt in range(4)]
    sources += [p_all.at[pl.ds(2 * tt, 2)] for tt in range(4)]
    loads = [pltpu.make_async_copy(src, stream.at[n % 2], local_sems.at[7 + n]) for n, src in enumerate(sources)]
    slopes = [pltpu.make_async_copy(slope_all.at[tt], slope.at[n % 2], local_sems.at[1 + n]) for n, tt in enumerate(order)]
    for cp in loads[:2] + slopes[:2]:
        cp.start()
    def used(copies, n):
        if n + 2 < len(copies):
            copies[n + 2].start()
    down, up, rest = parts = [Scatter(net, w, g, bufs, c0, 512) for c0 in (1024, 512, 0)]

    half = lo.shape[0]
    tokens = 2 * half
    def grads(left, right, i):
        def fill(tt):
            def body(n, carry):
                rows = left[..., pl.ds(pl.multiple_of(n * 256, 256), 256)].reshape(tokens, 256)
                block = mm(rows, right[tt], ((0,), (0,))).astype(bf)
                g[tt, n // 2, n % 2, :, :, pl.ds(*PIECES[i])] = block.reshape(2, 128, PIECES[i][1])
                return carry
            lax.fori_loop(0, 4, body, 0)
        return fill
    def weight(tt, i):
        return wide[tt, :, :, :, :, pl.ds(*PIECES[i])].reshape(1024, PIECES[i][1])
    def attend_back(tt):
        loads[8 + tt].wait()
        upstream = mm(first_low[...].reshape(tokens, 1024), weight(tt, 1), ((1,), (0,))).astype(bf)
        agrad[0] = upstream[:, :HD]
        agrad[1] = upstream[:, HD:]
        dk[...] = jnp.zeros_like(dk)
        dv[...] = jnp.zeros_like(dv)
        def body(n, carry):
            h = n // 2
            head = 2 * tt + h
            rows = pl.ds(pl.multiple_of((n % 2) * half, half), half)
            p_low, above = stream[tt % 2, h, n % 2].reshape(half, tokens), agrad[h, rows, :]
            prob = p_low.astype(f32)
            prob_grad = mm(above, v[head], ((1,), (1,)))
            row_dot = jnp.sum(prob_grad * prob, axis=1, keepdims=True)
            score_grad = (prob * (prob_grad - row_dot)).astype(bf)
            dq[h, rows, :] = mm(score_grad, k[head], ((1,), (0,)))
            dk[h] += mm(score_grad, q[head, rows, :], ((0,), (0,)))
            dv[h] += mm(p_low, above, ((0,), (0,)))
            return carry
        lax.fori_loop(0, 4, body, 0)
        pieces = []
        for h in range(2):
            query_grad, value_grad = dq[h] * (HD ** -0.5), dv[h]
            pieces += [query_grad, dk[h] * (HD ** -0.5), value_grad]
            row = jnp.concatenate([jnp.sum(query_grad, axis=0, keepdims=True), jnp.sum(value_grad, axis=0, keepdims=True)], axis=1)
            sums_run[0, pl.ds(48 + 8 * w.e + 2 * tt + h, 1), :] = row
        mixed[tt] = jnp.concatenate([a.astype(bf) for a in pieces], axis=1)
        used(loads, 8 + tt)
    def activate(tt):
        n = order.index(tt)
        loads[n].wait()
        slopes[n].wait()
        hidden_grad = mm(second_low[...], stream[n % 2].reshape(1024, 512), ((1,), (0,)))
        act_grad = hidden_grad * slope[n % 2].astype(f32)
        act_low[tt] = act_grad.astype(bf)
        used(loads, n)
        used(slopes, n)
        total = jnp.sum(act_grad, axis=0, keepdims=True)
        for i in range(4):
            sums_run[0, pl.ds(64 + 16 * w.e + 4 * tt + i, 1), :] = total[:, 128 * i : 128 * (i + 1)]
    def go_back():
        for tt in range(4):
            loads[4 + tt].wait()
            product = mm(act_low[tt], stream[tt % 2].reshape(1024, 512), ((1,), (1,)))
            back[...] = product if tt == 0 else back[...] + product
            used(loads, 4 + tt)
        part_two[...] = back[half:, :].astype(bf)
        net.send(pb, True, lambda: part_two, lambda: land_two, sibling)
    def first_back():
        net.recv(pb, True, lambda: land_two, sibling)
        norm_grad = second_grad[...] + (back[:half, :] + land_two[...].astype(f32))
        centered = first_sum[...] - jnp.mean(first_sum[...], axis=1, keepdims=True)
        inverse = lax.rsqrt(jnp.mean(centered * centered, axis=1, keepdims=True) + norm_epsilon)
        unit = centered * inverse
        slanted = norm_grad * gain[...]
        grad = inverse * (slanted - jnp.mean(slanted, axis=1, keepdims=True) - unit * jnp.mean(slanted * unit, axis=1, keepdims=True))
        first_grad[...] = grad
        first_low[0] = grad.astype(bf)
        net.send(pf, True, lambda: first_low.at[0], lambda: first_low.at[1], sibling)
        for at, value in ((0, norm_grad * unit), (16, grad), (24, norm_grad)):
            total = jnp.sum(value, axis=0, keepdims=True)
            for i in range(8):
                sums_run[0, at + i : at + i + 1, :] = total[:, 128 * i : 128 * (i + 1)]
    def input_rows(n):
        rows = pl.ds(n * half, half)
        return sum(mm(mixed[tt, rows, :], weight(tt, 0), ((1,), (1,))) for tt in range(4))

    ids = [[net.pair(), net.pair()] for _ in range(4)]
    pi, pb, pf = net.pair(), net.pair(), net.pair()
    def rows_out(kind, src, dst, local):
        for d in range(4):
            t2 = (w.t + d) % 4
            here = lambda t2=t2: src.at[pl.ds(pl.multiple_of(t2 * 64, 64), 64)]
            there = lambda: dst.at[w.t // 2, w.t % 2]
            net.send(ids[d][kind], True if d else jnp.logical_not(same), here, there, w.at(e=w.c, c=w.e, t=t2))
        cp = pltpu.make_async_copy(src.at[pl.ds(pl.multiple_of(w.t * 64, 64), 64)], dst.at[w.t // 2, w.t % 2], local)
        pl.when(same)(lambda: cp.start())
        return cp
    def rows_in(kind, dst):
        for d in range(4):
            t2 = (w.t + 4 - d) % 4
            net.recv(ids[d][kind], True if d else jnp.logical_not(same), lambda t2=t2: dst.at[t2 // 2, t2 % 2], w.at(e=w.c, c=w.e, t=t2))
    partners = (sibling, w.at(c=1 - w.c), w.at(y=1 - w.y), w.at(t=w.t + 1 - 2 * (w.t % 2)), w.at(t=(w.t + 2) % 4))
    sums_ids = [net.pair() for _ in partners]
    def sums_step(s):
        if s > 0:
            net.recv(sums_ids[s - 1], True, lambda: sums_land.at[s - 1], partners[s - 1])
            total = sums_run[s - 1] + sums_land[s - 1]
            if s == 5:
                sums_out[...] = total
            else:
                sums_run[s] = total
        if s < 5:
            net.send(sums_ids[s], True, lambda: sums_run.at[s], lambda: sums_land.at[s], partners[s])
    def finish(*pieces):
        for i in pieces:
            c0, cn = PIECES[i]
            ref = (o_qkv, o_out, o_up, o_down)[i]
            cols = pl.ds(c0, cn)
            ref[:, pl.ds(pl.multiple_of(w.e * cn, 128), cn)] = g[w.t, w.y, w.e, w.c, :, cols].astype(f32)
            ref[:, pl.ds(pl.multiple_of((1 - w.e) * cn, 128), cn)] = sib[:, cols].astype(f32)

    sums_run[0] = sums[...]
    down.stage(0, grads(second_low, hidden, 3))
    fill_up = grads(norm_low, act_low, 2)
    def fill_act(tt):
        activate(tt)
        fill_up(tt)
    up.stage(0, fill_act)
    go_back()
    own = [rows_out(0, lo, lo_out, local_sems.at[5])]
    down.stage(1)
    first_back()
    wide_copy.wait()
    net.recv(pf, True, lambda: first_low.at[1], sibling)
    for tt in range(4):
        attend_back(tt)
    fill_qkv, fill_out = grads(x, mixed, 0), grads(first_low, att, 1)
    def fill_rest(tt):
        fill_qkv(tt)
        fill_out(tt)
    rest.stage(0, fill_rest)
    up.stage(1)
    down.stage(2)
    sums_step(0)
    part[...] = input_rows(1).astype(bf)
    net.send(pi, True, lambda: part, lambda: land, sibling)
    ig_mine = first_grad[...] + input_rows(0)
    down.stage(3)
    up.stage(2)
    rest.stage(1)
    sums_step(1)
    net.recv(pi, True, lambda: land, sibling)
    ig[...] = (ig_mine + land[...].astype(f32)).astype(bf)
    own.append(rows_out(1, ig, ig_out, local_sems.at[6]))
    down.stage(4)
    up.stage(3)
    rest.stage(2)
    sums_step(2)
    down.stage(5)
    up.stage(4)
    rest.stage(3)
    sums_step(3)
    down.stage(6)
    finish(3)
    up.stage(5)
    rest.stage(4)
    sums_step(4)
    up.stage(6)
    finish(2)
    rest.stage(5)
    sums_step(5)
    rest.stage(6)
    finish(0, 1)
    for cp in own:
        pl.when(same)(lambda cp=cp: cp.wait())
    rows_in(0, lo_out)
    rows_in(1, ig_out)
    net.drain()

N_SCATTER = 109

def run_scatter(second_low, hidden, norm_low, slope, att, q, k, v, p_low, x, first_sum, second_grad, gain, full, lo, sums):
    any_ = pl.BlockSpec(memory_space=pl.ANY)
    vm = pl.BlockSpec(memory_space=pltpu.VMEM)
    f32, bf = jnp.float32, jnp.bfloat16
    n = full.shape[-1]
    rows, width = lo.shape
    tokens = 2 * rows
    share = rows // 4
    sd = jax.ShapeDtypeStruct
    return pl.pallas_call(
        scatter_kernel,
        out_shape=(sd((128, 768), f32), sd((128, 256), f32), sd((128, 1024), f32), sd((128, 1024), f32),
                   sd((2, 2, share, width), bf), sd((2, 2, share, width), bf), sd(sums.shape, f32)),
        in_specs=[vm] * 3 + [any_] + [vm] * 4 + [any_] + [vm] * 4 + [any_] + [vm] * 2,
        out_specs=(vm, vm, vm, vm, any_, any_, vm),
        scratch_shapes=[pltpu.VMEM((4, 2, 2, 2, 128, n), bf),
                        pltpu.VMEM((4, 2, 2, 48, n), bf), pltpu.VMEM((4, 2, 48, n), bf),
                        pltpu.VMEM((4, 2, 2, 48, n), bf), pltpu.VMEM((4, 2, 48, n), bf),
                        pltpu.VMEM((5, 2, 96, n), bf), pltpu.VMEM((5, 2, 2, 2, 32, n), bf),
                        pltpu.VMEM((2, 2, 32, n), bf), pltpu.VMEM((2, 32, n), bf), pltpu.VMEM((128, n), bf),
                        pltpu.VMEM((5,) + sums.shape, f32), pltpu.VMEM((5,) + sums.shape, f32),
                        pltpu.VMEM((4, 2, 2, 2, 128, 512), bf), pltpu.VMEM((2, 2, 2, 2, 128, 512), bf), pltpu.VMEM((2, tokens, 512), bf),
                        pltpu.VMEM((4, tokens, 512), bf), pltpu.VMEM((2, rows, width), bf), pltpu.VMEM((rows, width), f32), pltpu.VMEM((tokens, width), f32),
                        pltpu.VMEM((2, tokens, HD), bf), pltpu.VMEM((2, tokens, HD), f32), pltpu.VMEM((2, tokens, HD), f32),
                        pltpu.VMEM((2, tokens, HD), f32), pltpu.VMEM((4, tokens, 6 * HD), bf),
                        pltpu.VMEM((rows, width), bf), pltpu.VMEM((rows, width), bf), pltpu.VMEM((rows, width), bf), pltpu.VMEM((rows, width), bf), pltpu.VMEM((rows, width), bf),
                        pltpu.SemaphoreType.DMA((N_SCATTER,)), pltpu.SemaphoreType.DMA((N_SCATTER,)), pltpu.SemaphoreType.DMA((19,))],
        compiler_params=pltpu.CompilerParams(collective_id=1, has_side_effects=True, vmem_limit_bytes=67043328),
        name="scatter",
    )(second_low, hidden, norm_low, slope, att, q, k, v, p_low.reshape(8, 2, 2, 128, tokens), x, first_sum, second_grad, gain, full, lo, sums)


def swap_cores(value):
    return lax.ppermute(value, "fsdp", [(i, i ^ 1) for i in range(lax.axis_size("fsdp"))])


def own_rows(part):
    half = part.shape[0] // 2
    return part[:half] + swap_cores(part[half:].astype(jnp.bfloat16)).astype(jnp.float32)


def both_rows(rows_mine):
    return jnp.concatenate([rows_mine, swap_cores(rows_mine)], axis=0)


def dot32(spec, left, right):
    return jnp.einsum(spec, left, right, preferred_element_type=jnp.float32)


def fast_local(
    inputs, out_grad, segment_ids, w_qkv, bias_qv, w_out, w_up, bias_up, w_down, gains, shifts
):
    w = Where()
    bf, f32 = jnp.bfloat16, jnp.float32
    rows, model_width = inputs.shape[2:]
    tokens = 2 * rows
    score_scale = HD ** (-0.5)
    norms_in = jnp.concatenate([gains, shifts], axis=1).T
    qv = bias_qv.reshape(2, 2, 2, HD)
    qkv_bias = jnp.stack([qv[:, :, 0], jnp.zeros_like(qv[:, :, 0]), qv[:, :, 1]], axis=2)
    small = jnp.concatenate(
        [
            jnp.broadcast_to(norms_in, (2, 6, 128)),
            qkv_bias.reshape(2, 3, 128),
            bias_up.reshape(2, 4, 128),
            jnp.zeros((2, 3, 128), bf),
        ],
        axis=1,
    )
    ids = jnp.where(w.e == w.c, segment_ids, swap_cores(segment_ids)).reshape(4, 2, rows)
    ids = lax.dynamic_index_in_dim(ids, w.t, 0, keepdims=False)
    ids = jnp.where(w.e == 0, ids, ids[::-1]).reshape(tokens)
    (
        full_all, small_full, x_all, upstream, queries, key_rows, value_rows, p_low, attended_low,
        first_sum, norm_low, hidden, gelu_slope,
    ) = run_gather(w_qkv, w_out, w_up, w_down, small, inputs, out_grad, ids)
    full = full_all.reshape(4, model_width, -1)
    small_full = small_full.reshape(4, 8, 16, 128)
    norm_all = small_full[0, :, :6].transpose(1, 0, 2).reshape(6, model_width).astype(f32)
    gain_rows, shift_rows = norm_all[:2], norm_all[2:]
    full_down = full[:, :, PIECES[3][0] :]
    x_low = x_all.reshape(tokens, model_width)
    norm_low = norm_low.reshape(tokens, model_width)
    first_norm = norm_rows(first_sum, gain_rows[0], shift_rows[1])
    down_part = dot32("tnc,tkc->nk", hidden, full_down)
    second_sum = first_norm + own_rows(down_part) + shift_rows[2]
    result, second_back = jax.vjp(norm_rows, second_sum, gain_rows[1], shift_rows[3])
    layer_mine = result.astype(bf)
    second_grad, gain_two, shift_three = second_back(upstream.astype(f32))
    shift_two = jnp.sum(second_grad, axis=0)
    second_low = both_rows(second_grad.astype(bf))
    blank = jnp.zeros_like(shift_two)
    norm_sums = jnp.stack([blank, gain_two, blank, blank, shift_two, shift_three])
    sums = jnp.concatenate([norm_sums.reshape(48, 128), jnp.zeros((48, 128), f32)])
    g_qkv, g_out, g_up, g_down, layer_out, input_out, sums = run_scatter(
        second_low, hidden, norm_low, gelu_slope, attended_low, queries, key_rows, value_rows,
        p_low, x_low, first_sum, second_grad, gain_rows[:1], full_all, layer_mine, sums,
    )
    qv_mine = lax.dynamic_index_in_dim(sums[48:64].reshape(2, 4, 256), w.t, 1, keepdims=False)
    up_mine = lax.dynamic_index_in_dim(sums[64:].reshape(2, 4, 512), w.t, 1, keepdims=False)
    block = (2 * w.y + w.e) * 2 + w.c
    norm_mine = lax.dynamic_index_in_dim(sums[:48].reshape(6, 8, 128), block, 1, keepdims=False)
    return (
        layer_out,
        input_out.astype(f32),
        g_qkv,
        qv_mine.reshape(-1),
        g_out,
        g_up,
        up_mine.reshape(-1),
        g_down,
        norm_mine[:2].T,
        norm_mine[2:].T,
    )


def fits_fast(mesh):
    return dict(mesh.shape) == {"fsdp": 4, "ctx": 2, "tp": 4}


def solution(mesh):
    placed = (
        P(None, "fsdp", "ctx", None),
        P(None, "fsdp", "ctx", None),
        P(None, "fsdp", None),
        P(("fsdp", "ctx"), "tp"),
        P("tp"),
        P(("fsdp", "ctx"), "tp"),
        P(("fsdp", "ctx"), "tp"),
        P("tp"),
        P(("fsdp", "ctx"), "tp"),
        P(("fsdp", "ctx"), None),
        P(("fsdp", "ctx"), None),
    )
    return jax.shard_map(
        fast_local if fits_fast(mesh) else local,
        mesh=mesh,
        in_specs=placed,
        out_specs=(
            P(None, "fsdp", ("ctx", "tp"), None),
            P(None, "fsdp", ("ctx", "tp"), None),
            P(("fsdp", "ctx"), "tp"),
            P("tp"),
            P(("fsdp", "ctx"), "tp"),
            P(("fsdp", "ctx"), "tp"),
            P("tp"),
            P(("fsdp", "ctx"), "tp"),
            P(("fsdp", "ctx"), None),
            P(("fsdp", "ctx"), None),
        ),
        check_vma=False,
    )
```
